256 devices in a mesh: strip: 64 (over x, z, core), chan: 4 (over y).
Axes of the slice: x: 4, y: 4, z: 8, core: 2. Of those that a mesh axis runs over, the one named last changes fastest.
Arguments:
- section_input: bfloat16 [48, 8192, 256], P(None, 'strip'), may hold values from -6 to 6
- conv_weight: bfloat16 [3, 3, 256, 256], replicated, may hold values from -0.125 to 0.125
- conv_bias: float32 [256], replicated, may hold values from -3 to 3
- deep_weight: bfloat16 [3, 3, 256, 512], P(None, None, None, 'chan'), may hold values from -0.125 to 0.125
- deep_bias: float32 [512], P('chan'), may hold values from -3 to 3
- labels: int32 [24, 4096], P(None, 'strip'), may hold values from 0 to 32, as said below
- slot_ids: int32 [2048], P('strip'), may hold values from 0 to 4095, as said below
- embed_grad: float32 [4096, 512], P('strip', 'chan'), may hold values from -0.8 to 0.8
Outputs:
- embeddings: float32 [4096, 512], P('strip', 'chan')
- weight_grad: float32 [3, 3, 256, 512], P(None, None, None, 'chan')
- bias_grad: float32 [512], P('chan')
The draws below stay inside these ranges and needn't reach their ends.
Inputs may be any that keep to these rules, and one draw needn't show every extreme that they name: `labels`: the value 32 marks background; any other value v names entry v of the list of the strip that holds the pixel. `slot_ids`: A value s names slot s % 64 of owner s // 64 (an index of strip). The slots within one strip's list differ; a slot stands in the lists of at most two strips, which are neighbours (a crack across a strip border). Every owner holds at most 64 components and some owner holds exactly 64.
All inputs are finite; a program needn't handle non-finite values.
Results may differ from the reference program's by a relative error of at most 0.0035.
Values may be sent and summed in bfloat16 or wider, within the bound.
A program may use at most 64 MiB of HBM per device.

```python
import jax
import jax.numpy as jnp
from jax import lax

CMID = 256
CDEEP = 512
ROWS = 48
LIST_DEV = 32
SHARED = 4
OWNED = 64
COLS = 8192
HALF_DEV = 64
HALF_COLS = 4096
HALF_ROWS = 24
LISTS = 2048
SLOTS = 4096


def draw_labels(key, part):
    keys = jax.random.split(key, 4)
    column = jnp.arange(HALF_COLS, dtype=jnp.int32) % HALF_DEV
    quarter = max(HALF_DEV // 4, 1)
    left_lab = jax.random.randint(keys[0], (HALF_ROWS, HALF_COLS), 0, SHARED)
    right_lab = jax.random.randint(keys[1], (HALF_ROWS, HALF_COLS), LIST_DEV - SHARED, LIST_DEV)
    middle_lab = jax.random.randint(keys[2], (HALF_ROWS, HALF_COLS), SHARED, LIST_DEV - SHARED)
    backdrop = jax.random.randint(keys[3], (HALF_ROWS, HALF_COLS), 0, 4)
    chosen = jnp.where(column[None, :] < quarter, left_lab, jnp.where(column[None, :] >= HALF_DEV - quarter, right_lab, middle_lab))
    return jnp.where(backdrop == 0, LIST_DEV, chosen).astype(jnp.int32)


def draw_slot_ids(key, part):
    keys = jax.random.split(key, 3)
    strip_total = LISTS // LIST_DEV
    entries = jnp.arange(LISTS, dtype=jnp.int32)
    strip_of = entries // LIST_DEV
    within = entries % LIST_DEV
    step_size = LIST_DEV - SHARED
    own_id = jnp.where(strip_of == 0, within, LIST_DEV + (strip_of - 1) * step_size + (within - SHARED))
    prev_strip = strip_of - 1
    prev_entry = LIST_DEV - SHARED + within
    shared_id = jnp.where(prev_strip == 0, prev_entry, LIST_DEV + (prev_strip - 1) * step_size + (prev_entry - SHARED))
    component = jnp.where((strip_of >= 1) & (within < SHARED), shared_id, own_id)
    unique_total = LIST_DEV + (strip_total - 1) * step_size
    order_rank = jax.random.permutation(keys[0], unique_total)
    busiest = jax.random.randint(keys[1], (), 0, strip_total)
    spare_total = (strip_total - 1) * OWNED
    spare = jax.random.permutation(keys[2], spare_total)
    ranked = order_rank[component]
    picked = spare[jnp.clip(ranked - OWNED, 0, spare_total - 1)]
    other_owner = picked // OWNED
    other_owner = other_owner + (other_owner >= busiest).astype(jnp.int32)
    slot_value = jnp.where(ranked < OWNED, busiest * OWNED + ranked, other_owner * OWNED + picked % OWNED)
    return slot_value.astype(jnp.int32)


def shard_levels(rng, extent, cuts, low, top_value):
    level = 1.0
    for axis_at, parts in cuts:
        steps = jax.random.uniform(jax.random.fold_in(jax.random.fold_in(rng, 6), axis_at), (parts,), jnp.float32, low / len(cuts), top_value / len(cuts))
        level = level * jnp.repeat(jnp.exp(steps), extent[axis_at] // parts).reshape((-1,) + (1,) * (len(extent) - 1 - axis_at))
    return level


def noise(own_key, dims, scale, limit, cuts=(), held_as=jnp.bfloat16):
    values = scale * jax.random.normal(own_key, dims, jnp.float32)
    if cuts:
        values = values * shard_levels(own_key, dims, cuts, -0.22, 0.18)
    return jnp.clip(values, -limit, limit).astype(held_as)


def setup_inputs(seed: int = 0) -> dict:
    key_list = jax.random.split(jax.random.key(seed), 9)
    section_input = noise(key_list[0], (ROWS, COLS, CMID), 1.0, 6.0, ((1, 64),))
    conv_weight = noise(key_list[1], (3, 3, CMID, CMID), (9 * CMID) ** -0.5, 0.125)
    conv_bias = noise(key_list[2], (CMID,), 0.5, 3.0, (), jnp.float32)
    deep_weight = noise(key_list[3], (3, 3, CMID, CDEEP), (9 * CMID) ** -0.5, 0.125, ((3, 4),))
    deep_bias = noise(key_list[4], (CDEEP,), 0.5, 3.0, ((0, 4),), jnp.float32)
    labels = draw_labels(jax.random.fold_in(key_list[8], 71), 0)
    slot_ids = draw_slot_ids(jax.random.fold_in(key_list[8], 71), 0)
    embed_grad = noise(key_list[7], (SLOTS, CDEEP), 0.1, 0.8, ((0, 64), (1, 4)), jnp.float32)
    return dict(section_input=section_input, conv_weight=conv_weight, conv_bias=conv_bias, deep_weight=deep_weight, deep_bias=deep_bias, labels=labels, slot_ids=slot_ids, embed_grad=embed_grad)


def swish(value):
    return value * jax.nn.sigmoid(value)


def swish_slope(value):
    sigma = jax.nn.sigmoid(value)
    return sigma * (1.0 + value * (1.0 - sigma))


def convolve(padded, weight, row_count, col_count):
    channels = padded.shape[-1]
    running = None
    for shift_row in range(3):
        for shift_col in range(3):
            window = padded[shift_row:shift_row + row_count, shift_col:shift_col + col_count].reshape(row_count * col_count, channels)
            partial_term = jnp.dot(window, weight[shift_row, shift_col], preferred_element_type=jnp.float32)
            running = partial_term if running is None else running + partial_term
    return running.reshape(row_count, col_count, weight.shape[-1])


def pool_pairs(hidden):
    row_count, col_count, channels = hidden.shape
    return hidden.reshape(row_count // 2, 2, col_count // 2, 2, channels).mean(axis=(1, 3)).astype(jnp.bfloat16)


def reference(section_input, conv_weight, conv_bias, deep_weight, deep_bias, labels, slot_ids, embed_grad):
    padded = jnp.pad(section_input, ((1, 1), (1, 1), (0, 0)))

    def row_block(block_index):
        first_row = (block_index * 8).astype(jnp.int32)
        row_band = lax.dynamic_slice_in_dim(padded, first_row, 10, 0)
        hidden = swish(convolve(row_band, conv_weight, 8, COLS) + conv_bias)
        return pool_pairs(hidden)

    pooled = lax.map(row_block, jnp.arange(ROWS // 8, dtype=jnp.int32)).reshape(HALF_ROWS, HALF_COLS, CMID)
    padded_deep = jnp.pad(pooled, ((1, 1), (1, 1), (0, 0)))
    deep_pre = convolve(padded_deep, deep_weight, HALF_ROWS, HALF_COLS) + deep_bias
    features = swish(deep_pre).astype(jnp.bfloat16).reshape(-1, CDEEP)
    strip_of = jnp.arange(HALF_COLS, dtype=jnp.int32) // HALF_DEV
    entry_index = (strip_of[None, :] * LIST_DEV + jnp.minimum(labels, LIST_DEV - 1)).astype(jnp.int32)
    pixel_slot = jnp.where(labels < LIST_DEV, slot_ids[entry_index], SLOTS).reshape(-1).astype(jnp.int32)
    slot_sums = jax.ops.segment_sum(features.astype(jnp.float32), pixel_slot, num_segments=SLOTS + 1)[:SLOTS]
    counts = jax.ops.segment_sum(jnp.ones(pixel_slot.shape, jnp.float32), pixel_slot, num_segments=SLOTS + 1)[:SLOTS]
    divisor = jnp.maximum(counts, 1.0)[:, None]
    embeddings = slot_sums / divisor
    slot_grad = jnp.concatenate([embed_grad / divisor, jnp.zeros((1, CDEEP), jnp.float32)], axis=0)
    pixel_grad = slot_grad[pixel_slot] * swish_slope(deep_pre.reshape(-1, CDEEP))
    deep_grad = pixel_grad.astype(jnp.bfloat16)
    pieces = []
    for shift_row in range(3):
        for shift_col in range(3):
            window = padded_deep[shift_row:shift_row + HALF_ROWS, shift_col:shift_col + HALF_COLS].reshape(-1, CMID)
            pieces.append(lax.dot_general(window, deep_grad, (((0,), (0,)), ((), ())), preferred_element_type=jnp.float32))
    weight_grad = jnp.stack(pieces).reshape(3, 3, CMID, CDEEP)
    bias_grad = jnp.sum(deep_grad.astype(jnp.float32), axis=0)
    return embeddings, weight_grad, bias_grad
```

```python
import jax
import jax.numpy as jnp
from jax import lax
from jax.sharding import PartitionSpec as P


def with_halo(cells, sides, width):
    for axis, dim in sides:
        count = lax.axis_size(axis)
        ends = count - 1
        head = lax.slice_in_dim(cells, 0, width, axis=dim)
        tail = lax.slice_in_dim(cells, cells.shape[dim] - width, cells.shape[dim], axis=dim)
        cells = jnp.concatenate(
            [
                lax.ppermute(tail, axis, [(i, (i + 1) % count) for i in range(ends)]),
                cells,
                lax.ppermute(head, axis, [((i + 1) % count, i) for i in range(ends)]),
            ],
            axis=dim,
        )
    return cells


def swish(value):
    return value * jax.nn.sigmoid(value)


def swish_slope(value):
    sigma = jax.nn.sigmoid(value)
    return sigma * (1.0 + value * (1.0 - sigma))


def convolve(padded, weight, row_count, col_count):
    channels = padded.shape[-1]
    running = None
    for shift_row in range(3):
        for shift_col in range(3):
            window = padded[
                shift_row : shift_row + row_count, shift_col : shift_col + col_count
            ].reshape(row_count * col_count, channels)
            partial_term = jnp.dot(
                window, weight[shift_row, shift_col], preferred_element_type=jnp.float32
            )
            running = partial_term if running is None else running + partial_term
    return running.reshape(row_count, col_count, weight.shape[-1])


def pool_pairs(hidden):
    row_count, col_count, channels = hidden.shape
    return (
        hidden.reshape(row_count // 2, 2, col_count // 2, 2, channels)
        .mean(axis=(1, 3))
        .astype(jnp.bfloat16)
    )


def body(
    section_input, conv_weight, conv_bias, deep_weight, deep_bias, labels, slot_ids, embed_grad
):
    chan_count = lax.axis_size("chan")
    chan_pos = lax.axis_index("chan")
    strip_count = lax.axis_size("strip")
    strip_pos = lax.axis_index("strip")
    row_total, col_local, channels = section_input.shape
    row_part = row_total // chan_count
    half_cols = col_local // 2
    list_len = slot_ids.shape[0]
    owned, width_deep = embed_grad.shape
    lanes = embed_grad.shape[1]

    flat_labels = labels.reshape(-1)
    member = flat_labels[None, :] == jnp.arange(list_len, dtype=jnp.int32)[:, None]
    part_counts = jnp.sum(member.astype(jnp.float32), axis=1)
    meta = jnp.zeros((8, lanes), jnp.float32)
    meta = meta.at[0, :list_len].set(part_counts)
    meta = meta.at[0, list_len : 2 * list_len].set(slot_ids.astype(jnp.float32))
    packed = jnp.concatenate([embed_grad, meta], axis=0)
    every = lax.all_gather(packed, "strip", axis=0, tiled=False)
    every_grad = every[:, :owned].reshape(strip_count * owned, lanes)
    every_counts = every[:, owned, :list_len].reshape(-1)
    every_slots = jnp.round(every[:, owned, list_len : 2 * list_len]).astype(jnp.int32).reshape(-1)

    padded_rows = jnp.pad(section_input, ((1, 1), (0, 0), (0, 0)))
    own_rows = lax.dynamic_slice_in_dim(padded_rows, chan_pos * row_part, row_part + 2, 0)
    extended = with_halo(own_rows, (("strip", 1),), 3)
    hidden = swish(convolve(extended, conv_weight, row_part, col_local + 4) + conv_bias)
    pooled = pool_pairs(hidden)
    column = jnp.arange(half_cols + 2)
    outside = (column == 0) & (strip_pos == 0) | (column == half_cols + 1) & (
        strip_pos == strip_count - 1
    )
    pooled = jnp.where(outside[None, :, None], jnp.zeros_like(pooled), pooled)
    gathered = lax.all_gather(pooled, "chan", axis=0, tiled=True)
    padded_deep = jnp.pad(gathered, ((1, 1), (0, 0), (0, 0)))
    half_rows = gathered.shape[0]
    deep_pre = convolve(padded_deep, deep_weight, half_rows, half_cols) + deep_bias
    features = swish(deep_pre).astype(jnp.bfloat16).reshape(-1, width_deep)
    part_sums = jnp.dot(member.astype(jnp.bfloat16), features, preferred_element_type=jnp.float32)

    same_slot = (slot_ids[:, None] == every_slots[None, :]).astype(jnp.float32)
    entry_counts = jnp.dot(same_slot, every_counts, precision=lax.Precision.HIGHEST)
    entry_grad = every_grad[slot_ids] / jnp.maximum(entry_counts, 1.0)[:, None]
    pixel_grad = lax.dot_general(
        member.astype(jnp.float32),
        entry_grad,
        (((0,), (0,)), ((), ())),
        precision=lax.Precision.HIGHEST,
        preferred_element_type=jnp.float32,
    )
    deep_grad = (pixel_grad * swish_slope(deep_pre.reshape(-1, width_deep))).astype(jnp.bfloat16)
    pieces = []
    for shift_row in range(3):
        for shift_col in range(3):
            window = padded_deep[
                shift_row : shift_row + half_rows, shift_col : shift_col + half_cols
            ].reshape(-1, channels)
            pieces.append(
                lax.dot_general(
                    window, deep_grad, (((0,), (0,)), ((), ())), preferred_element_type=jnp.float32
                )
            )
    local_bias = jnp.sum(deep_grad.astype(jnp.float32), axis=0)
    bias_rows = jnp.zeros((8, width_deep), jnp.float32).at[0].set(local_bias)
    local_grads = jnp.concatenate(pieces + [bias_rows], axis=0)

    every_sums = lax.all_gather(part_sums, "strip", axis=0, tiled=True)
    mine = strip_pos * owned + jnp.arange(owned, dtype=jnp.int32)
    pick = (mine[:, None] == every_slots[None, :]).astype(jnp.float32)
    slot_sums = jnp.dot(pick, every_sums, precision=lax.Precision.HIGHEST)
    slot_counts = jnp.dot(pick, every_counts, precision=lax.Precision.HIGHEST)
    embeddings = slot_sums / jnp.maximum(slot_counts, 1.0)[:, None]

    total_grads = lax.psum(local_grads, "strip")
    weight_grad = total_grads[: 9 * channels].reshape(3, 3, channels, width_deep)
    bias_grad = total_grads[9 * channels]
    return (embeddings, weight_grad, bias_grad)


def solution(mesh):
    placed = (
        P(None, "strip", None),
        P(),
        P(),
        P(None, None, None, "chan"),
        P("chan"),
        P(None, "strip"),
        P("strip"),
        P("strip", "chan"),
    )
    return jax.shard_map(
        body,
        mesh=mesh,
        in_specs=placed,
        out_specs=(P("strip", "chan"), P(None, None, None, "chan"), P("chan")),
        check_vma=False,
    )
```

```python
import jax
import numpy as np
import jax.numpy as jnp
from jax import lax
from jax.sharding import PartitionSpec as P


def with_halo(cells, sides, width):
    for axis, dim in sides:
        count = lax.axis_size(axis)
        ends = count - 1
        head = lax.slice_in_dim(cells, 0, width, axis=dim)
        tail = lax.slice_in_dim(cells, cells.shape[dim] - width, cells.shape[dim], axis=dim)
        cells = jnp.concatenate(
            [
                lax.ppermute(tail, axis, [(i, (i + 1) % count) for i in range(ends)]),
                cells,
                lax.ppermute(head, axis, [((i + 1) % count, i) for i in range(ends)]),
            ],
            axis=dim,
        )
    return cells


def tree_gather(block, axis, order):
    count = lax.axis_size(axis)
    me = lax.axis_index(axis)
    held = block
    for dist in order:
        other = lax.ppermute(held, axis, [(i, i ^ dist) for i in range(count)])
        high = (me // dist) % 2
        size = held.shape[0]
        both = jnp.zeros((2 * size,) + held.shape[1:], held.dtype)
        both = lax.dynamic_update_slice_in_dim(both, held, high * size, 0)
        held = lax.dynamic_update_slice_in_dim(both, other, (1 - high) * size, 0)
    return held


def gather_position(order, count):
    return np.array(
        [sum(((j // dist) % 2) << k for k, dist in enumerate(order)) for j in range(count)],
        np.int32,
    )


def tree_sum(block, axis):
    count = lax.axis_size(axis)
    me = lax.axis_index(axis)
    order = [1 << k for k in range(count.bit_length() - 1)]
    held = block
    for dist in order:
        half = held.shape[0] // 2
        high = (me // dist) % 2
        keep = lax.dynamic_slice_in_dim(held, high * half, half, 0)
        send = lax.dynamic_slice_in_dim(held, (1 - high) * half, half, 0)
        held = keep + lax.ppermute(send, axis, [(i, i ^ dist) for i in range(count)])
    return tree_gather(held, axis, order[::-1])


def swish(value):
    return value * jax.nn.sigmoid(value)


def swish_slope(value):
    sigma = jax.nn.sigmoid(value)
    return sigma * (1.0 + value * (1.0 - sigma))


def convolve(padded, weight, row_count, col_count):
    channels = padded.shape[-1]
    running = None
    for shift_row in range(3):
        for shift_col in range(3):
            window = padded[
                shift_row : shift_row + row_count, shift_col : shift_col + col_count
            ].reshape(row_count * col_count, channels)
            partial_term = jnp.dot(
                window, weight[shift_row, shift_col], preferred_element_type=jnp.float32
            )
            running = partial_term if running is None else running + partial_term
    return running.reshape(row_count, col_count, weight.shape[-1])


def pool_pairs(hidden):
    row_count, col_count, channels = hidden.shape
    return (
        hidden.reshape(row_count // 2, 2, col_count // 2, 2, channels)
        .mean(axis=(1, 3))
        .astype(jnp.bfloat16)
    )


def body(
    section_input, conv_weight, conv_bias, deep_weight, deep_bias, labels, slot_ids, embed_grad
):
    chan_count = lax.axis_size("chan")
    chan_pos = lax.axis_index("chan")
    strip_count = lax.axis_size("strip")
    strip_pos = lax.axis_index("strip")
    row_total, col_local, channels = section_input.shape
    row_part = row_total // chan_count
    half_cols = col_local // 2
    list_len = slot_ids.shape[0]
    owned, width_deep = embed_grad.shape
    lanes = embed_grad.shape[1]

    flat_labels = labels.reshape(-1)
    member = flat_labels[None, :] == jnp.arange(list_len, dtype=jnp.int32)[:, None]
    part_counts = jnp.sum(member.astype(jnp.float32), axis=1)
    meta = jnp.zeros((8, lanes), jnp.float32)
    meta = meta.at[0, :list_len].set(part_counts)
    meta = meta.at[0, list_len : 2 * list_len].set(slot_ids.astype(jnp.float32))
    packed = jnp.concatenate([embed_grad, meta], axis=0)
    order = [strip_count >> (k + 1) for k in range(strip_count.bit_length() - 1)]
    every = tree_gather(packed, "strip", order).reshape(strip_count, owned + 8, lanes)
    every_grad = every[:, :owned].reshape(strip_count * owned, lanes)
    position = jnp.asarray(gather_position(order, strip_count))
    every_counts = every[:, owned, :list_len].reshape(-1)
    every_slots = jnp.round(every[:, owned, list_len : 2 * list_len]).astype(jnp.int32).reshape(-1)

    padded_rows = jnp.pad(section_input, ((1, 1), (0, 0), (0, 0)))
    own_rows = lax.dynamic_slice_in_dim(padded_rows, chan_pos * row_part, row_part + 2, 0)
    extended = with_halo(own_rows, (("strip", 1),), 3)
    hidden = swish(convolve(extended, conv_weight, row_part, col_local + 4) + conv_bias)
    pooled = pool_pairs(hidden)
    column = jnp.arange(half_cols + 2)
    outside = (column == 0) & (strip_pos == 0) | (column == half_cols + 1) & (
        strip_pos == strip_count - 1
    )
    pooled = jnp.where(outside[None, :, None], jnp.zeros_like(pooled), pooled)
    gathered = lax.all_gather(pooled, "chan", axis=0, tiled=True)
    padded_deep = jnp.pad(gathered, ((1, 1), (0, 0), (0, 0)))
    half_rows = gathered.shape[0]
    deep_pre = convolve(padded_deep, deep_weight, half_rows, half_cols) + deep_bias
    features = swish(deep_pre).astype(jnp.bfloat16).reshape(-1, width_deep)
    part_sums = jnp.dot(member.astype(jnp.bfloat16), features, preferred_element_type=jnp.float32)

    same_slot = (slot_ids[:, None] == every_slots[None, :]).astype(jnp.float32)
    entry_counts = jnp.dot(same_slot, every_counts, precision=lax.Precision.HIGHEST)
    grad_row = position[slot_ids // owned] * owned + slot_ids % owned
    entry_grad = every_grad[grad_row] / jnp.maximum(entry_counts, 1.0)[:, None]
    pixel_grad = lax.dot_general(
        member.astype(jnp.float32),
        entry_grad,
        (((0,), (0,)), ((), ())),
        precision=lax.Precision.HIGHEST,
        preferred_element_type=jnp.float32,
    )
    deep_grad = (pixel_grad * swish_slope(deep_pre.reshape(-1, width_deep))).astype(jnp.bfloat16)
    pieces = []
    for shift_row in range(3):
        for shift_col in range(3):
            window = padded_deep[
                shift_row : shift_row + half_rows, shift_col : shift_col + half_cols
            ].reshape(-1, channels)
            pieces.append(
                lax.dot_general(
                    window, deep_grad, (((0,), (0,)), ((), ())), preferred_element_type=jnp.float32
                )
            )
    local_bias = jnp.sum(deep_grad.astype(jnp.float32), axis=0)
    bias_rows = jnp.zeros((strip_count, width_deep), jnp.float32).at[0].set(local_bias)
    local_grads = jnp.concatenate(pieces + [bias_rows], axis=0)

    every_sums = tree_gather(part_sums, "strip", order)
    mine = strip_pos * owned + jnp.arange(owned, dtype=jnp.int32)
    pick = (mine[:, None] == every_slots[None, :]).astype(jnp.float32)
    slot_sums = jnp.dot(pick, every_sums, precision=lax.Precision.HIGHEST)
    slot_counts = jnp.dot(pick, every_counts, precision=lax.Precision.HIGHEST)
    embeddings = slot_sums / jnp.maximum(slot_counts, 1.0)[:, None]

    total_grads = tree_sum(local_grads, "strip")
    weight_grad = total_grads[: 9 * channels].reshape(3, 3, channels, width_deep)
    bias_grad = total_grads[9 * channels]
    return (embeddings, weight_grad, bias_grad)


def solution(mesh):
    placed = (
        P(None, "strip", None),
        P(),
        P(),
        P(None, None, None, "chan"),
        P("chan"),
        P(None, "strip"),
        P("strip"),
        P("strip", "chan"),
    )
    return jax.shard_map(
        body,
        mesh=mesh,
        in_specs=placed,
        out_specs=(P("strip", "chan"), P(None, None, None, "chan"), P("chan")),
        check_vma=False,
    )
```

```python
import jax
import numpy as np
import jax.numpy as jnp
from jax import lax
from jax.sharding import PartitionSpec as P


def with_halo(cells, sides, width):
    for axis, dim in sides:
        count = lax.axis_size(axis)
        ends = count - 1
        head = lax.slice_in_dim(cells, 0, width, axis=dim)
        tail = lax.slice_in_dim(cells, cells.shape[dim] - width, cells.shape[dim], axis=dim)
        cells = jnp.concatenate(
            [
                lax.ppermute(tail, axis, [(i, (i + 1) % count) for i in range(ends)]),
                cells,
                lax.ppermute(head, axis, [((i + 1) % count, i) for i in range(ends)]),
            ],
            axis=dim,
        )
    return cells


def tree_gather(block, axis, order):
    count = lax.axis_size(axis)
    me = lax.axis_index(axis)
    held = block
    for dist in order:
        other = lax.ppermute(held, axis, [(i, i ^ dist) for i in range(count)])
        high = (me // dist) % 2
        size = held.shape[0]
        both = jnp.zeros((2 * size,) + held.shape[1:], held.dtype)
        both = lax.dynamic_update_slice_in_dim(both, held, high * size, 0)
        held = lax.dynamic_update_slice_in_dim(both, other, (1 - high) * size, 0)
    return held


def gather_position(order, count):
    return np.array(
        [sum(((j // dist) % 2) << k for k, dist in enumerate(order)) for j in range(count)],
        np.int32,
    )


def tree_sum(block, axis, rider):
    count = lax.axis_size(axis)
    me = lax.axis_index(axis)
    order = [1 << k for k in range(count.bit_length() - 1)]
    held = block
    for dist in order:
        half = held.shape[0] // 2
        high = (me // dist) % 2
        keep = lax.dynamic_slice_in_dim(held, high * half, half, 0)
        send = lax.dynamic_slice_in_dim(held, (1 - high) * half, half, 0)
        held = keep + lax.ppermute(send, axis, [(i, i ^ dist) for i in range(count)])
    chunk = held.shape[0]
    both = tree_gather(jnp.concatenate([held, rider], axis=0), axis, order[::-1])
    both = both.reshape(count, chunk + rider.shape[0], *held.shape[1:])
    return both[:, :chunk].reshape(count * chunk, *held.shape[1:]), both[:, chunk:]


def swish(value):
    return value * jax.nn.sigmoid(value)


def swish_slope(value):
    sigma = jax.nn.sigmoid(value)
    return sigma * (1.0 + value * (1.0 - sigma))


def convolve(padded, weight, row_count, col_count):
    channels = padded.shape[-1]
    running = None
    for shift_row in range(3):
        for shift_col in range(3):
            window = padded[
                shift_row : shift_row + row_count, shift_col : shift_col + col_count
            ].reshape(row_count * col_count, channels)
            partial_term = jnp.dot(
                window, weight[shift_row, shift_col], preferred_element_type=jnp.float32
            )
            running = partial_term if running is None else running + partial_term
    return running.reshape(row_count, col_count, weight.shape[-1])


def pool_pairs(hidden):
    row_count, col_count, channels = hidden.shape
    return (
        hidden.reshape(row_count // 2, 2, col_count // 2, 2, channels)
        .mean(axis=(1, 3))
        .astype(jnp.bfloat16)
    )


def body(
    section_input, conv_weight, conv_bias, deep_weight, deep_bias, labels, slot_ids, embed_grad
):
    chan_count = lax.axis_size("chan")
    chan_pos = lax.axis_index("chan")
    strip_count = lax.axis_size("strip")
    strip_pos = lax.axis_index("strip")
    row_total, col_local, channels = section_input.shape
    row_part = row_total // chan_count
    half_cols = col_local // 2
    list_len = slot_ids.shape[0]
    owned, width_deep = embed_grad.shape
    lanes = embed_grad.shape[1]

    flat_labels = labels.reshape(-1)
    member = flat_labels[None, :] == jnp.arange(list_len, dtype=jnp.int32)[:, None]
    part_counts = jnp.sum(member.astype(jnp.float32), axis=1)
    meta = jnp.zeros((8, lanes), jnp.float32)
    meta = meta.at[0, :list_len].set(part_counts)
    meta = meta.at[0, list_len : 2 * list_len].set(slot_ids.astype(jnp.float32))
    packed = jnp.concatenate([embed_grad, meta], axis=0)
    order = [strip_count >> (k + 1) for k in range(strip_count.bit_length() - 1)]
    position = jnp.asarray(gather_position(order, strip_count))
    early = tree_gather(packed, "strip", order[:2])

    padded_rows = jnp.pad(section_input, ((1, 1), (0, 0), (0, 0)))
    own_rows = lax.dynamic_slice_in_dim(padded_rows, chan_pos * row_part, row_part + 2, 0)
    extended = with_halo(own_rows, (("strip", 1),), 3)
    extended, early = lax.optimization_barrier((extended, early))
    early = tree_gather(early, "strip", order[2:4])
    hidden = swish(convolve(extended, conv_weight, row_part, col_local + 4) + conv_bias)
    pooled = pool_pairs(hidden)
    column = jnp.arange(half_cols + 2)
    outside = (column == 0) & (strip_pos == 0) | (column == half_cols + 1) & (
        strip_pos == strip_count - 1
    )
    pooled = jnp.where(outside[None, :, None], jnp.zeros_like(pooled), pooled)
    pooled, early = lax.optimization_barrier((pooled, early))
    every = tree_gather(early, "strip", order[4:]).reshape(strip_count, owned + 8, lanes)
    every_grad = every[:, :owned].reshape(strip_count * owned, lanes)
    every_counts = every[:, owned, :list_len].reshape(-1)
    every_slots = jnp.round(every[:, owned, list_len : 2 * list_len]).astype(jnp.int32).reshape(-1)
    gathered = lax.all_gather(pooled, "chan", axis=0, tiled=True)
    padded_deep = jnp.pad(gathered, ((1, 1), (0, 0), (0, 0)))
    half_rows = gathered.shape[0]
    deep_pre = convolve(padded_deep, deep_weight, half_rows, half_cols) + deep_bias
    features = swish(deep_pre).astype(jnp.bfloat16).reshape(-1, width_deep)
    part_sums = jnp.dot(member.astype(jnp.bfloat16), features, preferred_element_type=jnp.float32)

    same_slot = (slot_ids[:, None] == every_slots[None, :]).astype(jnp.float32)
    entry_counts = jnp.dot(same_slot, every_counts, precision=lax.Precision.HIGHEST)
    grad_row = position[slot_ids // owned] * owned + slot_ids % owned
    entry_grad = every_grad[grad_row] / jnp.maximum(entry_counts, 1.0)[:, None]
    pixel_grad = lax.dot_general(
        member.astype(jnp.float32),
        entry_grad,
        (((0,), (0,)), ((), ())),
        precision=lax.Precision.HIGHEST,
        preferred_element_type=jnp.float32,
    )
    deep_grad = (pixel_grad * swish_slope(deep_pre.reshape(-1, width_deep))).astype(jnp.bfloat16)
    pieces = []
    for shift_row in range(3):
        for shift_col in range(3):
            window = padded_deep[
                shift_row : shift_row + half_rows, shift_col : shift_col + half_cols
            ].reshape(-1, channels)
            pieces.append(
                lax.dot_general(
                    window, deep_grad, (((0,), (0,)), ((), ())), preferred_element_type=jnp.float32
                )
            )
    local_bias = jnp.sum(deep_grad.astype(jnp.float32), axis=0)
    bias_rows = jnp.zeros((strip_count, width_deep), jnp.float32).at[0].set(local_bias)
    local_grads = jnp.concatenate(pieces + [bias_rows], axis=0)

    total_grads, every_sums = tree_sum(local_grads, "strip", part_sums)
    every_sums = every_sums.reshape(-1, width_deep)
    mine = strip_pos * owned + jnp.arange(owned, dtype=jnp.int32)
    pick = (mine[:, None] == every_slots[None, :]).astype(jnp.float32)
    slot_sums = jnp.dot(pick, every_sums, precision=lax.Precision.HIGHEST)
    slot_counts = jnp.dot(pick, every_counts, precision=lax.Precision.HIGHEST)
    embeddings = slot_sums / jnp.maximum(slot_counts, 1.0)[:, None]

    weight_grad = total_grads[: 9 * channels].reshape(3, 3, channels, width_deep)
    bias_grad = total_grads[9 * channels]
    return (embeddings, weight_grad, bias_grad)


def solution(mesh):
    placed = (
        P(None, "strip", None),
        P(),
        P(),
        P(None, None, None, "chan"),
        P("chan"),
        P(None, "strip"),
        P("strip"),
        P("strip", "chan"),
    )
    return jax.shard_map(
        body,
        mesh=mesh,
        in_specs=placed,
        out_specs=(P("strip", "chan"), P(None, None, None, "chan"), P("chan")),
        check_vma=False,
    )
```

```python
import jax
import numpy as np
import jax.numpy as jnp
from jax import lax
from jax.sharding import PartitionSpec as P


def with_halo(cells, sides, width):
    for axis, dim in sides:
        count = lax.axis_size(axis)
        ends = count - 1
        head = lax.slice_in_dim(cells, 0, width, axis=dim)
        tail = lax.slice_in_dim(cells, cells.shape[dim] - width, cells.shape[dim], axis=dim)
        cells = jnp.concatenate(
            [
                lax.ppermute(tail, axis, [(i, (i + 1) % count) for i in range(ends)]),
                cells,
                lax.ppermute(head, axis, [((i + 1) % count, i) for i in range(ends)]),
            ],
            axis=dim,
        )
    return cells


def tree_gather(block, axis, order):
    count = lax.axis_size(axis)
    me = lax.axis_index(axis)
    held = block
    for dist in order:
        other = lax.ppermute(held, axis, [(i, i ^ dist) for i in range(count)])
        high = (me // dist) % 2
        size = held.shape[0]
        both = jnp.zeros((2 * size,) + held.shape[1:], held.dtype)
        both = lax.dynamic_update_slice_in_dim(both, held, high * size, 0)
        held = lax.dynamic_update_slice_in_dim(both, other, (1 - high) * size, 0)
    return held


def gather_position(order, count):
    return np.array(
        [sum(((j // dist) % 2) << k for k, dist in enumerate(order)) for j in range(count)],
        np.int32,
    )


def tree_sum(block, axis, rider):
    count = lax.axis_size(axis)
    me = lax.axis_index(axis)
    order = [1 << k for k in range(count.bit_length() - 1)]
    held = block
    for dist in order:
        half = held.shape[0] // 2
        high = (me // dist) % 2
        keep = lax.dynamic_slice_in_dim(held, high * half, half, 0)
        send = lax.dynamic_slice_in_dim(held, (1 - high) * half, half, 0)
        held = keep + lax.ppermute(send, axis, [(i, i ^ dist) for i in range(count)])
    chunk = held.shape[0]
    both = tree_gather(jnp.concatenate([held, rider], axis=0), axis, order[::-1])
    both = both.reshape(count, chunk + rider.shape[0], *held.shape[1:])
    return both[:, :chunk].reshape(count * chunk, *held.shape[1:]), both[:, chunk:]


def swish(value):
    return value * jax.nn.sigmoid(value)


def swish_slope(value):
    sigma = jax.nn.sigmoid(value)
    return sigma * (1.0 + value * (1.0 - sigma))


def convolve(padded, weight, row_count, col_count):
    channels = padded.shape[-1]
    running = None
    for shift_row in range(3):
        for shift_col in range(3):
            window = padded[
                shift_row : shift_row + row_count, shift_col : shift_col + col_count
            ].reshape(row_count * col_count, channels)
            partial_term = jnp.dot(
                window, weight[shift_row, shift_col], preferred_element_type=jnp.float32
            )
            running = partial_term if running is None else running + partial_term
    return running.reshape(row_count, col_count, weight.shape[-1])


def pool_pairs(hidden):
    row_count, col_count, channels = hidden.shape
    return (
        hidden.reshape(row_count // 2, 2, col_count // 2, 2, channels)
        .mean(axis=(1, 3))
        .astype(jnp.bfloat16)
    )


def body(
    section_input, conv_weight, conv_bias, deep_weight, deep_bias, labels, slot_ids, embed_grad
):
    chan_count = lax.axis_size("chan")
    chan_pos = lax.axis_index("chan")
    strip_count = lax.axis_size("strip")
    strip_pos = lax.axis_index("strip")
    row_total, col_local, channels = section_input.shape
    row_part = row_total // chan_count
    half_cols = col_local // 2
    list_len = slot_ids.shape[0]
    owned, width_deep = embed_grad.shape
    lanes = embed_grad.shape[1]

    flat_labels = labels.reshape(-1)
    member = flat_labels[None, :] == jnp.arange(list_len, dtype=jnp.int32)[:, None]
    part_counts = jnp.sum(member.astype(jnp.float32), axis=1)
    meta = jnp.zeros((8, lanes), jnp.float32)
    meta = meta.at[0, :list_len].set(part_counts)
    meta = meta.at[0, list_len : 2 * list_len].set(slot_ids.astype(jnp.float32))
    packed = jnp.concatenate([embed_grad, meta], axis=0)
    order = [strip_count >> (k + 1) for k in range(strip_count.bit_length() - 1)]
    position = jnp.asarray(gather_position(order, strip_count))
    early = tree_gather(packed, "strip", order[:2])

    extended = with_halo(section_input, (("strip", 1),), 3)
    extended, early = lax.optimization_barrier((extended, early))
    early = tree_gather(early, "strip", order[2:4])
    dims = ("NHWC", "HWIO", "NHWC")
    mid = lax.conv_general_dilated(
        extended[None], conv_weight, (1, 1), ((1, 1), (0, 0)),
        dimension_numbers=dims, preferred_element_type=jnp.float32,
    )[0]
    hidden = swish(mid + conv_bias)
    pooled = pool_pairs(hidden)
    column = jnp.arange(half_cols + 2)
    outside = (column == 0) & (strip_pos == 0) | (column == half_cols + 1) & (
        strip_pos == strip_count - 1
    )
    pooled = jnp.where(outside[None, :, None], jnp.zeros_like(pooled), pooled)
    pooled, early = lax.optimization_barrier((pooled, early))
    every = tree_gather(early, "strip", order[4:]).reshape(strip_count, owned + 8, lanes)
    every_grad = every[:, :owned].reshape(strip_count * owned, lanes)
    every_counts = every[:, owned, :list_len].reshape(-1)
    every_slots = jnp.round(every[:, owned, list_len : 2 * list_len]).astype(jnp.int32).reshape(-1)
    padded_deep = jnp.pad(pooled, ((1, 1), (0, 0), (0, 0)))
    half_rows = pooled.shape[0]
    deep_pre = lax.conv_general_dilated(
        pooled[None], deep_weight, (1, 1), ((1, 1), (0, 0)),
        dimension_numbers=dims, preferred_element_type=jnp.float32,
    )[0] + deep_bias
    features = swish(deep_pre).astype(jnp.bfloat16).reshape(-1, width_deep)
    part_sums = jnp.dot(member.astype(jnp.bfloat16), features, preferred_element_type=jnp.float32)

    same_slot = (slot_ids[:, None] == every_slots[None, :]).astype(jnp.float32)
    entry_counts = jnp.dot(same_slot, every_counts, precision=lax.Precision.HIGHEST)
    grad_row = position[slot_ids // owned] * owned + slot_ids % owned
    entry_grad = every_grad[grad_row] / jnp.maximum(entry_counts, 1.0)[:, None]
    pixel_grad = lax.dot_general(
        member.astype(jnp.float32),
        entry_grad,
        (((0,), (0,)), ((), ())),
        precision=lax.Precision.HIGHEST,
        preferred_element_type=jnp.float32,
    )
    deep_grad = (pixel_grad * swish_slope(deep_pre.reshape(-1, width_deep))).astype(jnp.bfloat16)
    pieces = []
    for shift_row in range(3):
        for shift_col in range(3):
            window = padded_deep[
                shift_row : shift_row + half_rows, shift_col : shift_col + half_cols
            ].reshape(-1, channels)
            pieces.append(
                lax.dot_general(
                    window, deep_grad, (((0,), (0,)), ((), ())), preferred_element_type=jnp.float32
                )
            )
    local_bias = jnp.sum(deep_grad.astype(jnp.float32), axis=0)
    bias_rows = jnp.zeros((strip_count, width_deep), jnp.float32).at[0].set(local_bias)
    local_grads = jnp.concatenate(pieces + [bias_rows], axis=0)

    total_grads, every_sums = tree_sum(local_grads, "strip", part_sums)
    every_sums = every_sums.reshape(-1, width_deep)
    mine = strip_pos * owned + jnp.arange(owned, dtype=jnp.int32)
    pick = (mine[:, None] == every_slots[None, :]).astype(jnp.float32)
    slot_sums = jnp.dot(pick, every_sums, precision=lax.Precision.HIGHEST)
    slot_counts = jnp.dot(pick, every_counts, precision=lax.Precision.HIGHEST)
    embeddings = slot_sums / jnp.maximum(slot_counts, 1.0)[:, None]

    weight_grad = total_grads[: 9 * channels].reshape(3, 3, channels, width_deep)
    bias_grad = total_grads[9 * channels]
    return (embeddings, weight_grad, bias_grad)


def solution(mesh):
    placed = (
        P(None, "strip", None),
        P(),
        P(),
        P(None, None, None, "chan"),
        P("chan"),
        P(None, "strip"),
        P("strip"),
        P("strip", "chan"),
    )
    return jax.shard_map(
        body,
        mesh=mesh,
        in_specs=placed,
        out_specs=(P("strip", "chan"), P(None, None, None, "chan"), P("chan")),
        check_vma=False,
    )
```

```python
import functools

import jax
import numpy as np
import jax.numpy as jnp
from jax import lax
from jax.experimental import pallas as pl
from jax.experimental.pallas import tpu as pltpu
from jax.sharding import PartitionSpec as P


def with_halo(cells, sides, width):
    for axis, dim in sides:
        count = lax.axis_size(axis)
        ends = count - 1
        head = lax.slice_in_dim(cells, 0, width, axis=dim)
        tail = lax.slice_in_dim(cells, cells.shape[dim] - width, cells.shape[dim], axis=dim)
        cells = jnp.concatenate(
            [
                lax.ppermute(tail, axis, [(i, (i + 1) % count) for i in range(ends)]),
                cells,
                lax.ppermute(head, axis, [((i + 1) % count, i) for i in range(ends)]),
            ],
            axis=dim,
        )
    return cells


def tree_gather(block, axis, order):
    count = lax.axis_size(axis)
    me = lax.axis_index(axis)
    held = block
    for dist in order:
        other = lax.ppermute(held, axis, [(i, i ^ dist) for i in range(count)])
        high = (me // dist) % 2
        size = held.shape[0]
        both = jnp.zeros((2 * size,) + held.shape[1:], held.dtype)
        both = lax.dynamic_update_slice_in_dim(both, held, high * size, 0)
        held = lax.dynamic_update_slice_in_dim(both, other, (1 - high) * size, 0)
    return held


def gather_position(order, count):
    return np.array(
        [sum(((j // dist) % 2) << k for k, dist in enumerate(order)) for j in range(count)],
        np.int32,
    )


def tree_kernel(count, chunk, width, grads_ref, sums_ref, out_ref, every_ref, landing, sems, free):
    me = lax.axis_index("strip")
    chan = lax.axis_index("chan")
    dists = [1 << k for k in range(count.bit_length() - 1)]
    mesh_id = pl.DeviceIdType.MESH

    def partner(dist):
        return me + dist - 2 * dist * ((me // dist) % 2)

    barrier = pltpu.get_barrier_semaphore()
    for dist in dists:
        pl.semaphore_signal(barrier, inc=1, device_id=(partner(dist), chan), device_id_type=mesh_id)
    pl.semaphore_wait(barrier, len(dists))

    out_ref[...] = grads_ref[...]
    place = 0
    for k, dist in enumerate(dists):
        place = place + ((me // dist) % 2) * (count // (2 * dist))
    every_ref[pl.ds(pl.multiple_of(place * width, 8), width)] = sums_ref[...]

    low = 0
    size = count * chunk
    offset = 0
    for k, dist in enumerate(dists):
        half = size // 2
        high = (me // dist) % 2
        keep = low + high * half
        give = low + (1 - high) * half
        copy = pltpu.make_async_remote_copy(
            src_ref=out_ref.at[pl.ds(pl.multiple_of(give, 8), half)],
            dst_ref=landing.at[pl.ds(offset, half)],
            send_sem=sems.at[0, k],
            recv_sem=sems.at[1, k],
            device_id=(partner(dist), chan),
            device_id_type=mesh_id,
        )
        copy.start()
        copy.wait()
        pl.semaphore_signal(
            free.at[k], inc=1, device_id=(partner(dist), chan), device_id_type=mesh_id
        )

        def accumulate(step, carry, keep=keep, offset=offset):
            mine = pl.ds(pl.multiple_of(keep + step * chunk, 8), chunk)
            got = pl.ds(pl.multiple_of(offset + step * chunk, 8), chunk)
            out_ref[mine] = out_ref[mine] + landing[got]
            return carry

        lax.fori_loop(0, half // chunk, accumulate, 0)
        low = keep
        size = half
        offset += half

    blocks = 1
    for k in reversed(range(len(dists))):
        dist = dists[k]
        pl.semaphore_wait(free.at[k], 1)
        rows = pl.ds(pl.multiple_of(low, 8), size)
        spot = pl.ds(pl.multiple_of(place * width, 8), blocks * width)
        grads_copy = pltpu.make_async_remote_copy(
            src_ref=out_ref.at[rows],
            dst_ref=out_ref.at[rows],
            send_sem=sems.at[2, k],
            recv_sem=sems.at[3, k],
            device_id=(partner(dist), chan),
            device_id_type=mesh_id,
        )
        sums_copy = pltpu.make_async_remote_copy(
            src_ref=every_ref.at[spot],
            dst_ref=every_ref.at[spot],
            send_sem=sems.at[4, k],
            recv_sem=sems.at[5, k],
            device_id=(partner(dist), chan),
            device_id_type=mesh_id,
        )
        grads_copy.start()
        sums_copy.start()
        grads_copy.wait()
        sums_copy.wait()
        high = (me // dist) % 2
        low = low - high * size
        place = place - high * blocks
        size = size * 2
        blocks = blocks * 2


def tree_sum(grads, sums, axis):
    count = lax.axis_size(axis)
    rows, lanes = grads.shape
    chunk = rows // count
    width = sums.shape[0]
    steps = count.bit_length() - 1
    return pl.pallas_call(
        functools.partial(tree_kernel, count, chunk, width),
        out_shape=(
            jax.ShapeDtypeStruct((rows, lanes), jnp.float32),
            jax.ShapeDtypeStruct((count * width, lanes), jnp.float32),
        ),
        in_specs=[pl.BlockSpec(memory_space=pltpu.VMEM)] * 2,
        out_specs=(pl.BlockSpec(memory_space=pltpu.VMEM),) * 2,
        scratch_shapes=[
            pltpu.VMEM((rows, lanes), jnp.float32),
            pltpu.SemaphoreType.DMA((6, steps)),
            pltpu.SemaphoreType.REGULAR((steps,)),
        ],
        compiler_params=pltpu.CompilerParams(collective_id=0, has_side_effects=True),
    )(grads, sums)


def swish(value):
    return value * jax.nn.sigmoid(value)


def swish_slope(value):
    sigma = jax.nn.sigmoid(value)
    return sigma * (1.0 + value * (1.0 - sigma))


def convolve(padded, weight, row_count, col_count):
    channels = padded.shape[-1]
    running = None
    for shift_row in range(3):
        for shift_col in range(3):
            window = padded[
                shift_row : shift_row + row_count, shift_col : shift_col + col_count
            ].reshape(row_count * col_count, channels)
            partial_term = jnp.dot(
                window, weight[shift_row, shift_col], preferred_element_type=jnp.float32
            )
            running = partial_term if running is None else running + partial_term
    return running.reshape(row_count, col_count, weight.shape[-1])


def pool_pairs(hidden):
    row_count, col_count, channels = hidden.shape
    return (
        hidden.reshape(row_count // 2, 2, col_count // 2, 2, channels)
        .mean(axis=(1, 3))
        .astype(jnp.bfloat16)
    )


def body(
    section_input, conv_weight, conv_bias, deep_weight, deep_bias, labels, slot_ids, embed_grad
):
    chan_count = lax.axis_size("chan")
    chan_pos = lax.axis_index("chan")
    strip_count = lax.axis_size("strip")
    strip_pos = lax.axis_index("strip")
    row_total, col_local, channels = section_input.shape
    row_part = row_total // chan_count
    half_cols = col_local // 2
    list_len = slot_ids.shape[0]
    owned, width_deep = embed_grad.shape
    lanes = embed_grad.shape[1]

    flat_labels = labels.reshape(-1)
    member = flat_labels[None, :] == jnp.arange(list_len, dtype=jnp.int32)[:, None]
    part_counts = jnp.sum(member.astype(jnp.float32), axis=1)
    meta = jnp.zeros((8, lanes), jnp.float32)
    meta = meta.at[0, :list_len].set(part_counts)
    meta = meta.at[0, list_len : 2 * list_len].set(slot_ids.astype(jnp.float32))
    packed = jnp.concatenate([embed_grad, meta], axis=0)
    order = [strip_count >> (k + 1) for k in range(strip_count.bit_length() - 1)]
    position = jnp.asarray(gather_position(order, strip_count))
    early = tree_gather(packed, "strip", order[:2])

    padded_rows = jnp.pad(section_input, ((1, 1), (0, 0), (0, 0)))
    own_rows = lax.dynamic_slice_in_dim(padded_rows, chan_pos * row_part, row_part + 2, 0)
    extended = with_halo(own_rows, (("strip", 1),), 3)
    extended, early = lax.optimization_barrier((extended, early))
    early = tree_gather(early, "strip", order[2:4])
    hidden = swish(convolve(extended, conv_weight, row_part, col_local + 4) + conv_bias)
    pooled = pool_pairs(hidden)
    column = jnp.arange(half_cols + 2)
    outside = (column == 0) & (strip_pos == 0) | (column == half_cols + 1) & (
        strip_pos == strip_count - 1
    )
    pooled = jnp.where(outside[None, :, None], jnp.zeros_like(pooled), pooled)
    pooled, early = lax.optimization_barrier((pooled, early))
    every = tree_gather(early, "strip", order[4:]).reshape(strip_count, owned + 8, lanes)
    every_grad = every[:, :owned].reshape(strip_count * owned, lanes)
    every_counts = every[:, owned, :list_len].reshape(-1)
    every_slots = jnp.round(every[:, owned, list_len : 2 * list_len]).astype(jnp.int32).reshape(-1)
    gathered = lax.all_gather(pooled, "chan", axis=0, tiled=True)
    padded_deep = jnp.pad(gathered, ((1, 1), (0, 0), (0, 0)))
    half_rows = gathered.shape[0]
    deep_pre = convolve(padded_deep, deep_weight, half_rows, half_cols) + deep_bias
    features = swish(deep_pre).astype(jnp.bfloat16).reshape(-1, width_deep)
    part_sums = jnp.dot(member.astype(jnp.bfloat16), features, preferred_element_type=jnp.float32)

    same_slot = (slot_ids[:, None] == every_slots[None, :]).astype(jnp.float32)
    entry_counts = jnp.dot(same_slot, every_counts, precision=lax.Precision.HIGHEST)
    grad_row = position[slot_ids // owned] * owned + slot_ids % owned
    entry_grad = every_grad[grad_row] / jnp.maximum(entry_counts, 1.0)[:, None]
    pixel_grad = lax.dot_general(
        member.astype(jnp.float32),
        entry_grad,
        (((0,), (0,)), ((), ())),
        precision=lax.Precision.HIGHEST,
        preferred_element_type=jnp.float32,
    )
    deep_grad = (pixel_grad * swish_slope(deep_pre.reshape(-1, width_deep))).astype(jnp.bfloat16)
    pieces = []
    for shift_row in range(3):
        for shift_col in range(3):
            window = padded_deep[
                shift_row : shift_row + half_rows, shift_col : shift_col + half_cols
            ].reshape(-1, channels)
            pieces.append(
                lax.dot_general(
                    window, deep_grad, (((0,), (0,)), ((), ())), preferred_element_type=jnp.float32
                )
            )
    local_bias = jnp.sum(deep_grad.astype(jnp.float32), axis=0)
    bias_rows = jnp.zeros((strip_count * 8 - 9 * channels % (strip_count * 8), width_deep), jnp.float32)
    bias_rows = bias_rows.at[0].set(local_bias)
    local_grads = jnp.concatenate(pieces + [bias_rows], axis=0)

    total_grads, every_sums = tree_sum(local_grads, part_sums, "strip")
    mine = strip_pos * owned + jnp.arange(owned, dtype=jnp.int32)
    pick = (mine[:, None] == every_slots[None, :]).astype(jnp.float32)
    slot_sums = jnp.dot(pick, every_sums, precision=lax.Precision.HIGHEST)
    slot_counts = jnp.dot(pick, every_counts, precision=lax.Precision.HIGHEST)
    embeddings = slot_sums / jnp.maximum(slot_counts, 1.0)[:, None]

    weight_grad = total_grads[: 9 * channels].reshape(3, 3, channels, width_deep)
    bias_grad = total_grads[9 * channels]
    return (embeddings, weight_grad, bias_grad)


def solution(mesh):
    placed = (
        P(None, "strip", None),
        P(),
        P(),
        P(None, None, None, "chan"),
        P("chan"),
        P(None, "strip"),
        P("strip"),
        P("strip", "chan"),
    )
    return jax.shard_map(
        body,
        mesh=mesh,
        in_specs=placed,
        out_specs=(P("strip", "chan"), P(None, None, None, "chan"), P("chan")),
        check_vma=False,
    )
```

```python
import functools

import jax
import numpy as np
import jax.numpy as jnp
from jax import lax
from jax.experimental import pallas as pl
from jax.experimental.pallas import tpu as pltpu
from jax.sharding import PartitionSpec as P


def with_halo(cells, sides, width):
    for axis, dim in sides:
        count = lax.axis_size(axis)
        ends = count - 1
        head = lax.slice_in_dim(cells, 0, width, axis=dim)
        tail = lax.slice_in_dim(cells, cells.shape[dim] - width, cells.shape[dim], axis=dim)
        cells = jnp.concatenate(
            [
                lax.ppermute(tail, axis, [(i, (i + 1) % count) for i in range(ends)]),
                cells,
                lax.ppermute(head, axis, [((i + 1) % count, i) for i in range(ends)]),
            ],
            axis=dim,
        )
    return cells


def tree_gather(block, axis, order):
    count = lax.axis_size(axis)
    me = lax.axis_index(axis)
    held = block
    for dist in order:
        other = lax.ppermute(held, axis, [(i, i ^ dist) for i in range(count)])
        high = (me // dist) % 2
        size = held.shape[0]
        both = jnp.zeros((2 * size,) + held.shape[1:], held.dtype)
        both = lax.dynamic_update_slice_in_dim(both, held, high * size, 0)
        held = lax.dynamic_update_slice_in_dim(both, other, (1 - high) * size, 0)
    return held


def gather_position(order, count):
    return np.array(
        [sum(((j // dist) % 2) << k for k, dist in enumerate(order)) for j in range(count)],
        np.int32,
    )


def tree_kernel(count, orders, width, grads_ref, sums_ref, out_ref, every_ref, landing, sems, free):
    me = lax.axis_index("strip")
    chan = lax.axis_index("chan")
    mesh_id = pl.DeviceIdType.MESH
    steps = len(orders[0])
    rows = grads_ref.shape[0]
    sizes = [rows // 3, rows - rows // 3]
    bases = [0, rows // 3]
    chunks = [size // count for size in sizes]

    def partner(dist):
        return me + dist - 2 * dist * ((me // dist) % 2)

    def bit(dist):
        return (me // dist) % 2

    barrier = pltpu.get_barrier_semaphore()
    for dist in orders[0]:
        pl.semaphore_signal(barrier, inc=1, device_id=(partner(dist), chan), device_id_type=mesh_id)
    pl.semaphore_wait(barrier, steps)

    out_ref[...] = grads_ref[...]
    place = 0
    for k, dist in enumerate(orders[0]):
        place = place + bit(dist) * (count >> (k + 1))
    every_ref[pl.ds(pl.multiple_of(place * width, 8), width)] = sums_ref[...]

    lows = [0, 0]
    offsets = [0, 0]
    for k in range(steps):
        copies = []
        keeps = []
        for t in range(2):
            dist = orders[t][k]
            half = sizes[t] // 2
            keep = lows[t] + bit(dist) * half
            give = lows[t] + (1 - bit(dist)) * half
            copies.append(
                pltpu.make_async_remote_copy(
                    src_ref=out_ref.at[pl.ds(pl.multiple_of(bases[t] + give, 8), half)],
                    dst_ref=landing.at[pl.ds(bases[t] + offsets[t], half)],
                    send_sem=sems.at[0, t, k],
                    recv_sem=sems.at[1, t, k],
                    device_id=(partner(dist), chan),
                    device_id_type=mesh_id,
                )
            )
            keeps.append(keep)
        for copy in copies:
            copy.start()
        for t in range(2):
            copies[t].wait()
            pl.semaphore_signal(
                free.at[t, k], inc=1, device_id=(partner(orders[t][k]), chan),
                device_id_type=mesh_id,
            )
        for t in range(2):
            half = sizes[t] // 2
            chunk = chunks[t]

            def accumulate(step, carry, t=t, keep=keeps[t], offset=offsets[t], chunk=chunk):
                mine = pl.ds(pl.multiple_of(bases[t] + keep + step * chunk, 8), chunk)
                got = pl.ds(pl.multiple_of(bases[t] + offset + step * chunk, 8), chunk)
                out_ref[mine] = out_ref[mine] + landing[got]
                return carry

            lax.fori_loop(0, half // chunk, accumulate, 0)
            lows[t] = keeps[t]
            offsets[t] += half
            sizes[t] = half

    blocks = 1
    for k in reversed(range(steps)):
        copies = []
        for t in range(2):
            dist = orders[t][k]
            pl.semaphore_wait(free.at[t, k], 1)
            span = pl.ds(pl.multiple_of(bases[t] + lows[t], 8), sizes[t])
            copies.append(
                pltpu.make_async_remote_copy(
                    src_ref=out_ref.at[span],
                    dst_ref=out_ref.at[span],
                    send_sem=sems.at[2, t, k],
                    recv_sem=sems.at[3, t, k],
                    device_id=(partner(dist), chan),
                    device_id_type=mesh_id,
                )
            )
        spot = pl.ds(pl.multiple_of(place * width, 8), blocks * width)
        copies.append(
            pltpu.make_async_remote_copy(
                src_ref=every_ref.at[spot],
                dst_ref=every_ref.at[spot],
                send_sem=sems.at[4, 0, k],
                recv_sem=sems.at[5, 0, k],
                device_id=(partner(orders[0][k]), chan),
                device_id_type=mesh_id,
            )
        )
        for copy in copies:
            copy.start()
        for copy in copies:
            copy.wait()
        for t in range(2):
            lows[t] = lows[t] - bit(orders[t][k]) * sizes[t]
            sizes[t] = sizes[t] * 2
        place = place - bit(orders[0][k]) * blocks
        blocks = blocks * 2


def tree_sum(grads, sums, axis, orders):
    count = lax.axis_size(axis)
    rows, lanes = grads.shape
    width = sums.shape[0]
    steps = len(orders[0])
    return pl.pallas_call(
        functools.partial(tree_kernel, count, orders, width),
        out_shape=(
            jax.ShapeDtypeStruct((rows, lanes), jnp.float32),
            jax.ShapeDtypeStruct((count * width, lanes), jnp.float32),
        ),
        in_specs=[pl.BlockSpec(memory_space=pltpu.VMEM)] * 2,
        out_specs=(pl.BlockSpec(memory_space=pltpu.VMEM),) * 2,
        scratch_shapes=[
            pltpu.VMEM((rows, lanes), jnp.float32),
            pltpu.SemaphoreType.DMA((6, 2, steps)),
            pltpu.SemaphoreType.REGULAR((2, steps)),
        ],
        compiler_params=pltpu.CompilerParams(collective_id=0, has_side_effects=True),
    )(grads, sums)


def swish(value):
    return value * jax.nn.sigmoid(value)


def swish_slope(value):
    sigma = jax.nn.sigmoid(value)
    return sigma * (1.0 + value * (1.0 - sigma))


def convolve(padded, weight, row_count, col_count):
    channels = padded.shape[-1]
    running = None
    for shift_row in range(3):
        for shift_col in range(3):
            window = padded[
                shift_row : shift_row + row_count, shift_col : shift_col + col_count
            ].reshape(row_count * col_count, channels)
            partial_term = jnp.dot(
                window, weight[shift_row, shift_col], preferred_element_type=jnp.float32
            )
            running = partial_term if running is None else running + partial_term
    return running.reshape(row_count, col_count, weight.shape[-1])


def pool_pairs(hidden):
    row_count, col_count, channels = hidden.shape
    return (
        hidden.reshape(row_count // 2, 2, col_count // 2, 2, channels)
        .mean(axis=(1, 3))
        .astype(jnp.bfloat16)
    )


def body(
    section_input, conv_weight, conv_bias, deep_weight, deep_bias, labels, slot_ids, embed_grad
):
    chan_count = lax.axis_size("chan")
    chan_pos = lax.axis_index("chan")
    strip_count = lax.axis_size("strip")
    strip_pos = lax.axis_index("strip")
    row_total, col_local, channels = section_input.shape
    row_part = row_total // chan_count
    half_cols = col_local // 2
    list_len = slot_ids.shape[0]
    owned, width_deep = embed_grad.shape
    lanes = embed_grad.shape[1]

    flat_labels = labels.reshape(-1)
    member = flat_labels[None, :] == jnp.arange(list_len, dtype=jnp.int32)[:, None]
    part_counts = jnp.sum(member.astype(jnp.float32), axis=1)
    meta = jnp.zeros((8, lanes), jnp.float32)
    meta = meta.at[0, :list_len].set(part_counts)
    meta = meta.at[0, list_len : 2 * list_len].set(slot_ids.astype(jnp.float32))
    packed = jnp.concatenate([embed_grad, meta], axis=0)
    steps = strip_count.bit_length() - 1
    halving = [[1 << k for k in range(steps)], [1 << k for k in range(steps)]]
    if steps == 6:
        halving = [[1, 2, 16, 4, 32, 8], [2, 1, 4, 16, 8, 32]]
    order = halving[0][::-1]
    position = jnp.asarray(gather_position(order, strip_count))
    early = tree_gather(packed, "strip", order[:2])

    padded_rows = jnp.pad(section_input, ((1, 1), (0, 0), (0, 0)))
    own_rows = lax.dynamic_slice_in_dim(padded_rows, chan_pos * row_part, row_part + 2, 0)
    extended = with_halo(own_rows, (("strip", 1),), 3)
    extended, early = lax.optimization_barrier((extended, early))
    early = tree_gather(early, "strip", order[2:4])
    hidden = swish(convolve(extended, conv_weight, row_part, col_local + 4) + conv_bias)
    pooled = pool_pairs(hidden)
    column = jnp.arange(half_cols + 2)
    outside = (column == 0) & (strip_pos == 0) | (column == half_cols + 1) & (
        strip_pos == strip_count - 1
    )
    pooled = jnp.where(outside[None, :, None], jnp.zeros_like(pooled), pooled)
    pooled, early = lax.optimization_barrier((pooled, early))
    every = tree_gather(early, "strip", order[4:]).reshape(strip_count, owned + 8, lanes)
    every_grad = every[:, :owned].reshape(strip_count * owned, lanes)
    every_counts = every[:, owned, :list_len].reshape(-1)
    every_slots = jnp.round(every[:, owned, list_len : 2 * list_len]).astype(jnp.int32).reshape(-1)
    gathered = lax.all_gather(pooled, "chan", axis=0, tiled=True)
    padded_deep = jnp.pad(gathered, ((1, 1), (0, 0), (0, 0)))
    half_rows = gathered.shape[0]
    deep_pre = convolve(padded_deep, deep_weight, half_rows, half_cols) + deep_bias
    features = swish(deep_pre).astype(jnp.bfloat16).reshape(-1, width_deep)
    part_sums = jnp.dot(member.astype(jnp.bfloat16), features, preferred_element_type=jnp.float32)

    same_slot = (slot_ids[:, None] == every_slots[None, :]).astype(jnp.float32)
    entry_counts = jnp.dot(same_slot, every_counts, precision=lax.Precision.HIGHEST)
    grad_row = position[slot_ids // owned] * owned + slot_ids % owned
    entry_grad = every_grad[grad_row] / jnp.maximum(entry_counts, 1.0)[:, None]
    pixel_grad = lax.dot_general(
        member.astype(jnp.float32),
        entry_grad,
        (((0,), (0,)), ((), ())),
        precision=lax.Precision.HIGHEST,
        preferred_element_type=jnp.float32,
    )
    deep_grad = (pixel_grad * swish_slope(deep_pre.reshape(-1, width_deep))).astype(jnp.bfloat16)
    pieces = []
    for shift_row in range(3):
        for shift_col in range(3):
            window = padded_deep[
                shift_row : shift_row + half_rows, shift_col : shift_col + half_cols
            ].reshape(-1, channels)
            pieces.append(
                lax.dot_general(
                    window, deep_grad, (((0,), (0,)), ((), ())), preferred_element_type=jnp.float32
                )
            )
    local_bias = jnp.sum(deep_grad.astype(jnp.float32), axis=0)
    bias_rows = jnp.zeros((strip_count * 48 - 9 * channels % (strip_count * 48), width_deep), jnp.float32)
    bias_rows = bias_rows.at[0].set(local_bias)
    local_grads = jnp.concatenate(pieces + [bias_rows], axis=0)

    total_grads, every_sums = tree_sum(local_grads, part_sums, "strip", halving)
    mine = strip_pos * owned + jnp.arange(owned, dtype=jnp.int32)
    pick = (mine[:, None] == every_slots[None, :]).astype(jnp.float32)
    slot_sums = jnp.dot(pick, every_sums, precision=lax.Precision.HIGHEST)
    slot_counts = jnp.dot(pick, every_counts, precision=lax.Precision.HIGHEST)
    embeddings = slot_sums / jnp.maximum(slot_counts, 1.0)[:, None]

    weight_grad = total_grads[: 9 * channels].reshape(3, 3, channels, width_deep)
    bias_grad = total_grads[9 * channels]
    return (embeddings, weight_grad, bias_grad)


def solution(mesh):
    placed = (
        P(None, "strip", None),
        P(),
        P(),
        P(None, None, None, "chan"),
        P("chan"),
        P(None, "strip"),
        P("strip"),
        P("strip", "chan"),
    )
    return jax.shard_map(
        body,
        mesh=mesh,
        in_specs=placed,
        out_specs=(P("strip", "chan"), P(None, None, None, "chan"), P("chan")),
        check_vma=False,
    )
```

```python
import functools

import jax
import numpy as np
import jax.numpy as jnp
from jax import lax
from jax.experimental import pallas as pl
from jax.experimental.pallas import tpu as pltpu
from jax.sharding import PartitionSpec as P


def with_halo(cells, sides, width):
    for axis, dim in sides:
        count = lax.axis_size(axis)
        ends = count - 1
        head = lax.slice_in_dim(cells, 0, width, axis=dim)
        tail = lax.slice_in_dim(cells, cells.shape[dim] - width, cells.shape[dim], axis=dim)
        cells = jnp.concatenate(
            [
                lax.ppermute(tail, axis, [(i, (i + 1) % count) for i in range(ends)]),
                cells,
                lax.ppermute(head, axis, [((i + 1) % count, i) for i in range(ends)]),
            ],
            axis=dim,
        )
    return cells


def tree_gather(block, axis, order):
    count = lax.axis_size(axis)
    me = lax.axis_index(axis)
    held = block
    for dist in order:
        other = lax.ppermute(held, axis, [(i, i ^ dist) for i in range(count)])
        high = (me // dist) % 2
        size = held.shape[0]
        both = jnp.zeros((2 * size,) + held.shape[1:], held.dtype)
        both = lax.dynamic_update_slice_in_dim(both, held, high * size, 0)
        held = lax.dynamic_update_slice_in_dim(both, other, (1 - high) * size, 0)
    return held


def gather_position(order, count):
    return np.array(
        [sum(((j // dist) % 2) << k for k, dist in enumerate(order)) for j in range(count)],
        np.int32,
    )


def tree_kernel(count, chunk, width, dists, grads_ref, sums_ref, out_ref, every_ref, landing, sems, free):
    me = lax.axis_index("strip")
    chan = lax.axis_index("chan")
    mesh_id = pl.DeviceIdType.MESH

    def partner(dist):
        return me + dist - 2 * dist * ((me // dist) % 2)

    barrier = pltpu.get_barrier_semaphore()
    for dist in dists:
        pl.semaphore_signal(barrier, inc=1, device_id=(partner(dist), chan), device_id_type=mesh_id)
    pl.semaphore_wait(barrier, len(dists))

    out_ref[...] = grads_ref[...]
    place = 0
    for k, dist in enumerate(dists):
        place = place + ((me // dist) % 2) * (count >> (k + 1))
    every_ref[pl.ds(pl.multiple_of(place * width, 8), width)] = sums_ref[...]

    low = 0
    size = count * chunk
    offset = 0
    for k, dist in enumerate(dists):
        half = size // 2
        high = (me // dist) % 2
        keep = low + high * half
        give = low + (1 - high) * half
        copy = pltpu.make_async_remote_copy(
            src_ref=out_ref.at[pl.ds(pl.multiple_of(give, 8), half)],
            dst_ref=landing.at[pl.ds(offset, half)],
            send_sem=sems.at[0, k],
            recv_sem=sems.at[1, k],
            device_id=(partner(dist), chan),
            device_id_type=mesh_id,
        )
        copy.start()
        copy.wait()
        pl.semaphore_signal(
            free.at[k], inc=1, device_id=(partner(dist), chan), device_id_type=mesh_id
        )

        def accumulate(step, carry, keep=keep, offset=offset):
            mine = pl.ds(pl.multiple_of(keep + step * chunk, 8), chunk)
            got = pl.ds(pl.multiple_of(offset + step * chunk, 8), chunk)
            out_ref[mine] = out_ref[mine] + landing[got]
            return carry

        lax.fori_loop(0, half // chunk, accumulate, 0)
        low = keep
        size = half
        offset += half

    blocks = 1
    for k in reversed(range(len(dists))):
        dist = dists[k]
        pl.semaphore_wait(free.at[k], 1)
        rows = pl.ds(pl.multiple_of(low, 8), size)
        spot = pl.ds(pl.multiple_of(place * width, 8), blocks * width)
        grads_copy = pltpu.make_async_remote_copy(
            src_ref=out_ref.at[rows],
            dst_ref=out_ref.at[rows],
            send_sem=sems.at[2, k],
            recv_sem=sems.at[3, k],
            device_id=(partner(dist), chan),
            device_id_type=mesh_id,
        )
        sums_copy = pltpu.make_async_remote_copy(
            src_ref=every_ref.at[spot],
            dst_ref=every_ref.at[spot],
            send_sem=sems.at[4, k],
            recv_sem=sems.at[5, k],
            device_id=(partner(dist), chan),
            device_id_type=mesh_id,
        )
        grads_copy.start()
        sums_copy.start()
        grads_copy.wait()
        sums_copy.wait()
        high = (me // dist) % 2
        low = low - high * size
        place = place - high * blocks
        size = size * 2
        blocks = blocks * 2


def tree_sum(grads, sums, axis, dists):
    count = lax.axis_size(axis)
    rows, lanes = grads.shape
    chunk = rows // count
    width = sums.shape[0]
    steps = count.bit_length() - 1
    return pl.pallas_call(
        functools.partial(tree_kernel, count, chunk, width, dists),
        out_shape=(
            jax.ShapeDtypeStruct((rows, lanes), jnp.float32),
            jax.ShapeDtypeStruct((count * width, lanes), jnp.float32),
        ),
        in_specs=[pl.BlockSpec(memory_space=pltpu.VMEM)] * 2,
        out_specs=(pl.BlockSpec(memory_space=pltpu.VMEM),) * 2,
        scratch_shapes=[
            pltpu.VMEM((rows, lanes), jnp.float32),
            pltpu.SemaphoreType.DMA((6, steps)),
            pltpu.SemaphoreType.REGULAR((steps,)),
        ],
        compiler_params=pltpu.CompilerParams(collective_id=0, has_side_effects=True),
    )(grads, sums)


def swish(value):
    return value * jax.nn.sigmoid(value)


def swish_slope(value):
    sigma = jax.nn.sigmoid(value)
    return sigma * (1.0 + value * (1.0 - sigma))


def convolve(padded, weight, row_count, col_count):
    channels = padded.shape[-1]
    running = None
    for shift_row in range(3):
        for shift_col in range(3):
            window = padded[
                shift_row : shift_row + row_count, shift_col : shift_col + col_count
            ].reshape(row_count * col_count, channels)
            partial_term = jnp.dot(
                window, weight[shift_row, shift_col], preferred_element_type=jnp.float32
            )
            running = partial_term if running is None else running + partial_term
    return running.reshape(row_count, col_count, weight.shape[-1])


def pool_pairs(hidden):
    row_count, col_count, channels = hidden.shape
    return (
        hidden.reshape(row_count // 2, 2, col_count // 2, 2, channels)
        .mean(axis=(1, 3))
        .astype(jnp.bfloat16)
    )


def body(
    section_input, conv_weight, conv_bias, deep_weight, deep_bias, labels, slot_ids, embed_grad
):
    chan_count = lax.axis_size("chan")
    chan_pos = lax.axis_index("chan")
    strip_count = lax.axis_size("strip")
    strip_pos = lax.axis_index("strip")
    row_total, col_local, channels = section_input.shape
    row_part = row_total // chan_count
    half_cols = col_local // 2
    list_len = slot_ids.shape[0]
    owned, width_deep = embed_grad.shape
    lanes = embed_grad.shape[1]

    flat_labels = labels.reshape(-1)
    member = flat_labels[None, :] == jnp.arange(list_len, dtype=jnp.int32)[:, None]
    part_counts = jnp.sum(member.astype(jnp.float32), axis=1)
    meta = jnp.zeros((8, lanes), jnp.float32)
    meta = meta.at[0, :list_len].set(part_counts)
    meta = meta.at[0, list_len : 2 * list_len].set(slot_ids.astype(jnp.float32))
    packed = jnp.concatenate([embed_grad, meta], axis=0)
    halving = [1 << k for k in range(strip_count.bit_length() - 1)]
    if len(halving) == 6:
        halving = [1, 2, 16, 4, 32, 8]
    order = halving[::-1]
    position = jnp.asarray(gather_position(order, strip_count))
    early = tree_gather(packed, "strip", order[:2])

    padded_rows = jnp.pad(section_input, ((1, 1), (0, 0), (0, 0)))
    own_rows = lax.dynamic_slice_in_dim(padded_rows, chan_pos * row_part, row_part + 2, 0)
    extended = with_halo(own_rows, (("strip", 1),), 3)
    extended, early = lax.optimization_barrier((extended, early))
    early = tree_gather(early, "strip", order[2:4])
    hidden = swish(convolve(extended, conv_weight, row_part, col_local + 4) + conv_bias)
    pooled = pool_pairs(hidden)
    column = jnp.arange(half_cols + 2)
    outside = (column == 0) & (strip_pos == 0) | (column == half_cols + 1) & (
        strip_pos == strip_count - 1
    )
    pooled = jnp.where(outside[None, :, None], jnp.zeros_like(pooled), pooled)
    pooled, early = lax.optimization_barrier((pooled, early))
    every = tree_gather(early, "strip", order[4:]).reshape(strip_count, owned + 8, lanes)
    every_grad = every[:, :owned].reshape(strip_count * owned, lanes)
    every_counts = every[:, owned, :list_len].reshape(-1)
    every_slots = jnp.round(every[:, owned, list_len : 2 * list_len]).astype(jnp.int32).reshape(-1)
    gathered = lax.all_gather(pooled, "chan", axis=0, tiled=True)
    padded_deep = jnp.pad(gathered, ((1, 1), (0, 0), (0, 0)))
    half_rows = gathered.shape[0]
    deep_pre = convolve(padded_deep, deep_weight, half_rows, half_cols) + deep_bias
    features = swish(deep_pre).astype(jnp.bfloat16).reshape(-1, width_deep)
    part_sums = jnp.dot(member.astype(jnp.bfloat16), features, preferred_element_type=jnp.float32)

    same_slot = (slot_ids[:, None] == every_slots[None, :]).astype(jnp.float32)
    entry_counts = jnp.dot(same_slot, every_counts, precision=lax.Precision.HIGHEST)
    grad_row = position[slot_ids // owned] * owned + slot_ids % owned
    entry_grad = every_grad[grad_row] / jnp.maximum(entry_counts, 1.0)[:, None]
    pixel_grad = lax.dot_general(
        member.astype(jnp.float32),
        entry_grad,
        (((0,), (0,)), ((), ())),
        precision=lax.Precision.HIGHEST,
        preferred_element_type=jnp.float32,
    )
    deep_grad = (pixel_grad * swish_slope(deep_pre.reshape(-1, width_deep))).astype(jnp.bfloat16)
    pieces = []
    for shift_row in range(3):
        for shift_col in range(3):
            window = padded_deep[
                shift_row : shift_row + half_rows, shift_col : shift_col + half_cols
            ].reshape(-1, channels)
            pieces.append(
                lax.dot_general(
                    window, deep_grad, (((0,), (0,)), ((), ())), preferred_element_type=jnp.float32
                )
            )
    local_bias = jnp.sum(deep_grad.astype(jnp.float32), axis=0)
    bias_rows = jnp.zeros((strip_count * 8 - 9 * channels % (strip_count * 8), width_deep), jnp.float32)
    bias_rows = bias_rows.at[0].set(local_bias)
    local_grads = jnp.concatenate(pieces + [bias_rows], axis=0)

    total_grads, every_sums = tree_sum(local_grads, part_sums, "strip", halving)
    mine = strip_pos * owned + jnp.arange(owned, dtype=jnp.int32)
    pick = (mine[:, None] == every_slots[None, :]).astype(jnp.float32)
    slot_sums = jnp.dot(pick, every_sums, precision=lax.Precision.HIGHEST)
    slot_counts = jnp.dot(pick, every_counts, precision=lax.Precision.HIGHEST)
    embeddings = slot_sums / jnp.maximum(slot_counts, 1.0)[:, None]

    weight_grad = total_grads[: 9 * channels].reshape(3, 3, channels, width_deep)
    bias_grad = total_grads[9 * channels]
    return (embeddings, weight_grad, bias_grad)


def solution(mesh):
    placed = (
        P(None, "strip", None),
        P(),
        P(),
        P(None, None, None, "chan"),
        P("chan"),
        P(None, "strip"),
        P("strip"),
        P("strip", "chan"),
    )
    return jax.shard_map(
        body,
        mesh=mesh,
        in_specs=placed,
        out_specs=(P("strip", "chan"), P(None, None, None, "chan"), P("chan")),
        check_vma=False,
    )
```

```python
import functools

import jax
import numpy as np
import jax.numpy as jnp
from jax import lax
from jax.experimental import pallas as pl
from jax.experimental.pallas import tpu as pltpu
from jax.sharding import PartitionSpec as P


def with_halo(cells, sides, width):
    for axis, dim in sides:
        count = lax.axis_size(axis)
        ends = count - 1
        head = lax.slice_in_dim(cells, 0, width, axis=dim)
        tail = lax.slice_in_dim(cells, cells.shape[dim] - width, cells.shape[dim], axis=dim)
        cells = jnp.concatenate(
            [
                lax.ppermute(tail, axis, [(i, (i + 1) % count) for i in range(ends)]),
                cells,
                lax.ppermute(head, axis, [((i + 1) % count, i) for i in range(ends)]),
            ],
            axis=dim,
        )
    return cells


def chip_view(index, shifted):
    if not shifted:
        return index
    core = index % 2
    return ((index // 16 + core) % 4 * 8 + (index // 2 + core) % 8) * 2 + core


def chip_unview(index, shifted):
    if not shifted:
        return index
    core = index % 2
    return ((index // 16 + 4 - core) % 4 * 8 + (index // 2 + 8 - core) % 8) * 2 + core


def strip_partner(index, dist, shifted):
    if dist == 1:
        return index + 1 - 2 * (index % 2)
    view = chip_view(index, shifted)
    return chip_unview(view + dist - 2 * dist * ((view // dist) % 2), shifted)


def strip_bit(index, dist, shifted):
    if dist == 1:
        return index % 2
    return (chip_view(index, shifted) // dist) % 2


def tree_gather(block, axis, order, shifted):
    count = lax.axis_size(axis)
    me = lax.axis_index(axis)
    held = block
    for dist in order:
        pairs = [(i, strip_partner(i, dist, shifted)) for i in range(count)]
        other = lax.ppermute(held, axis, pairs)
        high = strip_bit(me, dist, shifted)
        size = held.shape[0]
        both = jnp.zeros((2 * size,) + held.shape[1:], held.dtype)
        both = lax.dynamic_update_slice_in_dim(both, held, high * size, 0)
        held = lax.dynamic_update_slice_in_dim(both, other, (1 - high) * size, 0)
    return held


def gather_position(order, count, shifted):
    return np.array(
        [sum(strip_bit(j, dist, shifted) << k for k, dist in enumerate(order)) for j in range(count)],
        np.int32,
    )


def tree_kernel(count, chunk, width, dists, shifted, grads_ref, sums_ref, out_ref, every_ref, landing, sems, free):
    me = lax.axis_index("strip")
    chan = lax.axis_index("chan")
    mesh_id = pl.DeviceIdType.MESH

    def partner(dist):
        return strip_partner(me, dist, shifted)

    barrier = pltpu.get_barrier_semaphore()
    for dist in dists:
        pl.semaphore_signal(barrier, inc=1, device_id=(partner(dist), chan), device_id_type=mesh_id)
    pl.semaphore_wait(barrier, len(dists))

    out_ref[...] = grads_ref[...]
    place = 0
    for k, dist in enumerate(dists):
        place = place + (strip_bit(me, dist, shifted)) * (count >> (k + 1))
    every_ref[pl.ds(pl.multiple_of(place * width, 8), width)] = sums_ref[...]

    low = 0
    size = count * chunk
    offset = 0
    for k, dist in enumerate(dists):
        half = size // 2
        high = strip_bit(me, dist, shifted)
        keep = low + high * half
        give = low + (1 - high) * half
        copy = pltpu.make_async_remote_copy(
            src_ref=out_ref.at[pl.ds(pl.multiple_of(give, 8), half)],
            dst_ref=landing.at[pl.ds(offset, half)],
            send_sem=sems.at[0, k],
            recv_sem=sems.at[1, k],
            device_id=(partner(dist), chan),
            device_id_type=mesh_id,
        )
        copy.start()
        copy.wait()
        pl.semaphore_signal(
            free.at[k], inc=1, device_id=(partner(dist), chan), device_id_type=mesh_id
        )

        def accumulate(step, carry, keep=keep, offset=offset):
            mine = pl.ds(pl.multiple_of(keep + step * chunk, 8), chunk)
            got = pl.ds(pl.multiple_of(offset + step * chunk, 8), chunk)
            out_ref[mine] = out_ref[mine] + landing[got]
            return carry

        lax.fori_loop(0, half // chunk, accumulate, 0)
        low = keep
        size = half
        offset += half

    blocks = 1
    for k in reversed(range(len(dists))):
        dist = dists[k]
        pl.semaphore_wait(free.at[k], 1)
        rows = pl.ds(pl.multiple_of(low, 8), size)
        spot = pl.ds(pl.multiple_of(place * width, 8), blocks * width)
        grads_copy = pltpu.make_async_remote_copy(
            src_ref=out_ref.at[rows],
            dst_ref=out_ref.at[rows],
            send_sem=sems.at[2, k],
            recv_sem=sems.at[3, k],
            device_id=(partner(dist), chan),
            device_id_type=mesh_id,
        )
        sums_copy = pltpu.make_async_remote_copy(
            src_ref=every_ref.at[spot],
            dst_ref=every_ref.at[spot],
            send_sem=sems.at[4, k],
            recv_sem=sems.at[5, k],
            device_id=(partner(dist), chan),
            device_id_type=mesh_id,
        )
        grads_copy.start()
        sums_copy.start()
        grads_copy.wait()
        sums_copy.wait()
        high = strip_bit(me, dist, shifted)
        low = low - high * size
        place = place - high * blocks
        size = size * 2
        blocks = blocks * 2


def tree_sum(grads, sums, axis, dists, shifted):
    count = lax.axis_size(axis)
    rows, lanes = grads.shape
    chunk = rows // count
    width = sums.shape[0]
    steps = count.bit_length() - 1
    return pl.pallas_call(
        functools.partial(tree_kernel, count, chunk, width, dists, shifted),
        out_shape=(
            jax.ShapeDtypeStruct((rows, lanes), jnp.float32),
            jax.ShapeDtypeStruct((count * width, lanes), jnp.float32),
        ),
        in_specs=[pl.BlockSpec(memory_space=pltpu.VMEM)] * 2,
        out_specs=(pl.BlockSpec(memory_space=pltpu.VMEM),) * 2,
        scratch_shapes=[
            pltpu.VMEM((rows, lanes), jnp.float32),
            pltpu.SemaphoreType.DMA((6, steps)),
            pltpu.SemaphoreType.REGULAR((steps,)),
        ],
        compiler_params=pltpu.CompilerParams(collective_id=0, has_side_effects=True),
    )(grads, sums)


def swish(value):
    return value * jax.nn.sigmoid(value)


def swish_slope(value):
    sigma = jax.nn.sigmoid(value)
    return sigma * (1.0 + value * (1.0 - sigma))


def convolve(padded, weight, row_count, col_count):
    channels = padded.shape[-1]
    running = None
    for shift_row in range(3):
        for shift_col in range(3):
            window = padded[
                shift_row : shift_row + row_count, shift_col : shift_col + col_count
            ].reshape(row_count * col_count, channels)
            partial_term = jnp.dot(
                window, weight[shift_row, shift_col], preferred_element_type=jnp.float32
            )
            running = partial_term if running is None else running + partial_term
    return running.reshape(row_count, col_count, weight.shape[-1])


def pool_pairs(hidden):
    row_count, col_count, channels = hidden.shape
    return (
        hidden.reshape(row_count // 2, 2, col_count // 2, 2, channels)
        .mean(axis=(1, 3))
        .astype(jnp.bfloat16)
    )


def body(
    section_input, conv_weight, conv_bias, deep_weight, deep_bias, labels, slot_ids, embed_grad
):
    chan_count = lax.axis_size("chan")
    chan_pos = lax.axis_index("chan")
    strip_count = lax.axis_size("strip")
    strip_pos = lax.axis_index("strip")
    row_total, col_local, channels = section_input.shape
    row_part = row_total // chan_count
    half_cols = col_local // 2
    list_len = slot_ids.shape[0]
    owned, width_deep = embed_grad.shape
    lanes = embed_grad.shape[1]

    flat_labels = labels.reshape(-1)
    member = flat_labels[None, :] == jnp.arange(list_len, dtype=jnp.int32)[:, None]
    part_counts = jnp.sum(member.astype(jnp.float32), axis=1)
    meta = jnp.zeros((8, lanes), jnp.float32)
    meta = meta.at[0, :list_len].set(part_counts)
    meta = meta.at[0, list_len : 2 * list_len].set(slot_ids.astype(jnp.float32))
    packed = jnp.concatenate([embed_grad, meta], axis=0)
    halving = [1 << k for k in range(strip_count.bit_length() - 1)]
    if len(halving) == 6:
        halving = [1, 2, 16, 4, 32, 8]
    order = halving[::-1]
    shifted = strip_count == 64
    position = jnp.asarray(gather_position(order, strip_count, shifted))
    early = tree_gather(packed, "strip", order[:2], shifted)

    padded_rows = jnp.pad(section_input, ((1, 1), (0, 0), (0, 0)))
    own_rows = lax.dynamic_slice_in_dim(padded_rows, chan_pos * row_part, row_part + 2, 0)
    extended = with_halo(own_rows, (("strip", 1),), 3)
    extended, early = lax.optimization_barrier((extended, early))
    early = tree_gather(early, "strip", order[2:4], shifted)
    hidden = swish(convolve(extended, conv_weight, row_part, col_local + 4) + conv_bias)
    pooled = pool_pairs(hidden)
    column = jnp.arange(half_cols + 2)
    outside = (column == 0) & (strip_pos == 0) | (column == half_cols + 1) & (
        strip_pos == strip_count - 1
    )
    pooled = jnp.where(outside[None, :, None], jnp.zeros_like(pooled), pooled)
    pooled, early = lax.optimization_barrier((pooled, early))
    every = tree_gather(early, "strip", order[4:], shifted).reshape(strip_count, owned + 8, lanes)
    every_grad = every[:, :owned].reshape(strip_count * owned, lanes)
    every_counts = every[:, owned, :list_len].reshape(-1)
    every_slots = jnp.round(every[:, owned, list_len : 2 * list_len]).astype(jnp.int32).reshape(-1)
    gathered = lax.all_gather(pooled, "chan", axis=0, tiled=True)
    padded_deep = jnp.pad(gathered, ((1, 1), (0, 0), (0, 0)))
    half_rows = gathered.shape[0]
    deep_pre = convolve(padded_deep, deep_weight, half_rows, half_cols) + deep_bias
    features = swish(deep_pre).astype(jnp.bfloat16).reshape(-1, width_deep)
    part_sums = jnp.dot(member.astype(jnp.bfloat16), features, preferred_element_type=jnp.float32)

    same_slot = (slot_ids[:, None] == every_slots[None, :]).astype(jnp.float32)
    entry_counts = jnp.dot(same_slot, every_counts, precision=lax.Precision.HIGHEST)
    grad_row = position[slot_ids // owned] * owned + slot_ids % owned
    entry_grad = every_grad[grad_row] / jnp.maximum(entry_counts, 1.0)[:, None]
    pixel_grad = lax.dot_general(
        member.astype(jnp.float32),
        entry_grad,
        (((0,), (0,)), ((), ())),
        precision=lax.Precision.HIGHEST,
        preferred_element_type=jnp.float32,
    )
    deep_grad = (pixel_grad * swish_slope(deep_pre.reshape(-1, width_deep))).astype(jnp.bfloat16)
    pieces = []
    for shift_row in range(3):
        for shift_col in range(3):
            window = padded_deep[
                shift_row : shift_row + half_rows, shift_col : shift_col + half_cols
            ].reshape(-1, channels)
            pieces.append(
                lax.dot_general(
                    window, deep_grad, (((0,), (0,)), ((), ())), preferred_element_type=jnp.float32
                )
            )
    local_bias = jnp.sum(deep_grad.astype(jnp.float32), axis=0)
    bias_rows = jnp.zeros((strip_count * 8 - 9 * channels % (strip_count * 8), width_deep), jnp.float32)
    bias_rows = bias_rows.at[0].set(local_bias)
    local_grads = jnp.concatenate(pieces + [bias_rows], axis=0)

    total_grads, every_sums = tree_sum(local_grads, part_sums, "strip", halving, shifted)
    mine = strip_pos * owned + jnp.arange(owned, dtype=jnp.int32)
    pick = (mine[:, None] == every_slots[None, :]).astype(jnp.float32)
    slot_sums = jnp.dot(pick, every_sums, precision=lax.Precision.HIGHEST)
    slot_counts = jnp.dot(pick, every_counts, precision=lax.Precision.HIGHEST)
    embeddings = slot_sums / jnp.maximum(slot_counts, 1.0)[:, None]

    weight_grad = total_grads[: 9 * channels].reshape(3, 3, channels, width_deep)
    bias_grad = total_grads[9 * channels]
    return (embeddings, weight_grad, bias_grad)


def solution(mesh):
    placed = (
        P(None, "strip", None),
        P(),
        P(),
        P(None, None, None, "chan"),
        P("chan"),
        P(None, "strip"),
        P("strip"),
        P("strip", "chan"),
    )
    return jax.shard_map(
        body,
        mesh=mesh,
        in_specs=placed,
        out_specs=(P("strip", "chan"), P(None, None, None, "chan"), P("chan")),
        check_vma=False,
    )
```

```python
import functools

import jax
import numpy as np
import jax.numpy as jnp
from jax import lax
from jax.experimental import pallas as pl
from jax.experimental.pallas import tpu as pltpu
from jax.sharding import PartitionSpec as P


def with_halo(cells, sides, width):
    for axis, dim in sides:
        count = lax.axis_size(axis)
        ends = count - 1
        head = lax.slice_in_dim(cells, 0, width, axis=dim)
        tail = lax.slice_in_dim(cells, cells.shape[dim] - width, cells.shape[dim], axis=dim)
        cells = jnp.concatenate(
            [
                lax.ppermute(tail, axis, [(i, (i + 1) % count) for i in range(ends)]),
                cells,
                lax.ppermute(head, axis, [((i + 1) % count, i) for i in range(ends)]),
            ],
            axis=dim,
        )
    return cells


def chip_view(index, shifted):
    if not shifted:
        return index
    core = index % 2
    return ((index // 16 + core) % 4 * 8 + (index // 2 + core) % 8) * 2 + core


def chip_unview(index, shifted):
    if not shifted:
        return index
    core = index % 2
    return ((index // 16 + 4 - core) % 4 * 8 + (index // 2 + 8 - core) % 8) * 2 + core


def strip_partner(index, dist, shifted):
    if dist == 1:
        return index + 1 - 2 * (index % 2)
    view = chip_view(index, shifted)
    return chip_unview(view + dist - 2 * dist * ((view // dist) % 2), shifted)


def strip_bit(index, dist, shifted):
    if dist == 1:
        return index % 2
    return (chip_view(index, shifted) // dist) % 2


def tree_gather(block, axis, order, shifted):
    count = lax.axis_size(axis)
    me = lax.axis_index(axis)
    held = block
    for dist in order:
        pairs = [(i, strip_partner(i, dist, shifted)) for i in range(count)]
        other = lax.ppermute(held, axis, pairs)
        high = strip_bit(me, dist, shifted)
        size = held.shape[0]
        both = jnp.zeros((2 * size,) + held.shape[1:], held.dtype)
        both = lax.dynamic_update_slice_in_dim(both, held, high * size, 0)
        held = lax.dynamic_update_slice_in_dim(both, other, (1 - high) * size, 0)
    return held


def gather_position(order, count, shifted):
    return np.array(
        [sum(strip_bit(j, dist, shifted) << k for k, dist in enumerate(order)) for j in range(count)],
        np.int32,
    )


def tree_kernel(count, chunk, width, dists, shifted, grads_ref, sums_ref, out_ref, every_ref, landing, sems, free):
    me = lax.axis_index("strip")
    chan = lax.axis_index("chan")
    mesh_id = pl.DeviceIdType.MESH

    def partner(dist):
        return strip_partner(me, dist, shifted)

    barrier = pltpu.get_barrier_semaphore()
    for dist in dists:
        pl.semaphore_signal(barrier, inc=1, device_id=(partner(dist), chan), device_id_type=mesh_id)
    pl.semaphore_wait(barrier, len(dists))

    out_ref[...] = grads_ref[...]
    place = 0
    for k, dist in enumerate(dists):
        place = place + (strip_bit(me, dist, shifted)) * (count >> (k + 1))
    every_ref[pl.ds(pl.multiple_of(place * width, 8), width)] = sums_ref[...]

    low = 0
    size = count * chunk
    offset = 0
    for k, dist in enumerate(dists):
        half = size // 2
        high = strip_bit(me, dist, shifted)
        keep = low + high * half
        give = low + (1 - high) * half
        copy = pltpu.make_async_remote_copy(
            src_ref=out_ref.at[pl.ds(pl.multiple_of(give, 8), half)],
            dst_ref=landing.at[pl.ds(offset, half)],
            send_sem=sems.at[0, k],
            recv_sem=sems.at[1, k],
            device_id=(partner(dist), chan),
            device_id_type=mesh_id,
        )
        copy.start()
        copy.wait()
        pl.semaphore_signal(
            free.at[k], inc=1, device_id=(partner(dist), chan), device_id_type=mesh_id
        )

        def accumulate(step, carry, keep=keep, offset=offset):
            mine = pl.ds(pl.multiple_of(keep + step * chunk, 8), chunk)
            got = pl.ds(pl.multiple_of(offset + step * chunk, 8), chunk)
            out_ref[mine] = out_ref[mine] + landing[got]
            return carry

        lax.fori_loop(0, half // chunk, accumulate, 0)
        low = keep
        size = half
        offset += half

    blocks = 1
    for k in reversed(range(len(dists))):
        dist = dists[k]
        pl.semaphore_wait(free.at[k], 1)
        rows = pl.ds(pl.multiple_of(low, 8), size)
        spot = pl.ds(pl.multiple_of(place * width, 8), blocks * width)
        grads_copy = pltpu.make_async_remote_copy(
            src_ref=out_ref.at[rows],
            dst_ref=out_ref.at[rows],
            send_sem=sems.at[2, k],
            recv_sem=sems.at[3, k],
            device_id=(partner(dist), chan),
            device_id_type=mesh_id,
        )
        sums_copy = pltpu.make_async_remote_copy(
            src_ref=every_ref.at[spot],
            dst_ref=every_ref.at[spot],
            send_sem=sems.at[4, k],
            recv_sem=sems.at[5, k],
            device_id=(partner(dist), chan),
            device_id_type=mesh_id,
        )
        grads_copy.start()
        sums_copy.start()
        grads_copy.wait()
        sums_copy.wait()
        high = strip_bit(me, dist, shifted)
        low = low - high * size
        place = place - high * blocks
        size = size * 2
        blocks = blocks * 2


def tree_sum(grads, sums, axis, dists, shifted):
    count = lax.axis_size(axis)
    rows, lanes = grads.shape
    chunk = rows // count
    width = sums.shape[0]
    steps = count.bit_length() - 1
    return pl.pallas_call(
        functools.partial(tree_kernel, count, chunk, width, dists, shifted),
        out_shape=(
            jax.ShapeDtypeStruct((rows, lanes), jnp.float32),
            jax.ShapeDtypeStruct((count * width, lanes), jnp.float32),
        ),
        in_specs=[pl.BlockSpec(memory_space=pltpu.VMEM)] * 2,
        out_specs=(pl.BlockSpec(memory_space=pltpu.VMEM),) * 2,
        scratch_shapes=[
            pltpu.VMEM((rows, lanes), jnp.float32),
            pltpu.SemaphoreType.DMA((6, steps)),
            pltpu.SemaphoreType.REGULAR((steps,)),
        ],
        compiler_params=pltpu.CompilerParams(collective_id=0, has_side_effects=True),
    )(grads, sums)


def swish(value):
    return value * jax.nn.sigmoid(value)


def swish_slope(value):
    sigma = jax.nn.sigmoid(value)
    return sigma * (1.0 + value * (1.0 - sigma))


def convolve(padded, weight, row_count, col_count):
    channels = padded.shape[-1]
    running = None
    for shift_row in range(3):
        for shift_col in range(3):
            window = padded[
                shift_row : shift_row + row_count, shift_col : shift_col + col_count
            ].reshape(row_count * col_count, channels)
            partial_term = jnp.dot(
                window, weight[shift_row, shift_col], preferred_element_type=jnp.float32
            )
            running = partial_term if running is None else running + partial_term
    return running.reshape(row_count, col_count, weight.shape[-1])


def pool_pairs(hidden):
    row_count, col_count, channels = hidden.shape
    return (
        hidden.reshape(row_count // 2, 2, col_count // 2, 2, channels)
        .mean(axis=(1, 3))
        .astype(jnp.bfloat16)
    )


def body(
    section_input, conv_weight, conv_bias, deep_weight, deep_bias, labels, slot_ids, embed_grad
):
    chan_count = lax.axis_size("chan")
    chan_pos = lax.axis_index("chan")
    strip_count = lax.axis_size("strip")
    strip_pos = lax.axis_index("strip")
    row_total, col_local, channels = section_input.shape
    row_part = row_total // chan_count
    half_cols = col_local // 2
    list_len = slot_ids.shape[0]
    owned, width_deep = embed_grad.shape
    lanes = embed_grad.shape[1]

    flat_labels = labels.reshape(-1)
    member = flat_labels[None, :] == jnp.arange(list_len, dtype=jnp.int32)[:, None]
    part_counts = jnp.sum(member.astype(jnp.float32), axis=1)
    meta = jnp.zeros((8, lanes), jnp.float32)
    meta = meta.at[0, :list_len].set(part_counts)
    meta = meta.at[0, list_len : 2 * list_len].set(slot_ids.astype(jnp.float32))
    packed = jnp.concatenate([embed_grad, meta], axis=0)
    halving = [1 << k for k in range(strip_count.bit_length() - 1)]
    if len(halving) == 6:
        halving = [1, 2, 16, 4, 32, 8]
    order = halving[::-1]
    shifted = strip_count == 64
    position = jnp.asarray(gather_position(order, strip_count, shifted))
    early = tree_gather(packed, "strip", order[:2], shifted)

    padded_rows = jnp.pad(section_input, ((1, 1), (0, 0), (0, 0)))
    own_rows = lax.dynamic_slice_in_dim(padded_rows, chan_pos * row_part, row_part + 2, 0)
    extended = with_halo(own_rows, (("strip", 1),), 3)
    extended, early = lax.optimization_barrier((extended, early))
    early = tree_gather(early, "strip", order[2:4], shifted)
    hidden = swish(convolve(extended, conv_weight, row_part, col_local + 4) + conv_bias)
    pooled = pool_pairs(hidden)
    column = jnp.arange(half_cols + 2)
    outside = (column == 0) & (strip_pos == 0) | (column == half_cols + 1) & (
        strip_pos == strip_count - 1
    )
    pooled = jnp.where(outside[None, :, None], jnp.zeros_like(pooled), pooled)
    pooled, early = lax.optimization_barrier((pooled, early))
    every = tree_gather(early, "strip", order[4:], shifted).reshape(strip_count, owned + 8, lanes)
    every_grad = every[:, :owned].reshape(strip_count * owned, lanes)
    every_counts = every[:, owned, :list_len].reshape(-1)
    every_slots = jnp.round(every[:, owned, list_len : 2 * list_len]).astype(jnp.int32).reshape(-1)
    part_rows = pooled.shape[0]
    gathered = jnp.zeros((chan_count * part_rows,) + pooled.shape[1:], pooled.dtype)
    for shift in range(chan_count):
        block = pooled
        if shift:
            block = lax.ppermute(
                pooled, "chan", [(i, (i + shift) % chan_count) for i in range(chan_count)]
            )
        source = (chan_pos + chan_count - shift) % chan_count
        gathered = lax.dynamic_update_slice_in_dim(gathered, block, source * part_rows, 0)
    padded_deep = jnp.pad(gathered, ((1, 1), (0, 0), (0, 0)))
    half_rows = gathered.shape[0]
    deep_pre = convolve(padded_deep, deep_weight, half_rows, half_cols) + deep_bias
    features = swish(deep_pre).astype(jnp.bfloat16).reshape(-1, width_deep)
    part_sums = jnp.dot(member.astype(jnp.bfloat16), features, preferred_element_type=jnp.float32)

    same_slot = (slot_ids[:, None] == every_slots[None, :]).astype(jnp.float32)
    entry_counts = jnp.dot(same_slot, every_counts, precision=lax.Precision.HIGHEST)
    grad_row = position[slot_ids // owned] * owned + slot_ids % owned
    entry_grad = every_grad[grad_row] / jnp.maximum(entry_counts, 1.0)[:, None]
    pixel_grad = lax.dot_general(
        member.astype(jnp.float32),
        entry_grad,
        (((0,), (0,)), ((), ())),
        precision=lax.Precision.HIGHEST,
        preferred_element_type=jnp.float32,
    )
    deep_grad = (pixel_grad * swish_slope(deep_pre.reshape(-1, width_deep))).astype(jnp.bfloat16)
    pieces = []
    for shift_row in range(3):
        for shift_col in range(3):
            window = padded_deep[
                shift_row : shift_row + half_rows, shift_col : shift_col + half_cols
            ].reshape(-1, channels)
            pieces.append(
                lax.dot_general(
                    window, deep_grad, (((0,), (0,)), ((), ())), preferred_element_type=jnp.float32
                )
            )
    local_bias = jnp.sum(deep_grad.astype(jnp.float32), axis=0)
    bias_rows = jnp.zeros((strip_count * 8 - 9 * channels % (strip_count * 8), width_deep), jnp.float32)
    bias_rows = bias_rows.at[0].set(local_bias)
    local_grads = jnp.concatenate(pieces + [bias_rows], axis=0)

    total_grads, every_sums = tree_sum(local_grads, part_sums, "strip", halving, shifted)
    mine = strip_pos * owned + jnp.arange(owned, dtype=jnp.int32)
    pick = (mine[:, None] == every_slots[None, :]).astype(jnp.float32)
    slot_sums = jnp.dot(pick, every_sums, precision=lax.Precision.HIGHEST)
    slot_counts = jnp.dot(pick, every_counts, precision=lax.Precision.HIGHEST)
    embeddings = slot_sums / jnp.maximum(slot_counts, 1.0)[:, None]

    weight_grad = total_grads[: 9 * channels].reshape(3, 3, channels, width_deep)
    bias_grad = total_grads[9 * channels]
    return (embeddings, weight_grad, bias_grad)


def solution(mesh):
    placed = (
        P(None, "strip", None),
        P(),
        P(),
        P(None, None, None, "chan"),
        P("chan"),
        P(None, "strip"),
        P("strip"),
        P("strip", "chan"),
    )
    return jax.shard_map(
        body,
        mesh=mesh,
        in_specs=placed,
        out_specs=(P("strip", "chan"), P(None, None, None, "chan"), P("chan")),
        check_vma=False,
    )
```

```python
import functools

import jax
import numpy as np
import jax.numpy as jnp
from jax import lax
from jax.experimental import pallas as pl
from jax.experimental.pallas import tpu as pltpu
from jax.sharding import PartitionSpec as P


def with_halo(cells, sides, width):
    for axis, dim in sides:
        count = lax.axis_size(axis)
        ends = count - 1
        head = lax.slice_in_dim(cells, 0, width, axis=dim)
        tail = lax.slice_in_dim(cells, cells.shape[dim] - width, cells.shape[dim], axis=dim)
        cells = jnp.concatenate(
            [
                lax.ppermute(tail, axis, [(i, (i + 1) % count) for i in range(ends)]),
                cells,
                lax.ppermute(head, axis, [((i + 1) % count, i) for i in range(ends)]),
            ],
            axis=dim,
        )
    return cells


def chip_view(index, shifted):
    if not shifted:
        return index
    core = index % 2
    return ((index // 16 + core) % 4 * 8 + (index // 2 + core) % 8) * 2 + core


def chip_unview(index, shifted):
    if not shifted:
        return index
    core = index % 2
    return ((index // 16 + 4 - core) % 4 * 8 + (index // 2 + 8 - core) % 8) * 2 + core


def strip_partner(index, dist, shifted):
    if dist == 1:
        return index + 1 - 2 * (index % 2)
    view = chip_view(index, shifted)
    return chip_unview(view + dist - 2 * dist * ((view // dist) % 2), shifted)


def strip_bit(index, dist, shifted):
    if dist == 1:
        return index % 2
    return (chip_view(index, shifted) // dist) % 2


def tree_gather(block, axis, order, shifted):
    count = lax.axis_size(axis)
    me = lax.axis_index(axis)
    held = block
    for dist in order:
        pairs = [(i, strip_partner(i, dist, shifted)) for i in range(count)]
        other = lax.ppermute(held, axis, pairs)
        high = strip_bit(me, dist, shifted)
        size = held.shape[0]
        both = jnp.zeros((2 * size,) + held.shape[1:], held.dtype)
        both = lax.dynamic_update_slice_in_dim(both, held, high * size, 0)
        held = lax.dynamic_update_slice_in_dim(both, other, (1 - high) * size, 0)
    return held


def gather_position(order, count, shifted):
    return np.array(
        [sum(strip_bit(j, dist, shifted) << k for k, dist in enumerate(order)) for j in range(count)],
        np.int32,
    )


def tree_kernel(count, chunk, width, dists, shifted, grads_ref, sums_ref, out_ref, every_ref, landing, sems, free):
    me = lax.axis_index("strip")
    chan = lax.axis_index("chan")
    mesh_id = pl.DeviceIdType.MESH

    def partner(dist):
        return strip_partner(me, dist, shifted)

    barrier = pltpu.get_barrier_semaphore()
    for dist in dists:
        pl.semaphore_signal(barrier, inc=1, device_id=(partner(dist), chan), device_id_type=mesh_id)
    pl.semaphore_wait(barrier, len(dists))

    out_ref[...] = grads_ref[...]
    place = 0
    for k, dist in enumerate(dists):
        place = place + (strip_bit(me, dist, shifted)) * (count >> (k + 1))
    every_ref[pl.ds(pl.multiple_of(place * width, 8), width)] = sums_ref[...]

    low = 0
    size = count * chunk
    offset = 0
    for k, dist in enumerate(dists):
        half = size // 2
        high = strip_bit(me, dist, shifted)
        keep = low + high * half
        give = low + (1 - high) * half
        copy = pltpu.make_async_remote_copy(
            src_ref=out_ref.at[pl.ds(pl.multiple_of(give, 8), half)],
            dst_ref=landing.at[pl.ds(offset, half)],
            send_sem=sems.at[0, k],
            recv_sem=sems.at[1, k],
            device_id=(partner(dist), chan),
            device_id_type=mesh_id,
        )
        copy.start()
        copy.wait()
        pl.semaphore_signal(
            free.at[k], inc=1, device_id=(partner(dist), chan), device_id_type=mesh_id
        )

        def accumulate(step, carry, keep=keep, offset=offset):
            mine = pl.ds(pl.multiple_of(keep + step * chunk, 8), chunk)
            got = pl.ds(pl.multiple_of(offset + step * chunk, 8), chunk)
            out_ref[mine] = out_ref[mine] + landing[got]
            return carry

        lax.fori_loop(0, half // chunk, accumulate, 0)
        low = keep
        size = half
        offset += half

    blocks = 1
    for k in reversed(range(len(dists))):
        dist = dists[k]
        pl.semaphore_wait(free.at[k], 1)
        rows = pl.ds(pl.multiple_of(low, 8), size)
        spot = pl.ds(pl.multiple_of(place * width, 8), blocks * width)
        grads_copy = pltpu.make_async_remote_copy(
            src_ref=out_ref.at[rows],
            dst_ref=out_ref.at[rows],
            send_sem=sems.at[2, k],
            recv_sem=sems.at[3, k],
            device_id=(partner(dist), chan),
            device_id_type=mesh_id,
        )
        sums_copy = pltpu.make_async_remote_copy(
            src_ref=every_ref.at[spot],
            dst_ref=every_ref.at[spot],
            send_sem=sems.at[4, k],
            recv_sem=sems.at[5, k],
            device_id=(partner(dist), chan),
            device_id_type=mesh_id,
        )
        grads_copy.start()
        sums_copy.start()
        grads_copy.wait()
        sums_copy.wait()
        high = strip_bit(me, dist, shifted)
        low = low - high * size
        place = place - high * blocks
        size = size * 2
        blocks = blocks * 2


def tree_sum(grads, sums, axis, dists, shifted):
    count = lax.axis_size(axis)
    rows, lanes = grads.shape
    chunk = rows // count
    width = sums.shape[0]
    steps = count.bit_length() - 1
    return pl.pallas_call(
        functools.partial(tree_kernel, count, chunk, width, dists, shifted),
        out_shape=(
            jax.ShapeDtypeStruct((rows, lanes), jnp.float32),
            jax.ShapeDtypeStruct((count * width, lanes), jnp.float32),
        ),
        in_specs=[pl.BlockSpec(memory_space=pltpu.VMEM)] * 2,
        out_specs=(pl.BlockSpec(memory_space=pltpu.VMEM),) * 2,
        scratch_shapes=[
            pltpu.VMEM((rows, lanes), jnp.float32),
            pltpu.SemaphoreType.DMA((6, steps)),
            pltpu.SemaphoreType.REGULAR((steps,)),
        ],
        compiler_params=pltpu.CompilerParams(collective_id=0, has_side_effects=True),
    )(grads, sums)


def swish(value):
    return value * jax.nn.sigmoid(value)


def swish_slope(value):
    sigma = jax.nn.sigmoid(value)
    return sigma * (1.0 + value * (1.0 - sigma))


def convolve(padded, weight, row_count, col_count):
    channels = padded.shape[-1]
    width = -(-padded.shape[1] // 16) * 16
    padded = jnp.pad(padded, ((0, 0), (0, width - padded.shape[1]), (0, 0)))
    running = None
    for shift_col in range(3):
        column_sum = None
        for shift_row in range(3):
            band = padded[shift_row : shift_row + row_count].reshape(row_count * width, channels)
            partial_term = jnp.dot(
                band, weight[shift_row, shift_col], preferred_element_type=jnp.float32
            )
            column_sum = partial_term if column_sum is None else column_sum + partial_term
        column_sum = column_sum.reshape(row_count, width, weight.shape[-1])
        shifted = column_sum[:, shift_col : shift_col + col_count]
        running = shifted if running is None else running + shifted
    return running


def pool_pairs(hidden):
    row_count, col_count, channels = hidden.shape
    return (
        hidden.reshape(row_count // 2, 2, col_count // 2, 2, channels)
        .mean(axis=(1, 3))
        .astype(jnp.bfloat16)
    )


def body(
    section_input, conv_weight, conv_bias, deep_weight, deep_bias, labels, slot_ids, embed_grad
):
    chan_count = lax.axis_size("chan")
    chan_pos = lax.axis_index("chan")
    strip_count = lax.axis_size("strip")
    strip_pos = lax.axis_index("strip")
    row_total, col_local, channels = section_input.shape
    row_part = row_total // chan_count
    half_cols = col_local // 2
    list_len = slot_ids.shape[0]
    owned, width_deep = embed_grad.shape
    lanes = embed_grad.shape[1]

    flat_labels = labels.reshape(-1)
    member = flat_labels[None, :] == jnp.arange(list_len, dtype=jnp.int32)[:, None]
    part_counts = jnp.sum(member.astype(jnp.float32), axis=1)
    meta = jnp.zeros((8, lanes), jnp.float32)
    meta = meta.at[0, :list_len].set(part_counts)
    meta = meta.at[0, list_len : 2 * list_len].set(slot_ids.astype(jnp.float32))
    packed = jnp.concatenate([embed_grad, meta], axis=0)
    halving = [1 << k for k in range(strip_count.bit_length() - 1)]
    if len(halving) == 6:
        halving = [1, 2, 16, 4, 32, 8]
    order = halving[::-1]
    shifted = strip_count == 64
    position = jnp.asarray(gather_position(order, strip_count, shifted))
    early = tree_gather(packed, "strip", order[:2], shifted)

    padded_rows = jnp.pad(section_input, ((1, 1), (0, 0), (0, 0)))
    own_rows = lax.dynamic_slice_in_dim(padded_rows, chan_pos * row_part, row_part + 2, 0)
    extended = with_halo(own_rows, (("strip", 1),), 3)
    extended, early = lax.optimization_barrier((extended, early))
    early = tree_gather(early, "strip", order[2:4], shifted)
    hidden = swish(convolve(extended, conv_weight, row_part, col_local + 4) + conv_bias)
    pooled = pool_pairs(hidden)
    column = jnp.arange(half_cols + 2)
    outside = (column == 0) & (strip_pos == 0) | (column == half_cols + 1) & (
        strip_pos == strip_count - 1
    )
    pooled = jnp.where(outside[None, :, None], jnp.zeros_like(pooled), pooled)
    pooled, early = lax.optimization_barrier((pooled, early))
    every = tree_gather(early, "strip", order[4:], shifted).reshape(strip_count, owned + 8, lanes)
    every_grad = every[:, :owned].reshape(strip_count * owned, lanes)
    every_counts = every[:, owned, :list_len].reshape(-1)
    every_slots = jnp.round(every[:, owned, list_len : 2 * list_len]).astype(jnp.int32).reshape(-1)
    part_rows = pooled.shape[0]
    gathered = jnp.zeros((chan_count * part_rows,) + pooled.shape[1:], pooled.dtype)
    for shift in range(chan_count):
        block = pooled
        if shift:
            block = lax.ppermute(
                pooled, "chan", [(i, (i + shift) % chan_count) for i in range(chan_count)]
            )
        source = (chan_pos + chan_count - shift) % chan_count
        gathered = lax.dynamic_update_slice_in_dim(gathered, block, source * part_rows, 0)
    padded_deep = jnp.pad(gathered, ((1, 1), (0, 0), (0, 0)))
    half_rows = gathered.shape[0]
    deep_pre = convolve(padded_deep, deep_weight, half_rows, half_cols) + deep_bias
    features = swish(deep_pre).astype(jnp.bfloat16).reshape(-1, width_deep)
    part_sums = jnp.dot(member.astype(jnp.bfloat16), features, preferred_element_type=jnp.float32)

    same_slot = (slot_ids[:, None] == every_slots[None, :]).astype(jnp.float32)
    entry_counts = jnp.dot(same_slot, every_counts, precision=lax.Precision.HIGHEST)
    grad_row = position[slot_ids // owned] * owned + slot_ids % owned
    entry_grad = every_grad[grad_row] / jnp.maximum(entry_counts, 1.0)[:, None]
    pixel_grad = lax.dot_general(
        member.astype(jnp.float32),
        entry_grad,
        (((0,), (0,)), ((), ())),
        precision=lax.Precision.HIGHEST,
        preferred_element_type=jnp.float32,
    )
    deep_grad = (pixel_grad * swish_slope(deep_pre.reshape(-1, width_deep))).astype(jnp.bfloat16)
    pieces = []
    for shift_row in range(3):
        for shift_col in range(3):
            window = padded_deep[
                shift_row : shift_row + half_rows, shift_col : shift_col + half_cols
            ].reshape(-1, channels)
            pieces.append(
                lax.dot_general(
                    window, deep_grad, (((0,), (0,)), ((), ())), preferred_element_type=jnp.float32
                )
            )
    local_bias = jnp.sum(deep_grad.astype(jnp.float32), axis=0)
    bias_rows = jnp.zeros((strip_count * 8 - 9 * channels % (strip_count * 8), width_deep), jnp.float32)
    bias_rows = bias_rows.at[0].set(local_bias)
    local_grads = jnp.concatenate(pieces + [bias_rows], axis=0)

    total_grads, every_sums = tree_sum(local_grads, part_sums, "strip", halving, shifted)
    mine = strip_pos * owned + jnp.arange(owned, dtype=jnp.int32)
    pick = (mine[:, None] == every_slots[None, :]).astype(jnp.float32)
    slot_sums = jnp.dot(pick, every_sums, precision=lax.Precision.HIGHEST)
    slot_counts = jnp.dot(pick, every_counts, precision=lax.Precision.HIGHEST)
    embeddings = slot_sums / jnp.maximum(slot_counts, 1.0)[:, None]

    weight_grad = total_grads[: 9 * channels].reshape(3, 3, channels, width_deep)
    bias_grad = total_grads[9 * channels]
    return (embeddings, weight_grad, bias_grad)


def solution(mesh):
    placed = (
        P(None, "strip", None),
        P(),
        P(),
        P(None, None, None, "chan"),
        P("chan"),
        P(None, "strip"),
        P("strip"),
        P("strip", "chan"),
    )
    return jax.shard_map(
        body,
        mesh=mesh,
        in_specs=placed,
        out_specs=(P("strip", "chan"), P(None, None, None, "chan"), P("chan")),
        check_vma=False,
    )
```

```python
import functools

import jax
import numpy as np
import jax.numpy as jnp
from jax import lax
from jax.experimental import pallas as pl
from jax.experimental.pallas import tpu as pltpu
from jax.sharding import PartitionSpec as P


def with_halo(cells, sides, width):
    for axis, dim in sides:
        count = lax.axis_size(axis)
        ends = count - 1
        head = lax.slice_in_dim(cells, 0, width, axis=dim)
        tail = lax.slice_in_dim(cells, cells.shape[dim] - width, cells.shape[dim], axis=dim)
        cells = jnp.concatenate(
            [
                lax.ppermute(tail, axis, [(i, (i + 1) % count) for i in range(ends)]),
                cells,
                lax.ppermute(head, axis, [((i + 1) % count, i) for i in range(ends)]),
            ],
            axis=dim,
        )
    return cells


def chip_view(index, shifted):
    if not shifted:
        return index
    core = index % 2
    return ((index // 16 + core) % 4 * 8 + (index // 2 + core) % 8) * 2 + core


def chip_unview(index, shifted):
    if not shifted:
        return index
    core = index % 2
    return ((index // 16 + 4 - core) % 4 * 8 + (index // 2 + 8 - core) % 8) * 2 + core


def strip_partner(index, dist, shifted):
    if dist == 1:
        return index + 1 - 2 * (index % 2)
    view = chip_view(index, shifted)
    return chip_unview(view + dist - 2 * dist * ((view // dist) % 2), shifted)


def strip_bit(index, dist, shifted):
    if dist == 1:
        return index % 2
    return (chip_view(index, shifted) // dist) % 2


def tree_gather(block, axis, order, shifted):
    count = lax.axis_size(axis)
    me = lax.axis_index(axis)
    held = block
    for dist in order:
        pairs = [(i, strip_partner(i, dist, shifted)) for i in range(count)]
        other = lax.ppermute(held, axis, pairs)
        high = strip_bit(me, dist, shifted)
        size = held.shape[0]
        both = jnp.zeros((2 * size,) + held.shape[1:], held.dtype)
        both = lax.dynamic_update_slice_in_dim(both, held, high * size, 0)
        held = lax.dynamic_update_slice_in_dim(both, other, (1 - high) * size, 0)
    return held


def gather_position(order, count, shifted):
    return np.array(
        [sum(strip_bit(j, dist, shifted) << k for k, dist in enumerate(order)) for j in range(count)],
        np.int32,
    )


def tree_kernel(count, chunk, width, dists, shifted, grads_ref, sums_ref, out_ref, every_ref, landing, sems, free):
    me = lax.axis_index("strip")
    chan = lax.axis_index("chan")
    mesh_id = pl.DeviceIdType.MESH

    def partner(dist):
        return strip_partner(me, dist, shifted)

    barrier = pltpu.get_barrier_semaphore()
    for dist in dists:
        pl.semaphore_signal(barrier, inc=1, device_id=(partner(dist), chan), device_id_type=mesh_id)
    pl.semaphore_wait(barrier, len(dists))

    out_ref[...] = grads_ref[...]
    place = 0
    for k, dist in enumerate(dists):
        place = place + (strip_bit(me, dist, shifted)) * (count >> (k + 1))
    every_ref[pl.ds(pl.multiple_of(place * width, 8), width)] = sums_ref[...]

    low = 0
    size = count * chunk
    offset = 0
    for k, dist in enumerate(dists):
        half = size // 2
        high = strip_bit(me, dist, shifted)
        keep = low + high * half
        give = low + (1 - high) * half
        copy = pltpu.make_async_remote_copy(
            src_ref=out_ref.at[pl.ds(pl.multiple_of(give, 8), half)],
            dst_ref=landing.at[pl.ds(offset, half)],
            send_sem=sems.at[0, k],
            recv_sem=sems.at[1, k],
            device_id=(partner(dist), chan),
            device_id_type=mesh_id,
        )
        copy.start()
        copy.wait()
        pl.semaphore_signal(
            free.at[k], inc=1, device_id=(partner(dist), chan), device_id_type=mesh_id
        )

        def accumulate(step, carry, keep=keep, offset=offset):
            mine = pl.ds(pl.multiple_of(keep + step * chunk, 8), chunk)
            got = pl.ds(pl.multiple_of(offset + step * chunk, 8), chunk)
            out_ref[mine] = out_ref[mine] + landing[got]
            return carry

        lax.fori_loop(0, half // chunk, accumulate, 0)
        low = keep
        size = half
        offset += half

    blocks = 1
    for k in reversed(range(len(dists))):
        dist = dists[k]
        pl.semaphore_wait(free.at[k], 1)
        rows = pl.ds(pl.multiple_of(low, 8), size)
        spot = pl.ds(pl.multiple_of(place * width, 8), blocks * width)
        grads_copy = pltpu.make_async_remote_copy(
            src_ref=out_ref.at[rows],
            dst_ref=out_ref.at[rows],
            send_sem=sems.at[2, k],
            recv_sem=sems.at[3, k],
            device_id=(partner(dist), chan),
            device_id_type=mesh_id,
        )
        sums_copy = pltpu.make_async_remote_copy(
            src_ref=every_ref.at[spot],
            dst_ref=every_ref.at[spot],
            send_sem=sems.at[4, k],
            recv_sem=sems.at[5, k],
            device_id=(partner(dist), chan),
            device_id_type=mesh_id,
        )
        grads_copy.start()
        sums_copy.start()
        grads_copy.wait()
        sums_copy.wait()
        high = strip_bit(me, dist, shifted)
        low = low - high * size
        place = place - high * blocks
        size = size * 2
        blocks = blocks * 2


def tree_sum(grads, sums, axis, dists, shifted):
    count = lax.axis_size(axis)
    rows, lanes = grads.shape
    chunk = rows // count
    width = sums.shape[0]
    steps = count.bit_length() - 1
    return pl.pallas_call(
        functools.partial(tree_kernel, count, chunk, width, dists, shifted),
        out_shape=(
            jax.ShapeDtypeStruct((rows, lanes), jnp.float32),
            jax.ShapeDtypeStruct((count * width, lanes), jnp.float32),
        ),
        in_specs=[pl.BlockSpec(memory_space=pltpu.VMEM)] * 2,
        out_specs=(pl.BlockSpec(memory_space=pltpu.VMEM),) * 2,
        scratch_shapes=[
            pltpu.VMEM((rows, lanes), jnp.float32),
            pltpu.SemaphoreType.DMA((6, steps)),
            pltpu.SemaphoreType.REGULAR((steps,)),
        ],
        compiler_params=pltpu.CompilerParams(collective_id=0, has_side_effects=True),
    )(grads, sums)


def swish(value):
    return value * jax.nn.sigmoid(value)


def swish_slope(value):
    sigma = jax.nn.sigmoid(value)
    return sigma * (1.0 + value * (1.0 - sigma))


def convolve(padded, weight, row_count, col_count):
    channels = padded.shape[-1]
    width = -(-padded.shape[1] // 16) * 16
    padded = jnp.pad(padded, ((0, 0), (0, width - padded.shape[1]), (0, 0)))
    running = None
    for shift_col in range(3):
        column_sum = None
        for shift_row in range(3):
            band = padded[shift_row : shift_row + row_count].reshape(row_count * width, channels)
            partial_term = jnp.dot(
                band, weight[shift_row, shift_col], preferred_element_type=jnp.float32
            )
            column_sum = partial_term if column_sum is None else column_sum + partial_term
        column_sum = column_sum.reshape(row_count, width, weight.shape[-1])
        shifted = column_sum[:, shift_col : shift_col + col_count]
        running = shifted if running is None else running + shifted
    return running


def pool_pairs(hidden):
    row_count, col_count, channels = hidden.shape
    return (
        hidden.reshape(row_count // 2, 2, col_count // 2, 2, channels)
        .mean(axis=(1, 3))
        .astype(jnp.bfloat16)
    )


def body(
    section_input, conv_weight, conv_bias, deep_weight, deep_bias, labels, slot_ids, embed_grad
):
    chan_count = lax.axis_size("chan")
    chan_pos = lax.axis_index("chan")
    strip_count = lax.axis_size("strip")
    strip_pos = lax.axis_index("strip")
    row_total, col_local, channels = section_input.shape
    row_part = row_total // chan_count
    half_cols = col_local // 2
    list_len = slot_ids.shape[0]
    owned, width_deep = embed_grad.shape
    lanes = embed_grad.shape[1]

    flat_labels = labels.reshape(-1)
    member = flat_labels[None, :] == jnp.arange(list_len, dtype=jnp.int32)[:, None]
    part_counts = jnp.sum(member.astype(jnp.float32), axis=1)
    meta = jnp.zeros((8, lanes), jnp.float32)
    meta = meta.at[0, :list_len].set(part_counts)
    meta = meta.at[0, list_len : 2 * list_len].set(slot_ids.astype(jnp.float32))
    packed = jnp.concatenate([embed_grad, meta], axis=0)
    halving = [1 << k for k in range(strip_count.bit_length() - 1)]
    if len(halving) == 6:
        halving = [1, 2, 16, 4, 32, 8]
    order = halving[::-1]
    shifted = strip_count == 64
    position = jnp.asarray(gather_position(order, strip_count, shifted))
    early = tree_gather(packed, "strip", order[:2], shifted)

    padded_rows = jnp.pad(section_input, ((1, 1), (0, 0), (0, 0)))
    own_rows = lax.dynamic_slice_in_dim(padded_rows, chan_pos * row_part, row_part + 2, 0)
    extended = with_halo(own_rows, (("strip", 1),), 3)
    extended, early = lax.optimization_barrier((extended, early))
    early = tree_gather(early, "strip", order[2:4], shifted)
    hidden = swish(convolve(extended, conv_weight, row_part, col_local + 4) + conv_bias)
    pooled = pool_pairs(hidden)
    column = jnp.arange(half_cols + 2)
    outside = (column == 0) & (strip_pos == 0) | (column == half_cols + 1) & (
        strip_pos == strip_count - 1
    )
    pooled = jnp.where(outside[None, :, None], jnp.zeros_like(pooled), pooled)
    pooled, early = lax.optimization_barrier((pooled, early))
    every = tree_gather(early, "strip", order[4:], shifted).reshape(strip_count, owned + 8, lanes)
    every_grad = every[:, :owned].reshape(strip_count * owned, lanes)
    every_counts = every[:, owned, :list_len].reshape(-1)
    every_slots = jnp.round(every[:, owned, list_len : 2 * list_len]).astype(jnp.int32).reshape(-1)
    part_rows = pooled.shape[0]
    gathered = jnp.zeros((chan_count * part_rows,) + pooled.shape[1:], pooled.dtype)
    for shift in range(chan_count):
        block = pooled
        if shift:
            block = lax.ppermute(
                pooled, "chan", [(i, (i + shift) % chan_count) for i in range(chan_count)]
            )
        source = (chan_pos + chan_count - shift) % chan_count
        gathered = lax.dynamic_update_slice_in_dim(gathered, block, source * part_rows, 0)
    padded_deep = jnp.pad(gathered, ((1, 1), (0, 0), (0, 0)))
    half_rows = gathered.shape[0]
    deep_pre = convolve(padded_deep, deep_weight, half_rows, half_cols) + deep_bias
    features = swish(deep_pre).astype(jnp.bfloat16).reshape(-1, width_deep)
    part_sums = jnp.dot(member.astype(jnp.bfloat16), features, preferred_element_type=jnp.float32)

    same_slot = (slot_ids[:, None] == every_slots[None, :]).astype(jnp.float32)
    entry_counts = jnp.dot(same_slot, every_counts, precision=lax.Precision.HIGHEST)
    grad_row = position[slot_ids // owned] * owned + slot_ids % owned
    entry_grad = every_grad[grad_row] / jnp.maximum(entry_counts, 1.0)[:, None]
    pixel_grad = lax.dot_general(
        member.astype(jnp.float32),
        entry_grad,
        (((0,), (0,)), ((), ())),
        precision=lax.Precision.HIGHEST,
        preferred_element_type=jnp.float32,
    )
    deep_grad = (pixel_grad * swish_slope(deep_pre.reshape(-1, width_deep))).astype(jnp.bfloat16)
    deep_width = -(-padded_deep.shape[1] // 16) * 16
    wide_deep = jnp.pad(padded_deep, ((0, 0), (0, deep_width - padded_deep.shape[1]), (0, 0)))
    grid_grad = deep_grad.reshape(half_rows, half_cols, width_deep)
    placed_grads = [
        jnp.pad(
            grid_grad, ((0, 0), (shift_col, deep_width - half_cols - shift_col), (0, 0))
        ).reshape(-1, width_deep)
        for shift_col in range(3)
    ]
    pieces = []
    for shift_row in range(3):
        band = wide_deep[shift_row : shift_row + half_rows].reshape(-1, channels)
        for shift_col in range(3):
            pieces.append(
                lax.dot_general(
                    band,
                    placed_grads[shift_col],
                    (((0,), (0,)), ((), ())),
                    preferred_element_type=jnp.float32,
                )
            )
    local_bias = jnp.sum(deep_grad.astype(jnp.float32), axis=0)
    bias_rows = jnp.zeros((strip_count * 8 - 9 * channels % (strip_count * 8), width_deep), jnp.float32)
    bias_rows = bias_rows.at[0].set(local_bias)
    local_grads = jnp.concatenate(pieces + [bias_rows], axis=0)

    total_grads, every_sums = tree_sum(local_grads, part_sums, "strip", halving, shifted)
    mine = strip_pos * owned + jnp.arange(owned, dtype=jnp.int32)
    pick = (mine[:, None] == every_slots[None, :]).astype(jnp.float32)
    slot_sums = jnp.dot(pick, every_sums, precision=lax.Precision.HIGHEST)
    slot_counts = jnp.dot(pick, every_counts, precision=lax.Precision.HIGHEST)
    embeddings = slot_sums / jnp.maximum(slot_counts, 1.0)[:, None]

    weight_grad = total_grads[: 9 * channels].reshape(3, 3, channels, width_deep)
    bias_grad = total_grads[9 * channels]
    return (embeddings, weight_grad, bias_grad)


def solution(mesh):
    placed = (
        P(None, "strip", None),
        P(),
        P(),
        P(None, None, None, "chan"),
        P("chan"),
        P(None, "strip"),
        P("strip"),
        P("strip", "chan"),
    )
    return jax.shard_map(
        body,
        mesh=mesh,
        in_specs=placed,
        out_specs=(P("strip", "chan"), P(None, None, None, "chan"), P("chan")),
        check_vma=False,
    )
```

```python
import functools

import jax
import numpy as np
import jax.numpy as jnp
from jax import lax
from jax.experimental import pallas as pl
from jax.experimental.pallas import tpu as pltpu
from jax.sharding import PartitionSpec as P


def with_halo(cells, sides, width):
    for axis, dim in sides:
        count = lax.axis_size(axis)
        ends = count - 1
        head = lax.slice_in_dim(cells, 0, width, axis=dim)
        tail = lax.slice_in_dim(cells, cells.shape[dim] - width, cells.shape[dim], axis=dim)
        cells = jnp.concatenate(
            [
                lax.ppermute(tail, axis, [(i, (i + 1) % count) for i in range(ends)]),
                cells,
                lax.ppermute(head, axis, [((i + 1) % count, i) for i in range(ends)]),
            ],
            axis=dim,
        )
    return cells


def chip_view(index, shifted):
    if not shifted:
        return index
    core = index % 2
    return ((index // 16 + core) % 4 * 8 + (index // 2 + core) % 8) * 2 + core


def chip_unview(index, shifted):
    if not shifted:
        return index
    core = index % 2
    return ((index // 16 + 4 - core) % 4 * 8 + (index // 2 + 8 - core) % 8) * 2 + core


def strip_partner(index, dist, shifted):
    if dist == 1:
        return index + 1 - 2 * (index % 2)
    view = chip_view(index, shifted)
    return chip_unview(view + dist - 2 * dist * ((view // dist) % 2), shifted)


def strip_bit(index, dist, shifted):
    if dist == 1:
        return index % 2
    return (chip_view(index, shifted) // dist) % 2


def tree_gather(block, axis, order, shifted):
    count = lax.axis_size(axis)
    me = lax.axis_index(axis)
    held = block
    for dist in order:
        pairs = [(i, strip_partner(i, dist, shifted)) for i in range(count)]
        other = lax.ppermute(held, axis, pairs)
        high = strip_bit(me, dist, shifted)
        size = held.shape[0]
        both = jnp.zeros((2 * size,) + held.shape[1:], held.dtype)
        both = lax.dynamic_update_slice_in_dim(both, held, high * size, 0)
        held = lax.dynamic_update_slice_in_dim(both, other, (1 - high) * size, 0)
    return held


def gather_position(order, count, shifted):
    return np.array(
        [sum(strip_bit(j, dist, shifted) << k for k, dist in enumerate(order)) for j in range(count)],
        np.int32,
    )


def tree_kernel(count, chunk, width, dists, shifted, grads_ref, sums_ref, out_ref, every_ref, landing, sems, free):
    me = lax.axis_index("strip")
    chan = lax.axis_index("chan")
    mesh_id = pl.DeviceIdType.MESH

    def partner(dist):
        return strip_partner(me, dist, shifted)

    barrier = pltpu.get_barrier_semaphore()
    for dist in dists:
        pl.semaphore_signal(barrier, inc=1, device_id=(partner(dist), chan), device_id_type=mesh_id)
    pl.semaphore_wait(barrier, len(dists))

    out_ref[...] = grads_ref[...]
    place = 0
    for k, dist in enumerate(dists):
        place = place + (strip_bit(me, dist, shifted)) * (count >> (k + 1))
    every_ref[pl.ds(pl.multiple_of(place * width, 8), width)] = sums_ref[...]

    low = 0
    size = count * chunk
    offset = 0
    for k, dist in enumerate(dists):
        half = size // 2
        high = strip_bit(me, dist, shifted)
        keep = low + high * half
        give = low + (1 - high) * half
        copy = pltpu.make_async_remote_copy(
            src_ref=out_ref.at[pl.ds(pl.multiple_of(give, 8), half)],
            dst_ref=landing.at[pl.ds(offset, half)],
            send_sem=sems.at[0, k],
            recv_sem=sems.at[1, k],
            device_id=(partner(dist), chan),
            device_id_type=mesh_id,
        )
        copy.start()
        copy.wait()
        pl.semaphore_signal(
            free.at[k], inc=1, device_id=(partner(dist), chan), device_id_type=mesh_id
        )

        def accumulate(step, carry, keep=keep, offset=offset):
            mine = pl.ds(pl.multiple_of(keep + step * chunk, 8), chunk)
            got = pl.ds(pl.multiple_of(offset + step * chunk, 8), chunk)
            out_ref[mine] = out_ref[mine] + landing[got]
            return carry

        lax.fori_loop(0, half // chunk, accumulate, 0)
        low = keep
        size = half
        offset += half

    blocks = 1
    for k in reversed(range(len(dists))):
        dist = dists[k]
        pl.semaphore_wait(free.at[k], 1)
        rows = pl.ds(pl.multiple_of(low, 8), size)
        spot = pl.ds(pl.multiple_of(place * width, 8), blocks * width)
        grads_copy = pltpu.make_async_remote_copy(
            src_ref=out_ref.at[rows],
            dst_ref=out_ref.at[rows],
            send_sem=sems.at[2, k],
            recv_sem=sems.at[3, k],
            device_id=(partner(dist), chan),
            device_id_type=mesh_id,
        )
        sums_copy = pltpu.make_async_remote_copy(
            src_ref=every_ref.at[spot],
            dst_ref=every_ref.at[spot],
            send_sem=sems.at[4, k],
            recv_sem=sems.at[5, k],
            device_id=(partner(dist), chan),
            device_id_type=mesh_id,
        )
        grads_copy.start()
        sums_copy.start()
        grads_copy.wait()
        sums_copy.wait()
        high = strip_bit(me, dist, shifted)
        low = low - high * size
        place = place - high * blocks
        size = size * 2
        blocks = blocks * 2


def tree_sum(grads, sums, axis, dists, shifted):
    count = lax.axis_size(axis)
    rows, lanes = grads.shape
    chunk = rows // count
    width = sums.shape[0]
    steps = count.bit_length() - 1
    return pl.pallas_call(
        functools.partial(tree_kernel, count, chunk, width, dists, shifted),
        out_shape=(
            jax.ShapeDtypeStruct((rows, lanes), jnp.float32),
            jax.ShapeDtypeStruct((count * width, lanes), jnp.float32),
        ),
        in_specs=[pl.BlockSpec(memory_space=pltpu.VMEM)] * 2,
        out_specs=(pl.BlockSpec(memory_space=pltpu.VMEM),) * 2,
        scratch_shapes=[
            pltpu.VMEM((rows, lanes), jnp.float32),
            pltpu.SemaphoreType.DMA((6, steps)),
            pltpu.SemaphoreType.REGULAR((steps,)),
        ],
        compiler_params=pltpu.CompilerParams(collective_id=0, has_side_effects=True),
    )(grads, sums)


def swish(value):
    return value * jax.nn.sigmoid(value)


def swish_slope(value):
    sigma = jax.nn.sigmoid(value)
    return sigma * (1.0 + value * (1.0 - sigma))


def convolve(padded, weight, row_count, col_count):
    channels = padded.shape[-1]
    width = -(-padded.shape[1] // 16) * 16
    padded = jnp.pad(padded, ((0, 0), (0, width - padded.shape[1]), (0, 0)))
    running = None
    for shift_col in range(3):
        column_sum = None
        for shift_row in range(3):
            band = padded[shift_row : shift_row + row_count].reshape(row_count * width, channels)
            partial_term = jnp.dot(
                band, weight[shift_row, shift_col], preferred_element_type=jnp.float32
            )
            column_sum = partial_term if column_sum is None else column_sum + partial_term
        column_sum = column_sum.reshape(row_count, width, weight.shape[-1])
        shifted = column_sum[:, shift_col : shift_col + col_count]
        running = shifted if running is None else running + shifted
    return running


def pool_pairs(hidden):
    row_count, col_count, channels = hidden.shape
    return (
        hidden.reshape(row_count // 2, 2, col_count // 2, 2, channels)
        .mean(axis=(1, 3))
        .astype(jnp.bfloat16)
    )


def body(
    section_input, conv_weight, conv_bias, deep_weight, deep_bias, labels, slot_ids, embed_grad
):
    chan_count = lax.axis_size("chan")
    chan_pos = lax.axis_index("chan")
    strip_count = lax.axis_size("strip")
    strip_pos = lax.axis_index("strip")
    row_total, col_local, channels = section_input.shape
    row_part = row_total // chan_count
    half_cols = col_local // 2
    list_len = slot_ids.shape[0]
    owned, width_deep = embed_grad.shape
    lanes = embed_grad.shape[1]

    flat_labels = labels.reshape(-1)
    member = flat_labels[None, :] == jnp.arange(list_len, dtype=jnp.int32)[:, None]
    part_counts = jnp.sum(member.astype(jnp.float32), axis=1)
    meta = jnp.concatenate(
        [part_counts, slot_ids.astype(jnp.float32), jnp.zeros((8 * lanes - 2 * list_len,), jnp.float32)]
    ).reshape(8, lanes)
    packed = jnp.concatenate([embed_grad, meta], axis=0)
    halving = [1 << k for k in range(strip_count.bit_length() - 1)]
    if len(halving) == 6:
        halving = [1, 2, 16, 4, 32, 8]
    order = halving[::-1]
    shifted = strip_count == 64
    position = jnp.asarray(gather_position(order, strip_count, shifted))
    early = tree_gather(packed, "strip", order[:2], shifted)

    padded_rows = jnp.pad(section_input, ((1, 1), (0, 0), (0, 0)))
    own_rows = lax.dynamic_slice_in_dim(padded_rows, chan_pos * row_part, row_part + 2, 0)
    extended = with_halo(own_rows, (("strip", 1),), 3)
    hidden = swish(convolve(extended, conv_weight, row_part, col_local + 4) + conv_bias)
    pooled = pool_pairs(hidden)
    column = jnp.arange(half_cols + 2)
    outside = (column == 0) & (strip_pos == 0) | (column == half_cols + 1) & (
        strip_pos == strip_count - 1
    )
    pooled = jnp.where(outside[None, :, None], jnp.zeros_like(pooled), pooled)
    pooled, early = lax.optimization_barrier((pooled, early))
    early = tree_gather(early, "strip", order[2:4], shifted)
    part_rows = pooled.shape[0]
    gathered = jnp.zeros((chan_count * part_rows,) + pooled.shape[1:], pooled.dtype)
    for shift in range(chan_count):
        block = pooled
        if shift:
            block = lax.ppermute(
                pooled, "chan", [(i, (i + shift) % chan_count) for i in range(chan_count)]
            )
        source = (chan_pos + chan_count - shift) % chan_count
        gathered = lax.dynamic_update_slice_in_dim(gathered, block, source * part_rows, 0)
    gathered, early = lax.optimization_barrier((gathered, early))
    every = tree_gather(early, "strip", order[4:], shifted).reshape(strip_count, owned + 8, lanes)
    every_grad = every[:, :owned].reshape(strip_count * owned, lanes)
    every_counts = every[:, owned, :list_len].reshape(-1)
    every_slots = jnp.round(every[:, owned, list_len : 2 * list_len]).astype(jnp.int32).reshape(-1)
    padded_deep = jnp.pad(gathered, ((1, 1), (0, 0), (0, 0)))
    half_rows = gathered.shape[0]
    deep_pre = convolve(padded_deep, deep_weight, half_rows, half_cols) + deep_bias
    features = swish(deep_pre).astype(jnp.bfloat16).reshape(-1, width_deep)
    part_sums = jnp.dot(member.astype(jnp.bfloat16), features, preferred_element_type=jnp.float32)

    same_slot = (slot_ids[:, None] == every_slots[None, :]).astype(jnp.float32)
    entry_counts = jnp.dot(same_slot, every_counts, precision=lax.Precision.HIGHEST)
    grad_row = position[slot_ids // owned] * owned + slot_ids % owned
    entry_grad = every_grad[grad_row] / jnp.maximum(entry_counts, 1.0)[:, None]
    pixel_grad = lax.dot_general(
        member.astype(jnp.float32),
        entry_grad,
        (((0,), (0,)), ((), ())),
        precision=lax.Precision.HIGHEST,
        preferred_element_type=jnp.float32,
    )
    deep_grad = (pixel_grad * swish_slope(deep_pre.reshape(-1, width_deep))).astype(jnp.bfloat16)
    deep_width = -(-padded_deep.shape[1] // 16) * 16
    wide_deep = jnp.pad(padded_deep, ((0, 0), (0, deep_width - padded_deep.shape[1]), (0, 0)))
    grid_grad = deep_grad.reshape(half_rows, half_cols, width_deep)
    placed_grads = [
        jnp.pad(
            grid_grad, ((0, 0), (shift_col, deep_width - half_cols - shift_col), (0, 0))
        ).reshape(-1, width_deep)
        for shift_col in range(3)
    ]
    pieces = []
    for shift_row in range(3):
        band = wide_deep[shift_row : shift_row + half_rows].reshape(-1, channels)
        for shift_col in range(3):
            pieces.append(
                lax.dot_general(
                    band,
                    placed_grads[shift_col],
                    (((0,), (0,)), ((), ())),
                    preferred_element_type=jnp.float32,
                )
            )
    local_bias = jnp.sum(deep_grad.astype(jnp.float32), axis=0)
    bias_rows = jnp.zeros((strip_count * 8 - 9 * channels % (strip_count * 8), width_deep), jnp.float32)
    bias_rows = bias_rows.at[0].set(local_bias)
    local_grads = jnp.concatenate(pieces + [bias_rows], axis=0)

    total_grads, every_sums = tree_sum(local_grads, part_sums, "strip", halving, shifted)
    mine = strip_pos * owned + jnp.arange(owned, dtype=jnp.int32)
    pick = (mine[:, None] == every_slots[None, :]).astype(jnp.float32)
    slot_sums = jnp.dot(pick, every_sums, precision=lax.Precision.HIGHEST)
    slot_counts = jnp.dot(pick, every_counts, precision=lax.Precision.HIGHEST)
    embeddings = slot_sums / jnp.maximum(slot_counts, 1.0)[:, None]

    weight_grad = total_grads[: 9 * channels].reshape(3, 3, channels, width_deep)
    bias_grad = total_grads[9 * channels]
    return (embeddings, weight_grad, bias_grad)


def solution(mesh):
    placed = (
        P(None, "strip", None),
        P(),
        P(),
        P(None, None, None, "chan"),
        P("chan"),
        P(None, "strip"),
        P("strip"),
        P("strip", "chan"),
    )
    return jax.shard_map(
        body,
        mesh=mesh,
        in_specs=placed,
        out_specs=(P("strip", "chan"), P(None, None, None, "chan"), P("chan")),
        check_vma=False,
    )
```

```python
import functools

import jax
import numpy as np
import jax.numpy as jnp
from jax import lax
from jax.experimental import pallas as pl
from jax.experimental.pallas import tpu as pltpu
from jax.sharding import PartitionSpec as P


def with_halo(cells, sides, width):
    for axis, dim in sides:
        count = lax.axis_size(axis)
        ends = count - 1
        head = lax.slice_in_dim(cells, 0, width, axis=dim)
        tail = lax.slice_in_dim(cells, cells.shape[dim] - width, cells.shape[dim], axis=dim)
        cells = jnp.concatenate(
            [
                lax.ppermute(tail, axis, [(i, (i + 1) % count) for i in range(ends)]),
                cells,
                lax.ppermute(head, axis, [((i + 1) % count, i) for i in range(ends)]),
            ],
            axis=dim,
        )
    return cells


def chip_view(index, shifted):
    if not shifted:
        return index
    core = index % 2
    return ((index // 16 + core) % 4 * 8 + (index // 2 + core) % 8) * 2 + core


def chip_unview(index, shifted):
    if not shifted:
        return index
    core = index % 2
    return ((index // 16 + 4 - core) % 4 * 8 + (index // 2 + 8 - core) % 8) * 2 + core


def strip_partner(index, dist, shifted):
    if dist == 1:
        return index + 1 - 2 * (index % 2)
    view = chip_view(index, shifted)
    return chip_unview(view + dist - 2 * dist * ((view // dist) % 2), shifted)


def strip_bit(index, dist, shifted):
    if dist == 1:
        return index % 2
    return (chip_view(index, shifted) // dist) % 2


def tree_gather(block, axis, order, shifted):
    count = lax.axis_size(axis)
    me = lax.axis_index(axis)
    held = block
    for dist in order:
        pairs = [(i, strip_partner(i, dist, shifted)) for i in range(count)]
        other = lax.ppermute(held, axis, pairs)
        high = strip_bit(me, dist, shifted)
        size = held.shape[0]
        both = jnp.zeros((2 * size,) + held.shape[1:], held.dtype)
        both = lax.dynamic_update_slice_in_dim(both, held, high * size, 0)
        held = lax.dynamic_update_slice_in_dim(both, other, (1 - high) * size, 0)
    return held


def gather_position(order, count, shifted):
    return np.array(
        [sum(strip_bit(j, dist, shifted) << k for k, dist in enumerate(order)) for j in range(count)],
        np.int32,
    )


def tree_kernel(count, chunk, width, dists, shifted, grads_ref, sums_ref, out_ref, every_ref, landing, sems, free):
    me = lax.axis_index("strip")
    chan = lax.axis_index("chan")
    mesh_id = pl.DeviceIdType.MESH

    def partner(dist):
        return strip_partner(me, dist, shifted)

    barrier = pltpu.get_barrier_semaphore()
    for dist in dists:
        pl.semaphore_signal(barrier, inc=1, device_id=(partner(dist), chan), device_id_type=mesh_id)
    pl.semaphore_wait(barrier, len(dists))

    out_ref[...] = grads_ref[...]
    place = 0
    for k, dist in enumerate(dists):
        place = place + (strip_bit(me, dist, shifted)) * (count >> (k + 1))
    every_ref[pl.ds(pl.multiple_of(place * width, 8), width)] = sums_ref[...]

    low = 0
    size = count * chunk
    offset = 0
    for k, dist in enumerate(dists):
        half = size // 2
        high = strip_bit(me, dist, shifted)
        keep = low + high * half
        give = low + (1 - high) * half
        copy = pltpu.make_async_remote_copy(
            src_ref=out_ref.at[pl.ds(pl.multiple_of(give, 8), half)],
            dst_ref=landing.at[pl.ds(offset, half)],
            send_sem=sems.at[0, k],
            recv_sem=sems.at[1, k],
            device_id=(partner(dist), chan),
            device_id_type=mesh_id,
        )
        copy.start()
        copy.wait()
        pl.semaphore_signal(
            free.at[k], inc=1, device_id=(partner(dist), chan), device_id_type=mesh_id
        )

        def accumulate(step, carry, keep=keep, offset=offset):
            mine = pl.ds(pl.multiple_of(keep + step * chunk, 8), chunk)
            got = pl.ds(pl.multiple_of(offset + step * chunk, 8), chunk)
            out_ref[mine] = out_ref[mine] + landing[got]
            return carry

        lax.fori_loop(0, half // chunk, accumulate, 0)
        low = keep
        size = half
        offset += half

    blocks = 1
    for k in reversed(range(len(dists))):
        dist = dists[k]
        pl.semaphore_wait(free.at[k], 1)
        rows = pl.ds(pl.multiple_of(low, 8), size)
        spot = pl.ds(pl.multiple_of(place * width, 8), blocks * width)
        grads_copy = pltpu.make_async_remote_copy(
            src_ref=out_ref.at[rows],
            dst_ref=out_ref.at[rows],
            send_sem=sems.at[2, k],
            recv_sem=sems.at[3, k],
            device_id=(partner(dist), chan),
            device_id_type=mesh_id,
        )
        sums_copy = pltpu.make_async_remote_copy(
            src_ref=every_ref.at[spot],
            dst_ref=every_ref.at[spot],
            send_sem=sems.at[4, k],
            recv_sem=sems.at[5, k],
            device_id=(partner(dist), chan),
            device_id_type=mesh_id,
        )
        grads_copy.start()
        sums_copy.start()
        grads_copy.wait()
        sums_copy.wait()
        high = strip_bit(me, dist, shifted)
        low = low - high * size
        place = place - high * blocks
        size = size * 2
        blocks = blocks * 2


def tree_sum(grads, sums, axis, dists, shifted):
    count = lax.axis_size(axis)
    rows, lanes = grads.shape
    chunk = rows // count
    width = sums.shape[0]
    steps = count.bit_length() - 1
    return pl.pallas_call(
        functools.partial(tree_kernel, count, chunk, width, dists, shifted),
        out_shape=(
            jax.ShapeDtypeStruct((rows, lanes), jnp.float32),
            jax.ShapeDtypeStruct((count * width, lanes), jnp.float32),
        ),
        in_specs=[pl.BlockSpec(memory_space=pltpu.VMEM)] * 2,
        out_specs=(pl.BlockSpec(memory_space=pltpu.VMEM),) * 2,
        scratch_shapes=[
            pltpu.VMEM((rows, lanes), jnp.float32),
            pltpu.SemaphoreType.DMA((6, steps)),
            pltpu.SemaphoreType.REGULAR((steps,)),
        ],
        compiler_params=pltpu.CompilerParams(collective_id=0, has_side_effects=True),
    )(grads, sums)


def swish(value):
    return value * jax.nn.sigmoid(value)


def swish_slope(value):
    sigma = jax.nn.sigmoid(value)
    return sigma * (1.0 + value * (1.0 - sigma))


def convolve(padded, weight, row_count, col_count):
    channels = padded.shape[-1]
    width = -(-padded.shape[1] // 16) * 16
    padded = jnp.pad(padded, ((0, 0), (0, width - padded.shape[1]), (0, 0)))
    running = None
    for shift_col in range(3):
        column_sum = None
        for shift_row in range(3):
            band = padded[shift_row : shift_row + row_count].reshape(row_count * width, channels)
            partial_term = jnp.dot(
                band, weight[shift_row, shift_col], preferred_element_type=jnp.float32
            )
            column_sum = partial_term if column_sum is None else column_sum + partial_term
        column_sum = column_sum.reshape(row_count, width, weight.shape[-1])
        shifted = column_sum[:, shift_col : shift_col + col_count]
        running = shifted if running is None else running + shifted
    return running


def pool_pairs(hidden):
    row_count, col_count, channels = hidden.shape
    return (
        hidden.reshape(row_count // 2, 2, col_count // 2, 2, channels)
        .mean(axis=(1, 3))
        .astype(jnp.bfloat16)
    )


def body(
    section_input, conv_weight, conv_bias, deep_weight, deep_bias, labels, slot_ids, embed_grad
):
    chan_count = lax.axis_size("chan")
    chan_pos = lax.axis_index("chan")
    strip_count = lax.axis_size("strip")
    strip_pos = lax.axis_index("strip")
    row_total, col_local, channels = section_input.shape
    row_part = row_total // chan_count
    half_cols = col_local // 2
    list_len = slot_ids.shape[0]
    owned, width_deep = embed_grad.shape
    lanes = embed_grad.shape[1]

    flat_labels = labels.reshape(-1)
    member = flat_labels[None, :] == jnp.arange(list_len, dtype=jnp.int32)[:, None]
    part_counts = jnp.sum(member.astype(jnp.float32), axis=1)
    meta = jnp.concatenate(
        [part_counts, slot_ids.astype(jnp.float32), jnp.zeros((8 * lanes - 2 * list_len,), jnp.float32)]
    ).reshape(8, lanes)
    packed = jnp.concatenate([embed_grad, meta], axis=0)
    halving = [1 << k for k in range(strip_count.bit_length() - 1)]
    if len(halving) == 6:
        halving = [1, 2, 16, 4, 32, 8]
    order = halving[::-1]
    shifted = strip_count == 64
    position = jnp.asarray(gather_position(order, strip_count, shifted))
    early = tree_gather(packed, "strip", order[:2], shifted)

    padded_rows = jnp.pad(section_input, ((1, 1), (0, 0), (0, 0)))
    own_rows = lax.dynamic_slice_in_dim(padded_rows, chan_pos * row_part, row_part + 2, 0)
    extended = with_halo(own_rows, (("strip", 1),), 3)
    extended, early = lax.optimization_barrier((extended, early))
    early = tree_gather(early, "strip", order[2:4], shifted)
    hidden = swish(convolve(extended, conv_weight, row_part, col_local + 4) + conv_bias)
    pooled = pool_pairs(hidden)
    column = jnp.arange(half_cols + 2)
    outside = (column == 0) & (strip_pos == 0) | (column == half_cols + 1) & (
        strip_pos == strip_count - 1
    )
    pooled = jnp.where(outside[None, :, None], jnp.zeros_like(pooled), pooled)
    pooled, early = lax.optimization_barrier((pooled, early))
    every = tree_gather(early, "strip", order[4:], shifted).reshape(strip_count, owned + 8, lanes)
    every_grad = every[:, :owned].reshape(strip_count * owned, lanes)
    every_counts = every[:, owned, :list_len].reshape(-1)
    every_slots = jnp.round(every[:, owned, list_len : 2 * list_len]).astype(jnp.int32).reshape(-1)
    part_rows = pooled.shape[0]
    gathered = jnp.zeros((chan_count * part_rows,) + pooled.shape[1:], pooled.dtype)
    for shift in range(chan_count):
        block = pooled
        if shift:
            block = lax.ppermute(
                pooled, "chan", [(i, (i + shift) % chan_count) for i in range(chan_count)]
            )
        source = (chan_pos + chan_count - shift) % chan_count
        gathered = lax.dynamic_update_slice_in_dim(gathered, block, source * part_rows, 0)
    padded_deep = jnp.pad(gathered, ((1, 1), (0, 0), (0, 0)))
    half_rows = gathered.shape[0]
    deep_pre = convolve(padded_deep, deep_weight, half_rows, half_cols) + deep_bias
    features = swish(deep_pre).astype(jnp.bfloat16).reshape(-1, width_deep)
    part_sums = jnp.dot(member.astype(jnp.bfloat16), features, preferred_element_type=jnp.float32)

    same_slot = (slot_ids[:, None] == every_slots[None, :]).astype(jnp.float32)
    entry_counts = jnp.dot(same_slot, every_counts, precision=lax.Precision.HIGHEST)
    grad_row = position[slot_ids // owned] * owned + slot_ids % owned
    entry_grad = every_grad[grad_row] / jnp.maximum(entry_counts, 1.0)[:, None]
    pixel_grad = lax.dot_general(
        member.astype(jnp.float32),
        entry_grad,
        (((0,), (0,)), ((), ())),
        precision=lax.Precision.HIGHEST,
        preferred_element_type=jnp.float32,
    )
    deep_grad = (pixel_grad * swish_slope(deep_pre.reshape(-1, width_deep))).astype(jnp.bfloat16)
    deep_width = -(-padded_deep.shape[1] // 16) * 16
    wide_deep = jnp.pad(padded_deep, ((0, 0), (0, deep_width - padded_deep.shape[1]), (0, 0)))
    grid_grad = deep_grad.reshape(half_rows, half_cols, width_deep)
    placed_grads = [
        jnp.pad(
            grid_grad, ((0, 0), (shift_col, deep_width - half_cols - shift_col), (0, 0))
        ).reshape(-1, width_deep)
        for shift_col in range(3)
    ]
    pieces = []
    for shift_row in range(3):
        band = wide_deep[shift_row : shift_row + half_rows].reshape(-1, channels)
        for shift_col in range(3):
            pieces.append(
                lax.dot_general(
                    band,
                    placed_grads[shift_col],
                    (((0,), (0,)), ((), ())),
                    preferred_element_type=jnp.float32,
                )
            )
    local_bias = jnp.sum(deep_grad.astype(jnp.float32), axis=0)
    bias_rows = jnp.zeros((strip_count * 8 - 9 * channels % (strip_count * 8), width_deep), jnp.float32)
    bias_rows = bias_rows.at[0].set(local_bias)
    local_grads = jnp.concatenate(pieces + [bias_rows], axis=0)

    total_grads, every_sums = tree_sum(local_grads, part_sums, "strip", halving, shifted)
    mine = strip_pos * owned + jnp.arange(owned, dtype=jnp.int32)
    pick = (mine[:, None] == every_slots[None, :]).astype(jnp.float32)
    slot_sums = jnp.dot(pick, every_sums, precision=lax.Precision.HIGHEST)
    slot_counts = jnp.dot(pick, every_counts, precision=lax.Precision.HIGHEST)
    embeddings = slot_sums / jnp.maximum(slot_counts, 1.0)[:, None]

    weight_grad = total_grads[: 9 * channels].reshape(3, 3, channels, width_deep)
    bias_grad = total_grads[9 * channels]
    return (embeddings, weight_grad, bias_grad)


def solution(mesh):
    placed = (
        P(None, "strip", None),
        P(),
        P(),
        P(None, None, None, "chan"),
        P("chan"),
        P(None, "strip"),
        P("strip"),
        P("strip", "chan"),
    )
    return jax.shard_map(
        body,
        mesh=mesh,
        in_specs=placed,
        out_specs=(P("strip", "chan"), P(None, None, None, "chan"), P("chan")),
        check_vma=False,
    )
```

```python
import functools

import jax
import numpy as np
import jax.numpy as jnp
from jax import lax
from jax.experimental import pallas as pl
from jax.experimental.pallas import tpu as pltpu
from jax.sharding import PartitionSpec as P


def with_halo(cells, sides, width):
    for axis, dim in sides:
        count = lax.axis_size(axis)
        ends = count - 1
        head = lax.slice_in_dim(cells, 0, width, axis=dim)
        tail = lax.slice_in_dim(cells, cells.shape[dim] - width, cells.shape[dim], axis=dim)
        cells = jnp.concatenate(
            [
                lax.ppermute(tail, axis, [(i, (i + 1) % count) for i in range(ends)]),
                cells,
                lax.ppermute(head, axis, [((i + 1) % count, i) for i in range(ends)]),
            ],
            axis=dim,
        )
    return cells


def chip_view(index, shifted):
    if not shifted:
        return index
    core = index % 2
    return ((index // 16 + core) % 4 * 8 + (index // 2 + core) % 8) * 2 + core


def chip_unview(index, shifted):
    if not shifted:
        return index
    core = index % 2
    return ((index // 16 + 4 - core) % 4 * 8 + (index // 2 + 8 - core) % 8) * 2 + core


def strip_partner(index, dist, shifted):
    if dist == 1:
        return index + 1 - 2 * (index % 2)
    view = chip_view(index, shifted)
    return chip_unview(view + dist - 2 * dist * ((view // dist) % 2), shifted)


def strip_bit(index, dist, shifted):
    if dist == 1:
        return index % 2
    return (chip_view(index, shifted) // dist) % 2


def tree_gather(block, axis, order, shifted):
    count = lax.axis_size(axis)
    me = lax.axis_index(axis)
    held = block
    for dist in order:
        pairs = [(i, strip_partner(i, dist, shifted)) for i in range(count)]
        other = lax.ppermute(held, axis, pairs)
        high = strip_bit(me, dist, shifted)
        size = held.shape[0]
        both = jnp.zeros((2 * size,) + held.shape[1:], held.dtype)
        both = lax.dynamic_update_slice_in_dim(both, held, high * size, 0)
        held = lax.dynamic_update_slice_in_dim(both, other, (1 - high) * size, 0)
    return held


def gather_position(order, count, shifted):
    return np.array(
        [sum(strip_bit(j, dist, shifted) << k for k, dist in enumerate(order)) for j in range(count)],
        np.int32,
    )


def tree_kernel(count, chunk, width, dists, shifted, grads_ref, sums_ref, out_ref, every_ref, landing, sems, free):
    me = lax.axis_index("strip")
    chan = lax.axis_index("chan")
    mesh_id = pl.DeviceIdType.MESH

    def partner(dist):
        return strip_partner(me, dist, shifted)

    barrier = pltpu.get_barrier_semaphore()
    for dist in dists:
        pl.semaphore_signal(barrier, inc=1, device_id=(partner(dist), chan), device_id_type=mesh_id)
    pl.semaphore_wait(barrier, len(dists))

    out_ref[...] = grads_ref[...]
    place = 0
    for k, dist in enumerate(dists):
        place = place + (strip_bit(me, dist, shifted)) * (count >> (k + 1))
    every_ref[pl.ds(pl.multiple_of(place * width, 8), width)] = sums_ref[...]

    low = 0
    size = count * chunk
    offset = 0
    for k, dist in enumerate(dists):
        half = size // 2
        high = strip_bit(me, dist, shifted)
        keep = low + high * half
        give = low + (1 - high) * half
        copy = pltpu.make_async_remote_copy(
            src_ref=out_ref.at[pl.ds(pl.multiple_of(give, 8), half)],
            dst_ref=landing.at[pl.ds(offset, half)],
            send_sem=sems.at[0, k],
            recv_sem=sems.at[1, k],
            device_id=(partner(dist), chan),
            device_id_type=mesh_id,
        )
        copy.start()
        copy.wait()
        pl.semaphore_signal(
            free.at[k], inc=1, device_id=(partner(dist), chan), device_id_type=mesh_id
        )

        def accumulate(step, carry, keep=keep, offset=offset):
            mine = pl.ds(pl.multiple_of(keep + step * chunk, 8), chunk)
            got = pl.ds(pl.multiple_of(offset + step * chunk, 8), chunk)
            out_ref[mine] = out_ref[mine] + landing[got]
            return carry

        lax.fori_loop(0, half // chunk, accumulate, 0)
        low = keep
        size = half
        offset += half

    blocks = 1
    for k in reversed(range(len(dists))):
        dist = dists[k]
        pl.semaphore_wait(free.at[k], 1)
        rows = pl.ds(pl.multiple_of(low, 8), size)
        spot = pl.ds(pl.multiple_of(place * width, 8), blocks * width)
        grads_copy = pltpu.make_async_remote_copy(
            src_ref=out_ref.at[rows],
            dst_ref=out_ref.at[rows],
            send_sem=sems.at[2, k],
            recv_sem=sems.at[3, k],
            device_id=(partner(dist), chan),
            device_id_type=mesh_id,
        )
        sums_copy = pltpu.make_async_remote_copy(
            src_ref=every_ref.at[spot],
            dst_ref=every_ref.at[spot],
            send_sem=sems.at[4, k],
            recv_sem=sems.at[5, k],
            device_id=(partner(dist), chan),
            device_id_type=mesh_id,
        )
        grads_copy.start()
        sums_copy.start()
        grads_copy.wait()
        sums_copy.wait()
        high = strip_bit(me, dist, shifted)
        low = low - high * size
        place = place - high * blocks
        size = size * 2
        blocks = blocks * 2


def tree_sum(grads, sums, axis, dists, shifted):
    count = lax.axis_size(axis)
    rows, lanes = grads.shape
    chunk = rows // count
    width = sums.shape[0]
    steps = count.bit_length() - 1
    return pl.pallas_call(
        functools.partial(tree_kernel, count, chunk, width, dists, shifted),
        out_shape=(
            jax.ShapeDtypeStruct((rows, lanes), jnp.float32),
            jax.ShapeDtypeStruct((count * width, lanes), jnp.float32),
        ),
        in_specs=[pl.BlockSpec(memory_space=pltpu.VMEM)] * 2,
        out_specs=(pl.BlockSpec(memory_space=pltpu.VMEM),) * 2,
        scratch_shapes=[
            pltpu.VMEM((rows, lanes), jnp.float32),
            pltpu.SemaphoreType.DMA((6, steps)),
            pltpu.SemaphoreType.REGULAR((steps,)),
        ],
        compiler_params=pltpu.CompilerParams(collective_id=0, has_side_effects=True),
    )(grads, sums)


def swish(value):
    return value * jax.nn.sigmoid(value)


def swish_slope(value):
    sigma = jax.nn.sigmoid(value)
    return sigma * (1.0 + value * (1.0 - sigma))


def convolve(padded, weight, row_count, col_count):
    channels = padded.shape[-1]
    width = -(-padded.shape[1] // 16) * 16
    padded = jnp.pad(padded, ((0, 0), (0, width - padded.shape[1]), (0, 0)))
    running = None
    for shift_col in range(3):
        column_sum = None
        for shift_row in range(3):
            band = padded[shift_row : shift_row + row_count].reshape(row_count * width, channels)
            partial_term = jnp.dot(
                band, weight[shift_row, shift_col], preferred_element_type=jnp.float32
            )
            column_sum = partial_term if column_sum is None else column_sum + partial_term
        column_sum = column_sum.reshape(row_count, width, weight.shape[-1])
        shifted = column_sum[:, shift_col : shift_col + col_count]
        running = shifted if running is None else running + shifted
    return running


def pool_pairs(hidden):
    row_count, col_count, channels = hidden.shape
    return (
        hidden.reshape(row_count // 2, 2, col_count // 2, 2, channels)
        .mean(axis=(1, 3))
        .astype(jnp.bfloat16)
    )


def body(
    section_input, conv_weight, conv_bias, deep_weight, deep_bias, labels, slot_ids, embed_grad
):
    chan_count = lax.axis_size("chan")
    chan_pos = lax.axis_index("chan")
    strip_count = lax.axis_size("strip")
    strip_pos = lax.axis_index("strip")
    row_total, col_local, channels = section_input.shape
    row_part = row_total // chan_count
    half_cols = col_local // 2
    list_len = slot_ids.shape[0]
    owned, width_deep = embed_grad.shape
    lanes = embed_grad.shape[1]

    flat_labels = labels.reshape(-1)
    member = flat_labels[None, :] == jnp.arange(list_len, dtype=jnp.int32)[:, None]
    part_counts = jnp.sum(member.astype(jnp.float32), axis=1)
    meta = jnp.concatenate(
        [part_counts, slot_ids.astype(jnp.float32), jnp.zeros((8 * lanes - 2 * list_len,), jnp.float32)]
    ).reshape(8, lanes)
    packed = jnp.concatenate([embed_grad, meta], axis=0)
    halving = [1 << k for k in range(strip_count.bit_length() - 1)]
    if len(halving) == 6:
        halving = [1, 2, 16, 4, 32, 8]
    order = halving[::-1]
    shifted = strip_count == 64
    position = jnp.asarray(gather_position(order, strip_count, shifted))
    early = tree_gather(packed, "strip", order[:2], shifted)

    padded_rows = jnp.pad(section_input, ((1, 1), (0, 0), (0, 0)))
    own_rows = lax.dynamic_slice_in_dim(padded_rows, chan_pos * row_part, row_part + 2, 0)
    extended = with_halo(own_rows, (("strip", 1),), 3)
    extended, early = lax.optimization_barrier((extended, early))
    early = tree_gather(early, "strip", order[2:4], shifted)
    hidden = swish(convolve(extended, conv_weight, row_part, col_local + 4) + conv_bias)
    pooled = pool_pairs(hidden)
    column = jnp.arange(half_cols + 2)
    outside = (column == 0) & (strip_pos == 0) | (column == half_cols + 1) & (
        strip_pos == strip_count - 1
    )
    pooled = jnp.where(outside[None, :, None], jnp.zeros_like(pooled), pooled)
    pooled, early = lax.optimization_barrier((pooled, early))
    every = tree_gather(early, "strip", order[4:], shifted).reshape(strip_count, owned + 8, lanes)
    every_counts = every[:, owned, :list_len].reshape(-1)
    every_slots = jnp.round(every[:, owned, list_len : 2 * list_len]).astype(jnp.int32).reshape(-1)
    part_rows = pooled.shape[0]
    gathered = jnp.zeros((chan_count * part_rows,) + pooled.shape[1:], pooled.dtype)
    for shift in range(chan_count):
        block = pooled
        if shift:
            block = lax.ppermute(
                pooled, "chan", [(i, (i + shift) % chan_count) for i in range(chan_count)]
            )
        source = (chan_pos + chan_count - shift) % chan_count
        gathered = lax.dynamic_update_slice_in_dim(gathered, block, source * part_rows, 0)
    padded_deep = jnp.pad(gathered, ((1, 1), (0, 0), (0, 0)))
    half_rows = gathered.shape[0]
    deep_pre = convolve(padded_deep, deep_weight, half_rows, half_cols) + deep_bias
    features = swish(deep_pre).astype(jnp.bfloat16).reshape(-1, width_deep)
    part_sums = jnp.dot(member.astype(jnp.bfloat16), features, preferred_element_type=jnp.float32)

    same_slot = (slot_ids[:, None] == every_slots[None, :]).astype(jnp.float32)
    entry_counts = jnp.dot(same_slot, every_counts, precision=lax.Precision.HIGHEST)
    entry_grad = every[position[slot_ids // owned], slot_ids % owned] / jnp.maximum(entry_counts, 1.0)[:, None]
    pixel_grad = lax.dot_general(
        member.astype(jnp.float32),
        entry_grad,
        (((0,), (0,)), ((), ())),
        precision=lax.Precision.HIGHEST,
        preferred_element_type=jnp.float32,
    )
    deep_grad = (pixel_grad * swish_slope(deep_pre.reshape(-1, width_deep))).astype(jnp.bfloat16)
    deep_width = -(-padded_deep.shape[1] // 16) * 16
    wide_deep = jnp.pad(padded_deep, ((0, 0), (0, deep_width - padded_deep.shape[1]), (0, 0)))
    grid_grad = deep_grad.reshape(half_rows, half_cols, width_deep)
    placed_grads = [
        jnp.pad(
            grid_grad, ((0, 0), (shift_col, deep_width - half_cols - shift_col), (0, 0))
        ).reshape(-1, width_deep)
        for shift_col in range(3)
    ]
    pieces = []
    for shift_row in range(3):
        band = wide_deep[shift_row : shift_row + half_rows].reshape(-1, channels)
        for shift_col in range(3):
            pieces.append(
                lax.dot_general(
                    band,
                    placed_grads[shift_col],
                    (((0,), (0,)), ((), ())),
                    preferred_element_type=jnp.float32,
                )
            )
    local_bias = jnp.sum(deep_grad.astype(jnp.float32), axis=0)
    bias_rows = jnp.zeros((strip_count * 8 - 9 * channels % (strip_count * 8), width_deep), jnp.float32)
    bias_rows = bias_rows.at[0].set(local_bias)
    local_grads = jnp.concatenate(pieces + [bias_rows], axis=0)

    total_grads, every_sums = tree_sum(local_grads, part_sums, "strip", halving, shifted)
    mine = strip_pos * owned + jnp.arange(owned, dtype=jnp.int32)
    pick = (mine[:, None] == every_slots[None, :]).astype(jnp.float32)
    slot_sums = jnp.dot(pick, every_sums, precision=lax.Precision.HIGHEST)
    slot_counts = jnp.dot(pick, every_counts, precision=lax.Precision.HIGHEST)
    embeddings = slot_sums / jnp.maximum(slot_counts, 1.0)[:, None]

    weight_grad = total_grads[: 9 * channels].reshape(3, 3, channels, width_deep)
    bias_grad = total_grads[9 * channels]
    return (embeddings, weight_grad, bias_grad)


def solution(mesh):
    placed = (
        P(None, "strip", None),
        P(),
        P(),
        P(None, None, None, "chan"),
        P("chan"),
        P(None, "strip"),
        P("strip"),
        P("strip", "chan"),
    )
    return jax.shard_map(
        body,
        mesh=mesh,
        in_specs=placed,
        out_specs=(P("strip", "chan"), P(None, None, None, "chan"), P("chan")),
        check_vma=False,
    )
```

```python
import functools

import jax
import numpy as np
import jax.numpy as jnp
from jax import lax
from jax.experimental import pallas as pl
from jax.experimental.pallas import tpu as pltpu
from jax.sharding import PartitionSpec as P


def with_halo(cells, sides, width):
    for axis, dim in sides:
        count = lax.axis_size(axis)
        ends = count - 1
        head = lax.slice_in_dim(cells, 0, width, axis=dim)
        tail = lax.slice_in_dim(cells, cells.shape[dim] - width, cells.shape[dim], axis=dim)
        cells = jnp.concatenate(
            [
                lax.ppermute(tail, axis, [(i, (i + 1) % count) for i in range(ends)]),
                cells,
                lax.ppermute(head, axis, [((i + 1) % count, i) for i in range(ends)]),
            ],
            axis=dim,
        )
    return cells


def chip_view(index, shifted):
    if not shifted:
        return index
    core = index % 2
    return ((index // 16 + core) % 4 * 8 + (index // 2 + core) % 8) * 2 + core


def chip_unview(index, shifted):
    if not shifted:
        return index
    core = index % 2
    return ((index // 16 + 4 - core) % 4 * 8 + (index // 2 + 8 - core) % 8) * 2 + core


def strip_partner(index, dist, shifted):
    if dist == 1:
        return index + 1 - 2 * (index % 2)
    view = chip_view(index, shifted)
    return chip_unview(view + dist - 2 * dist * ((view // dist) % 2), shifted)


def strip_bit(index, dist, shifted):
    if dist == 1:
        return index % 2
    return (chip_view(index, shifted) // dist) % 2


def tree_gather(block, axis, order, shifted):
    count = lax.axis_size(axis)
    me = lax.axis_index(axis)
    held = block
    for dist in order:
        pairs = [(i, strip_partner(i, dist, shifted)) for i in range(count)]
        other = lax.ppermute(held, axis, pairs)
        high = strip_bit(me, dist, shifted)
        size = held.shape[0]
        both = jnp.zeros((2 * size,) + held.shape[1:], held.dtype)
        both = lax.dynamic_update_slice_in_dim(both, held, high * size, 0)
        held = lax.dynamic_update_slice_in_dim(both, other, (1 - high) * size, 0)
    return held


def gather_position(order, count, shifted):
    return np.array(
        [sum(strip_bit(j, dist, shifted) << k for k, dist in enumerate(order)) for j in range(count)],
        np.int32,
    )


def tree_kernel(count, chunk, width, dists, shifted, grads_ref, sums_ref, out_ref, every_ref, landing, sems, free):
    me = lax.axis_index("strip")
    chan = lax.axis_index("chan")
    mesh_id = pl.DeviceIdType.MESH

    def partner(dist):
        return strip_partner(me, dist, shifted)

    barrier = pltpu.get_barrier_semaphore()
    for dist in dists:
        pl.semaphore_signal(barrier, inc=1, device_id=(partner(dist), chan), device_id_type=mesh_id)
    pl.semaphore_wait(barrier, len(dists))

    out_ref[...] = grads_ref[...]
    place = 0
    for k, dist in enumerate(dists):
        place = place + (strip_bit(me, dist, shifted)) * (count >> (k + 1))
    every_ref[pl.ds(pl.multiple_of(place * width, 8), width)] = sums_ref[...]

    low = 0
    size = count * chunk
    offset = 0
    for k, dist in enumerate(dists):
        half = size // 2
        high = strip_bit(me, dist, shifted)
        keep = low + high * half
        give = low + (1 - high) * half
        copy = pltpu.make_async_remote_copy(
            src_ref=out_ref.at[pl.ds(pl.multiple_of(give, 8), half)],
            dst_ref=landing.at[pl.ds(offset, half)],
            send_sem=sems.at[0, k],
            recv_sem=sems.at[1, k],
            device_id=(partner(dist), chan),
            device_id_type=mesh_id,
        )
        copy.start()
        copy.wait()
        pl.semaphore_signal(
            free.at[k], inc=1, device_id=(partner(dist), chan), device_id_type=mesh_id
        )

        def accumulate(step, carry, keep=keep, offset=offset):
            mine = pl.ds(pl.multiple_of(keep + step * chunk, 8), chunk)
            got = pl.ds(pl.multiple_of(offset + step * chunk, 8), chunk)
            out_ref[mine] = out_ref[mine] + landing[got]
            return carry

        lax.fori_loop(0, half // chunk, accumulate, 0)
        low = keep
        size = half
        offset += half

    blocks = 1
    for k in reversed(range(len(dists))):
        dist = dists[k]
        pl.semaphore_wait(free.at[k], 1)
        rows = pl.ds(pl.multiple_of(low, 8), size)
        spot = pl.ds(pl.multiple_of(place * width, 8), blocks * width)
        grads_copy = pltpu.make_async_remote_copy(
            src_ref=out_ref.at[rows],
            dst_ref=out_ref.at[rows],
            send_sem=sems.at[2, k],
            recv_sem=sems.at[3, k],
            device_id=(partner(dist), chan),
            device_id_type=mesh_id,
        )
        sums_copy = pltpu.make_async_remote_copy(
            src_ref=every_ref.at[spot],
            dst_ref=every_ref.at[spot],
            send_sem=sems.at[4, k],
            recv_sem=sems.at[5, k],
            device_id=(partner(dist), chan),
            device_id_type=mesh_id,
        )
        grads_copy.start()
        sums_copy.start()
        grads_copy.wait()
        sums_copy.wait()
        high = strip_bit(me, dist, shifted)
        low = low - high * size
        place = place - high * blocks
        size = size * 2
        blocks = blocks * 2


def tree_sum(grads, sums, axis, dists, shifted):
    count = lax.axis_size(axis)
    rows, lanes = grads.shape
    chunk = rows // count
    width = sums.shape[0]
    steps = count.bit_length() - 1
    return pl.pallas_call(
        functools.partial(tree_kernel, count, chunk, width, dists, shifted),
        out_shape=(
            jax.ShapeDtypeStruct((rows, lanes), jnp.float32),
            jax.ShapeDtypeStruct((count * width, lanes), jnp.float32),
        ),
        in_specs=[pl.BlockSpec(memory_space=pltpu.VMEM)] * 2,
        out_specs=(pl.BlockSpec(memory_space=pltpu.VMEM),) * 2,
        scratch_shapes=[
            pltpu.VMEM((rows, lanes), jnp.float32),
            pltpu.SemaphoreType.DMA((6, steps)),
            pltpu.SemaphoreType.REGULAR((steps,)),
        ],
        compiler_params=pltpu.CompilerParams(collective_id=0, has_side_effects=True),
    )(grads, sums)


def swish(value):
    return value * jax.nn.sigmoid(value)


def swish_slope(value):
    sigma = jax.nn.sigmoid(value)
    return sigma * (1.0 + value * (1.0 - sigma))


def convolve(padded, weight, row_count, col_count):
    channels = padded.shape[-1]
    width = -(-padded.shape[1] // 16) * 16
    padded = jnp.pad(padded, ((0, 0), (0, width - padded.shape[1]), (0, 0)))
    running = None
    for shift_col in range(3):
        column_sum = None
        for shift_row in range(3):
            band = padded[shift_row : shift_row + row_count].reshape(row_count * width, channels)
            partial_term = jnp.dot(
                band, weight[shift_row, shift_col], preferred_element_type=jnp.float32
            )
            column_sum = partial_term if column_sum is None else column_sum + partial_term
        column_sum = column_sum.reshape(row_count, width, weight.shape[-1])
        shifted = column_sum[:, shift_col : shift_col + col_count]
        running = shifted if running is None else running + shifted
    return running


def pool_pairs(hidden):
    row_count, col_count, channels = hidden.shape
    return (
        hidden.reshape(row_count // 2, 2, col_count // 2, 2, channels)
        .mean(axis=(1, 3))
        .astype(jnp.bfloat16)
    )


def body(
    section_input, conv_weight, conv_bias, deep_weight, deep_bias, labels, slot_ids, embed_grad
):
    chan_count = lax.axis_size("chan")
    chan_pos = lax.axis_index("chan")
    strip_count = lax.axis_size("strip")
    strip_pos = lax.axis_index("strip")
    row_total, col_local, channels = section_input.shape
    row_part = row_total // chan_count
    half_cols = col_local // 2
    list_len = slot_ids.shape[0]
    owned, width_deep = embed_grad.shape
    lanes = embed_grad.shape[1]

    flat_labels = labels.reshape(-1)
    member = flat_labels[None, :] == jnp.arange(list_len, dtype=jnp.int32)[:, None]
    part_counts = jnp.sum(member.astype(jnp.float32), axis=1)
    meta = jnp.concatenate(
        [part_counts, slot_ids.astype(jnp.float32), jnp.zeros((8 * lanes - 2 * list_len,), jnp.float32)]
    ).reshape(8, lanes)
    packed = jnp.concatenate([embed_grad, meta], axis=0)
    halving = [1 << k for k in range(strip_count.bit_length() - 1)]
    if len(halving) == 6:
        halving = [1, 2, 16, 4, 32, 8]
    order = halving[::-1]
    shifted = strip_count == 64
    position = jnp.asarray(gather_position(order, strip_count, shifted))
    early = tree_gather(packed, "strip", order[:2], shifted)

    padded_rows = jnp.pad(section_input, ((1, 1), (0, 0), (0, 0)))
    own_rows = lax.dynamic_slice_in_dim(padded_rows, chan_pos * row_part, row_part + 2, 0)
    extended = with_halo(own_rows, (("strip", 1),), 3)
    early = tree_gather(early, "strip", order[2:4], shifted)
    hidden = swish(convolve(extended, conv_weight, row_part, col_local + 4) + conv_bias)
    pooled = pool_pairs(hidden)
    column = jnp.arange(half_cols + 2)
    outside = (column == 0) & (strip_pos == 0) | (column == half_cols + 1) & (
        strip_pos == strip_count - 1
    )
    pooled = jnp.where(outside[None, :, None], jnp.zeros_like(pooled), pooled)
    pooled, early = lax.optimization_barrier((pooled, early))
    every = tree_gather(early, "strip", order[4:], shifted).reshape(strip_count, owned + 8, lanes)
    every_counts = every[:, owned, :list_len].reshape(-1)
    every_slots = jnp.round(every[:, owned, list_len : 2 * list_len]).astype(jnp.int32).reshape(-1)
    part_rows = pooled.shape[0]
    gathered = jnp.zeros((chan_count * part_rows,) + pooled.shape[1:], pooled.dtype)
    for shift in range(chan_count):
        block = pooled
        if shift:
            block = lax.ppermute(
                pooled, "chan", [(i, (i + shift) % chan_count) for i in range(chan_count)]
            )
        source = (chan_pos + chan_count - shift) % chan_count
        gathered = lax.dynamic_update_slice_in_dim(gathered, block, source * part_rows, 0)
    padded_deep = jnp.pad(gathered, ((1, 1), (0, 0), (0, 0)))
    half_rows = gathered.shape[0]
    deep_pre = convolve(padded_deep, deep_weight, half_rows, half_cols) + deep_bias
    features = swish(deep_pre).astype(jnp.bfloat16).reshape(-1, width_deep)
    part_sums = jnp.dot(member.astype(jnp.bfloat16), features, preferred_element_type=jnp.float32)

    same_slot = (slot_ids[:, None] == every_slots[None, :]).astype(jnp.float32)
    entry_counts = jnp.dot(same_slot, every_counts, precision=lax.Precision.HIGHEST)
    entry_grad = every[position[slot_ids // owned], slot_ids % owned] / jnp.maximum(entry_counts, 1.0)[:, None]
    pixel_grad = lax.dot_general(
        member.astype(jnp.float32),
        entry_grad,
        (((0,), (0,)), ((), ())),
        precision=lax.Precision.HIGHEST,
        preferred_element_type=jnp.float32,
    )
    deep_grad = (pixel_grad * swish_slope(deep_pre.reshape(-1, width_deep))).astype(jnp.bfloat16)
    deep_width = -(-padded_deep.shape[1] // 16) * 16
    wide_deep = jnp.pad(padded_deep, ((0, 0), (0, deep_width - padded_deep.shape[1]), (0, 0)))
    grid_grad = deep_grad.reshape(half_rows, half_cols, width_deep)
    placed_grads = [
        jnp.pad(
            grid_grad, ((0, 0), (shift_col, deep_width - half_cols - shift_col), (0, 0))
        ).reshape(-1, width_deep)
        for shift_col in range(3)
    ]
    pieces = []
    for shift_row in range(3):
        band = wide_deep[shift_row : shift_row + half_rows].reshape(-1, channels)
        for shift_col in range(3):
            pieces.append(
                lax.dot_general(
                    band,
                    placed_grads[shift_col],
                    (((0,), (0,)), ((), ())),
                    preferred_element_type=jnp.float32,
                )
            )
    local_bias = jnp.sum(deep_grad.astype(jnp.float32), axis=0)
    bias_rows = jnp.zeros((strip_count * 8 - 9 * channels % (strip_count * 8), width_deep), jnp.float32)
    bias_rows = bias_rows.at[0].set(local_bias)
    local_grads = jnp.concatenate(pieces + [bias_rows], axis=0)

    total_grads, every_sums = tree_sum(local_grads, part_sums, "strip", halving, shifted)
    mine = strip_pos * owned + jnp.arange(owned, dtype=jnp.int32)
    pick = (mine[:, None] == every_slots[None, :]).astype(jnp.float32)
    slot_sums = jnp.dot(pick, every_sums, precision=lax.Precision.HIGHEST)
    slot_counts = jnp.dot(pick, every_counts, precision=lax.Precision.HIGHEST)
    embeddings = slot_sums / jnp.maximum(slot_counts, 1.0)[:, None]

    weight_grad = total_grads[: 9 * channels].reshape(3, 3, channels, width_deep)
    bias_grad = total_grads[9 * channels]
    return (embeddings, weight_grad, bias_grad)


def solution(mesh):
    placed = (
        P(None, "strip", None),
        P(),
        P(),
        P(None, None, None, "chan"),
        P("chan"),
        P(None, "strip"),
        P("strip"),
        P("strip", "chan"),
    )
    return jax.shard_map(
        body,
        mesh=mesh,
        in_specs=placed,
        out_specs=(P("strip", "chan"), P(None, None, None, "chan"), P("chan")),
        check_vma=False,
    )
```

```python
import functools

import jax
import numpy as np
import jax.numpy as jnp
from jax import lax
from jax.experimental import pallas as pl
from jax.experimental.pallas import tpu as pltpu
from jax.sharding import PartitionSpec as P


def with_halo(cells, sides, width):
    for axis, dim in sides:
        count = lax.axis_size(axis)
        ends = count - 1
        head = lax.slice_in_dim(cells, 0, width, axis=dim)
        tail = lax.slice_in_dim(cells, cells.shape[dim] - width, cells.shape[dim], axis=dim)
        cells = jnp.concatenate(
            [
                lax.ppermute(tail, axis, [(i, (i + 1) % count) for i in range(ends)]),
                cells,
                lax.ppermute(head, axis, [((i + 1) % count, i) for i in range(ends)]),
            ],
            axis=dim,
        )
    return cells


def chip_view(index, shifted):
    if not shifted:
        return index
    core = index % 2
    return ((index // 16 + core) % 4 * 8 + (index // 2 + core) % 8) * 2 + core


def chip_unview(index, shifted):
    if not shifted:
        return index
    core = index % 2
    return ((index // 16 + 4 - core) % 4 * 8 + (index // 2 + 8 - core) % 8) * 2 + core


def strip_partner(index, dist, shifted):
    if dist == 1:
        return index + 1 - 2 * (index % 2)
    view = chip_view(index, shifted)
    return chip_unview(view + dist - 2 * dist * ((view // dist) % 2), shifted)


def strip_bit(index, dist, shifted):
    if dist == 1:
        return index % 2
    return (chip_view(index, shifted) // dist) % 2


def tree_gather(block, axis, order, shifted):
    count = lax.axis_size(axis)
    me = lax.axis_index(axis)
    held = block
    for dist in order:
        pairs = [(i, strip_partner(i, dist, shifted)) for i in range(count)]
        other = lax.ppermute(held, axis, pairs)
        high = strip_bit(me, dist, shifted)
        size = held.shape[0]
        both = jnp.zeros((2 * size,) + held.shape[1:], held.dtype)
        both = lax.dynamic_update_slice_in_dim(both, held, high * size, 0)
        held = lax.dynamic_update_slice_in_dim(both, other, (1 - high) * size, 0)
    return held


def gather_position(order, count, shifted):
    return np.array(
        [sum(strip_bit(j, dist, shifted) << k for k, dist in enumerate(order)) for j in range(count)],
        np.int32,
    )


def tree_kernel(
    count, chunk, width, dists, shifted, grads_ref, sums_ref, out_ref, every_ref, landing, sems, free, load
):
    me = lax.axis_index("strip")
    chan = lax.axis_index("chan")
    mesh_id = pl.DeviceIdType.MESH

    def partner(dist):
        return strip_partner(me, dist, shifted)

    staging = pltpu.make_async_copy(grads_ref, out_ref, load.at[0])
    staging.start()
    barrier = pltpu.get_barrier_semaphore()
    for dist in dists:
        pl.semaphore_signal(barrier, inc=1, device_id=(partner(dist), chan), device_id_type=mesh_id)
    pl.semaphore_wait(barrier, len(dists))

    staging.wait()
    place = 0
    for k, dist in enumerate(dists):
        place = place + (strip_bit(me, dist, shifted)) * (count >> (k + 1))
    every_ref[pl.ds(pl.multiple_of(place * width, 8), width)] = sums_ref[...]

    low = 0
    size = count * chunk
    offset = 0
    for k, dist in enumerate(dists):
        half = size // 2
        high = strip_bit(me, dist, shifted)
        keep = low + high * half
        give = low + (1 - high) * half
        copy = pltpu.make_async_remote_copy(
            src_ref=out_ref.at[pl.ds(pl.multiple_of(give, 8), half)],
            dst_ref=landing.at[pl.ds(offset, half)],
            send_sem=sems.at[0, k],
            recv_sem=sems.at[1, k],
            device_id=(partner(dist), chan),
            device_id_type=mesh_id,
        )
        copy.start()
        copy.wait()
        pl.semaphore_signal(
            free.at[k], inc=1, device_id=(partner(dist), chan), device_id_type=mesh_id
        )

        def accumulate(step, carry, keep=keep, offset=offset):
            mine = pl.ds(pl.multiple_of(keep + step * chunk, 8), chunk)
            got = pl.ds(pl.multiple_of(offset + step * chunk, 8), chunk)
            out_ref[mine] = out_ref[mine] + landing[got]
            return carry

        lax.fori_loop(0, half // chunk, accumulate, 0)
        low = keep
        size = half
        offset += half

    blocks = 1
    for k in reversed(range(len(dists))):
        dist = dists[k]
        pl.semaphore_wait(free.at[k], 1)
        rows = pl.ds(pl.multiple_of(low, 8), size)
        spot = pl.ds(pl.multiple_of(place * width, 8), blocks * width)
        grads_copy = pltpu.make_async_remote_copy(
            src_ref=out_ref.at[rows],
            dst_ref=out_ref.at[rows],
            send_sem=sems.at[2, k],
            recv_sem=sems.at[3, k],
            device_id=(partner(dist), chan),
            device_id_type=mesh_id,
        )
        sums_copy = pltpu.make_async_remote_copy(
            src_ref=every_ref.at[spot],
            dst_ref=every_ref.at[spot],
            send_sem=sems.at[4, k],
            recv_sem=sems.at[5, k],
            device_id=(partner(dist), chan),
            device_id_type=mesh_id,
        )
        grads_copy.start()
        sums_copy.start()
        grads_copy.wait()
        sums_copy.wait()
        high = strip_bit(me, dist, shifted)
        low = low - high * size
        place = place - high * blocks
        size = size * 2
        blocks = blocks * 2


def tree_sum(grads, sums, axis, dists, shifted):
    count = lax.axis_size(axis)
    rows, lanes = grads.shape
    chunk = rows // count
    width = sums.shape[0]
    steps = count.bit_length() - 1
    return pl.pallas_call(
        functools.partial(tree_kernel, count, chunk, width, dists, shifted),
        out_shape=(
            jax.ShapeDtypeStruct((rows, lanes), jnp.float32),
            jax.ShapeDtypeStruct((count * width, lanes), jnp.float32),
        ),
        in_specs=[pl.BlockSpec(memory_space=pl.ANY), pl.BlockSpec(memory_space=pltpu.VMEM)],
        out_specs=(pl.BlockSpec(memory_space=pltpu.VMEM),) * 2,
        scratch_shapes=[
            pltpu.VMEM((rows, lanes), jnp.float32),
            pltpu.SemaphoreType.DMA((6, steps)),
            pltpu.SemaphoreType.REGULAR((steps,)),
            pltpu.SemaphoreType.DMA((1,)),
        ],
        compiler_params=pltpu.CompilerParams(collective_id=0, has_side_effects=True),
    )(grads, sums)


def swish(value):
    return value * jax.nn.sigmoid(value)


def swish_slope(value):
    sigma = jax.nn.sigmoid(value)
    return sigma * (1.0 + value * (1.0 - sigma))


def convolve(padded, weight, row_count, col_count):
    channels = padded.shape[-1]
    width = -(-padded.shape[1] // 16) * 16
    padded = jnp.pad(padded, ((0, 0), (0, width - padded.shape[1]), (0, 0)))
    running = None
    for shift_col in range(3):
        column_sum = None
        for shift_row in range(3):
            band = padded[shift_row : shift_row + row_count].reshape(row_count * width, channels)
            partial_term = jnp.dot(
                band, weight[shift_row, shift_col], preferred_element_type=jnp.float32
            )
            column_sum = partial_term if column_sum is None else column_sum + partial_term
        column_sum = column_sum.reshape(row_count, width, weight.shape[-1])
        shifted = column_sum[:, shift_col : shift_col + col_count]
        running = shifted if running is None else running + shifted
    return running


def pool_pairs(hidden):
    row_count, col_count, channels = hidden.shape
    return (
        hidden.reshape(row_count // 2, 2, col_count // 2, 2, channels)
        .mean(axis=(1, 3))
        .astype(jnp.bfloat16)
    )


def body(
    section_input, conv_weight, conv_bias, deep_weight, deep_bias, labels, slot_ids, embed_grad
):
    chan_count = lax.axis_size("chan")
    chan_pos = lax.axis_index("chan")
    strip_count = lax.axis_size("strip")
    strip_pos = lax.axis_index("strip")
    row_total, col_local, channels = section_input.shape
    row_part = row_total // chan_count
    half_cols = col_local // 2
    list_len = slot_ids.shape[0]
    owned, width_deep = embed_grad.shape
    lanes = embed_grad.shape[1]

    flat_labels = labels.reshape(-1)
    member = flat_labels[None, :] == jnp.arange(list_len, dtype=jnp.int32)[:, None]
    part_counts = jnp.sum(member.astype(jnp.float32), axis=1)
    meta = jnp.concatenate(
        [part_counts, slot_ids.astype(jnp.float32), jnp.zeros((8 * lanes - 2 * list_len,), jnp.float32)]
    ).reshape(8, lanes)
    packed = jnp.concatenate([embed_grad, meta], axis=0)
    halving = [1 << k for k in range(strip_count.bit_length() - 1)]
    if len(halving) == 6:
        halving = [1, 2, 16, 4, 32, 8]
    order = halving[::-1]
    shifted = strip_count == 64
    position = jnp.asarray(gather_position(order, strip_count, shifted))
    early = tree_gather(packed, "strip", order[:2], shifted)

    padded_rows = jnp.pad(section_input, ((1, 1), (0, 0), (0, 0)))
    own_rows = lax.dynamic_slice_in_dim(padded_rows, chan_pos * row_part, row_part + 2, 0)
    extended = with_halo(own_rows, (("strip", 1),), 3)
    extended, early = lax.optimization_barrier((extended, early))
    early = tree_gather(early, "strip", order[2:4], shifted)
    hidden = swish(convolve(extended, conv_weight, row_part, col_local + 4) + conv_bias)
    pooled = pool_pairs(hidden)
    column = jnp.arange(half_cols + 2)
    outside = (column == 0) & (strip_pos == 0) | (column == half_cols + 1) & (
        strip_pos == strip_count - 1
    )
    pooled = jnp.where(outside[None, :, None], jnp.zeros_like(pooled), pooled)
    pooled, early = lax.optimization_barrier((pooled, early))
    every = tree_gather(early, "strip", order[4:], shifted).reshape(strip_count, owned + 8, lanes)
    every_counts = every[:, owned, :list_len].reshape(-1)
    every_slots = jnp.round(every[:, owned, list_len : 2 * list_len]).astype(jnp.int32).reshape(-1)
    part_rows = pooled.shape[0]
    gathered = jnp.zeros((chan_count * part_rows,) + pooled.shape[1:], pooled.dtype)
    for shift in range(chan_count):
        block = pooled
        if shift:
            block = lax.ppermute(
                pooled, "chan", [(i, (i + shift) % chan_count) for i in range(chan_count)]
            )
        source = (chan_pos + chan_count - shift) % chan_count
        gathered = lax.dynamic_update_slice_in_dim(gathered, block, source * part_rows, 0)
    padded_deep = jnp.pad(gathered, ((1, 1), (0, 0), (0, 0)))
    half_rows = gathered.shape[0]
    deep_pre = convolve(padded_deep, deep_weight, half_rows, half_cols) + deep_bias
    features = swish(deep_pre).astype(jnp.bfloat16).reshape(-1, width_deep)
    part_sums = jnp.dot(member.astype(jnp.bfloat16), features, preferred_element_type=jnp.float32)

    same_slot = (slot_ids[:, None] == every_slots[None, :]).astype(jnp.float32)
    entry_counts = jnp.dot(same_slot, every_counts, precision=lax.Precision.HIGHEST)
    entry_grad = every[position[slot_ids // owned], slot_ids % owned] / jnp.maximum(entry_counts, 1.0)[:, None]
    pixel_grad = lax.dot_general(
        member.astype(jnp.float32),
        entry_grad,
        (((0,), (0,)), ((), ())),
        precision=lax.Precision.HIGHEST,
        preferred_element_type=jnp.float32,
    )
    deep_grad = (pixel_grad * swish_slope(deep_pre.reshape(-1, width_deep))).astype(jnp.bfloat16)
    deep_width = -(-padded_deep.shape[1] // 16) * 16
    wide_deep = jnp.pad(padded_deep, ((0, 0), (0, deep_width - padded_deep.shape[1]), (0, 0)))
    grid_grad = deep_grad.reshape(half_rows, half_cols, width_deep)
    placed_grads = [
        jnp.pad(
            grid_grad, ((0, 0), (shift_col, deep_width - half_cols - shift_col), (0, 0))
        ).reshape(-1, width_deep)
        for shift_col in range(3)
    ]
    pieces = []
    for shift_row in range(3):
        band = wide_deep[shift_row : shift_row + half_rows].reshape(-1, channels)
        for shift_col in range(3):
            pieces.append(
                lax.dot_general(
                    band,
                    placed_grads[shift_col],
                    (((0,), (0,)), ((), ())),
                    preferred_element_type=jnp.float32,
                )
            )
    local_bias = jnp.sum(deep_grad.astype(jnp.float32), axis=0)
    bias_rows = jnp.zeros((strip_count * 8 - 9 * channels % (strip_count * 8), width_deep), jnp.float32)
    bias_rows = bias_rows.at[0].set(local_bias)
    local_grads = jnp.concatenate(pieces + [bias_rows], axis=0)

    total_grads, every_sums = tree_sum(local_grads, part_sums, "strip", halving, shifted)
    mine = strip_pos * owned + jnp.arange(owned, dtype=jnp.int32)
    pick = (mine[:, None] == every_slots[None, :]).astype(jnp.float32)
    slot_sums = jnp.dot(pick, every_sums, precision=lax.Precision.HIGHEST)
    slot_counts = jnp.dot(pick, every_counts, precision=lax.Precision.HIGHEST)
    embeddings = slot_sums / jnp.maximum(slot_counts, 1.0)[:, None]

    weight_grad = total_grads[: 9 * channels].reshape(3, 3, channels, width_deep)
    bias_grad = total_grads[9 * channels]
    return (embeddings, weight_grad, bias_grad)


def solution(mesh):
    placed = (
        P(None, "strip", None),
        P(),
        P(),
        P(None, None, None, "chan"),
        P("chan"),
        P(None, "strip"),
        P("strip"),
        P("strip", "chan"),
    )
    return jax.shard_map(
        body,
        mesh=mesh,
        in_specs=placed,
        out_specs=(P("strip", "chan"), P(None, None, None, "chan"), P("chan")),
        check_vma=False,
    )
```

```python
import functools

import jax
import numpy as np
import jax.numpy as jnp
from jax import lax
from jax.experimental import pallas as pl
from jax.experimental.pallas import tpu as pltpu
from jax.sharding import PartitionSpec as P


def with_halo(cells, sides, width):
    for axis, dim in sides:
        count = lax.axis_size(axis)
        ends = count - 1
        head = lax.slice_in_dim(cells, 0, width, axis=dim)
        tail = lax.slice_in_dim(cells, cells.shape[dim] - width, cells.shape[dim], axis=dim)
        cells = jnp.concatenate(
            [
                lax.ppermute(tail, axis, [(i, (i + 1) % count) for i in range(ends)]),
                cells,
                lax.ppermute(head, axis, [((i + 1) % count, i) for i in range(ends)]),
            ],
            axis=dim,
        )
    return cells


def chip_view(index, shifted):
    if not shifted:
        return index
    core = index % 2
    return ((index // 16 + core) % 4 * 8 + (index // 2 + core) % 8) * 2 + core


def chip_unview(index, shifted):
    if not shifted:
        return index
    core = index % 2
    return ((index // 16 + 4 - core) % 4 * 8 + (index // 2 + 8 - core) % 8) * 2 + core


def strip_partner(index, dist, shifted):
    if dist == 1:
        return index + 1 - 2 * (index % 2)
    view = chip_view(index, shifted)
    return chip_unview(view + dist - 2 * dist * ((view // dist) % 2), shifted)


def strip_bit(index, dist, shifted):
    if dist == 1:
        return index % 2
    return (chip_view(index, shifted) // dist) % 2


def tree_gather(block, axis, order, shifted):
    count = lax.axis_size(axis)
    me = lax.axis_index(axis)
    held = block
    for dist in order:
        pairs = [(i, strip_partner(i, dist, shifted)) for i in range(count)]
        other = lax.ppermute(held, axis, pairs)
        high = strip_bit(me, dist, shifted)
        size = held.shape[0]
        both = jnp.zeros((2 * size,) + held.shape[1:], held.dtype)
        both = lax.dynamic_update_slice_in_dim(both, held, high * size, 0)
        held = lax.dynamic_update_slice_in_dim(both, other, (1 - high) * size, 0)
    return held


def gather_position(order, count, shifted):
    return np.array(
        [sum(strip_bit(j, dist, shifted) << k for k, dist in enumerate(order)) for j in range(count)],
        np.int32,
    )


def tree_kernel(count, chunk, width, dists, shifted, grads_ref, sums_ref, out_ref, every_ref, landing, sems, free):
    me = lax.axis_index("strip")
    chan = lax.axis_index("chan")
    mesh_id = pl.DeviceIdType.MESH

    def partner(dist):
        return strip_partner(me, dist, shifted)

    barrier = pltpu.get_barrier_semaphore()
    for dist in dists:
        pl.semaphore_signal(barrier, inc=1, device_id=(partner(dist), chan), device_id_type=mesh_id)
    pl.semaphore_wait(barrier, len(dists))

    out_ref[...] = grads_ref[...]
    place = 0
    for k, dist in enumerate(dists):
        place = place + (strip_bit(me, dist, shifted)) * (count >> (k + 1))
    every_ref[pl.ds(pl.multiple_of(place * width, 8), width)] = sums_ref[...]

    low = 0
    size = count * chunk
    offset = 0
    for k, dist in enumerate(dists):
        half = size // 2
        high = strip_bit(me, dist, shifted)
        keep = low + high * half
        give = low + (1 - high) * half
        copy = pltpu.make_async_remote_copy(
            src_ref=out_ref.at[pl.ds(pl.multiple_of(give, 8), half)],
            dst_ref=landing.at[pl.ds(offset, half)],
            send_sem=sems.at[0, k],
            recv_sem=sems.at[1, k],
            device_id=(partner(dist), chan),
            device_id_type=mesh_id,
        )
        copy.start()
        copy.wait()
        pl.semaphore_signal(
            free.at[k], inc=1, device_id=(partner(dist), chan), device_id_type=mesh_id
        )

        def accumulate(step, carry, keep=keep, offset=offset):
            mine = pl.ds(pl.multiple_of(keep + step * chunk, 8), chunk)
            got = pl.ds(pl.multiple_of(offset + step * chunk, 8), chunk)
            out_ref[mine] = out_ref[mine] + landing[got]
            return carry

        lax.fori_loop(0, half // chunk, accumulate, 0)
        low = keep
        size = half
        offset += half

    blocks = 1
    for k in reversed(range(len(dists))):
        dist = dists[k]
        pl.semaphore_wait(free.at[k], 1)
        rows = pl.ds(pl.multiple_of(low, 8), size)
        spot = pl.ds(pl.multiple_of(place * width, 8), blocks * width)
        grads_copy = pltpu.make_async_remote_copy(
            src_ref=out_ref.at[rows],
            dst_ref=out_ref.at[rows],
            send_sem=sems.at[2, k],
            recv_sem=sems.at[3, k],
            device_id=(partner(dist), chan),
            device_id_type=mesh_id,
        )
        sums_copy = pltpu.make_async_remote_copy(
            src_ref=every_ref.at[spot],
            dst_ref=every_ref.at[spot],
            send_sem=sems.at[4, k],
            recv_sem=sems.at[5, k],
            device_id=(partner(dist), chan),
            device_id_type=mesh_id,
        )
        grads_copy.start()
        sums_copy.start()
        grads_copy.wait()
        sums_copy.wait()
        high = strip_bit(me, dist, shifted)
        low = low - high * size
        place = place - high * blocks
        size = size * 2
        blocks = blocks * 2


def tree_sum(grads, sums, axis, dists, shifted):
    count = lax.axis_size(axis)
    rows, lanes = grads.shape
    chunk = rows // count
    width = sums.shape[0]
    steps = count.bit_length() - 1
    return pl.pallas_call(
        functools.partial(tree_kernel, count, chunk, width, dists, shifted),
        out_shape=(
            jax.ShapeDtypeStruct((rows, lanes), jnp.float32),
            jax.ShapeDtypeStruct((count * width, lanes), jnp.float32),
        ),
        in_specs=[pl.BlockSpec(memory_space=pltpu.VMEM)] * 2,
        out_specs=(pl.BlockSpec(memory_space=pltpu.VMEM),) * 2,
        scratch_shapes=[
            pltpu.VMEM((rows, lanes), jnp.float32),
            pltpu.SemaphoreType.DMA((6, steps)),
            pltpu.SemaphoreType.REGULAR((steps,)),
        ],
        compiler_params=pltpu.CompilerParams(collective_id=0, has_side_effects=True),
    )(grads, sums)


def swish(value):
    return value * jax.nn.sigmoid(value)


def swish_slope(value):
    sigma = jax.nn.sigmoid(value)
    return sigma * (1.0 + value * (1.0 - sigma))


def convolve(padded, weight, row_count, col_count):
    channels = padded.shape[-1]
    width = -(-padded.shape[1] // 16) * 16
    padded = jnp.pad(padded, ((0, 0), (0, width - padded.shape[1]), (0, 0)))
    running = None
    for shift_col in range(3):
        column_sum = None
        for shift_row in range(3):
            band = padded[shift_row : shift_row + row_count].reshape(row_count * width, channels)
            partial_term = jnp.dot(
                band, weight[shift_row, shift_col], preferred_element_type=jnp.float32
            )
            column_sum = partial_term if column_sum is None else column_sum + partial_term
        column_sum = column_sum.reshape(row_count, width, weight.shape[-1])
        shifted = column_sum[:, shift_col : shift_col + col_count]
        running = shifted if running is None else running + shifted
    return running


def pool_pairs(hidden):
    row_count, col_count, channels = hidden.shape
    return (
        hidden.reshape(row_count // 2, 2, col_count // 2, 2, channels)
        .mean(axis=(1, 3))
        .astype(jnp.bfloat16)
    )


def body(
    section_input, conv_weight, conv_bias, deep_weight, deep_bias, labels, slot_ids, embed_grad
):
    chan_count = lax.axis_size("chan")
    chan_pos = lax.axis_index("chan")
    strip_count = lax.axis_size("strip")
    strip_pos = lax.axis_index("strip")
    row_total, col_local, channels = section_input.shape
    row_part = row_total // chan_count
    half_cols = col_local // 2
    list_len = slot_ids.shape[0]
    owned, width_deep = embed_grad.shape
    lanes = embed_grad.shape[1]

    flat_labels = labels.reshape(-1)
    member = flat_labels[None, :] == jnp.arange(list_len, dtype=jnp.int32)[:, None]
    part_counts = jnp.sum(member.astype(jnp.float32), axis=1)
    meta = jnp.concatenate(
        [part_counts, slot_ids.astype(jnp.float32), jnp.zeros((8 * lanes - 2 * list_len,), jnp.float32)]
    ).reshape(8, lanes)
    packed = jnp.concatenate([embed_grad, meta], axis=0)
    halving = [1 << k for k in range(strip_count.bit_length() - 1)]
    if len(halving) == 6:
        halving = [1, 2, 16, 4, 32, 8]
    order = halving[::-1]
    shifted = strip_count == 64
    position = jnp.asarray(gather_position(order, strip_count, shifted))
    early = tree_gather(packed, "strip", order[:2], shifted)

    padded_rows = jnp.pad(section_input, ((1, 1), (0, 0), (0, 0)))
    own_rows = lax.dynamic_slice_in_dim(padded_rows, chan_pos * row_part, row_part + 2, 0)
    extended = with_halo(own_rows, (("strip", 1),), 3)
    extended, early = lax.optimization_barrier((extended, early))
    early = tree_gather(early, "strip", order[2:4], shifted)
    hidden = swish(convolve(extended, conv_weight, row_part, col_local + 4) + conv_bias)
    pooled = pool_pairs(hidden)
    column = jnp.arange(half_cols + 2)
    outside = (column == 0) & (strip_pos == 0) | (column == half_cols + 1) & (
        strip_pos == strip_count - 1
    )
    pooled = jnp.where(outside[None, :, None], jnp.zeros_like(pooled), pooled)
    pooled, early = lax.optimization_barrier((pooled, early))
    every = tree_gather(early, "strip", order[4:], shifted).reshape(strip_count, owned + 8, lanes)
    every_counts = every[:, owned, :list_len].reshape(-1)
    every_slots = jnp.round(every[:, owned, list_len : 2 * list_len]).astype(jnp.int32).reshape(-1)
    part_rows = pooled.shape[0]
    gathered = jnp.zeros((chan_count * part_rows,) + pooled.shape[1:], pooled.dtype)
    for shift in range(chan_count):
        block = pooled
        if shift:
            block = lax.ppermute(
                pooled, "chan", [(i, (i + shift) % chan_count) for i in range(chan_count)]
            )
        source = (chan_pos + chan_count - shift) % chan_count
        gathered = lax.dynamic_update_slice_in_dim(gathered, block, source * part_rows, 0)
    padded_deep = jnp.pad(gathered, ((1, 1), (0, 0), (0, 0)))
    half_rows = gathered.shape[0]
    deep_pre = convolve(padded_deep, deep_weight, half_rows, half_cols) + deep_bias
    features = swish(deep_pre).astype(jnp.bfloat16).reshape(-1, width_deep)
    part_sums = jnp.dot(member.astype(jnp.bfloat16), features, preferred_element_type=jnp.float32)

    same_slot = (slot_ids[:, None] == every_slots[None, :]).astype(jnp.float32)
    entry_counts = jnp.dot(same_slot, every_counts, precision=lax.Precision.HIGHEST)
    entry_grad = every[position[slot_ids // owned], slot_ids % owned] / jnp.maximum(entry_counts, 1.0)[:, None]
    pixel_grad = lax.dot_general(
        member.astype(jnp.float32),
        entry_grad,
        (((0,), (0,)), ((), ())),
        precision=lax.Precision.HIGHEST,
        preferred_element_type=jnp.float32,
    )
    deep_grad = (pixel_grad * swish_slope(deep_pre.reshape(-1, width_deep))).astype(jnp.bfloat16)
    deep_width = -(-padded_deep.shape[1] // 16) * 16
    wide_deep = jnp.pad(padded_deep, ((0, 0), (0, deep_width - padded_deep.shape[1]), (0, 0)))
    grid_grad = deep_grad.reshape(half_rows, half_cols, width_deep)
    placed_grads = jnp.concatenate(
        [
            jnp.pad(
                grid_grad, ((0, 0), (shift_col, deep_width - half_cols - shift_col), (0, 0))
            ).reshape(-1, width_deep)
            for shift_col in range(3)
        ],
        axis=1,
    )
    pieces = []
    for shift_row in range(3):
        band = wide_deep[shift_row : shift_row + half_rows].reshape(-1, channels)
        row_terms = lax.dot_general(
            band, placed_grads, (((0,), (0,)), ((), ())), preferred_element_type=jnp.float32
        )
        for shift_col in range(3):
            pieces.append(row_terms[:, shift_col * width_deep : (shift_col + 1) * width_deep])
    local_bias = jnp.sum(deep_grad.astype(jnp.float32), axis=0)
    bias_rows = jnp.zeros((strip_count * 8 - 9 * channels % (strip_count * 8), width_deep), jnp.float32)
    bias_rows = bias_rows.at[0].set(local_bias)
    local_grads = jnp.concatenate(pieces + [bias_rows], axis=0)

    total_grads, every_sums = tree_sum(local_grads, part_sums, "strip", halving, shifted)
    mine = strip_pos * owned + jnp.arange(owned, dtype=jnp.int32)
    pick = (mine[:, None] == every_slots[None, :]).astype(jnp.float32)
    slot_sums = jnp.dot(pick, every_sums, precision=lax.Precision.HIGHEST)
    slot_counts = jnp.dot(pick, every_counts, precision=lax.Precision.HIGHEST)
    embeddings = slot_sums / jnp.maximum(slot_counts, 1.0)[:, None]

    weight_grad = total_grads[: 9 * channels].reshape(3, 3, channels, width_deep)
    bias_grad = total_grads[9 * channels]
    return (embeddings, weight_grad, bias_grad)


def solution(mesh):
    placed = (
        P(None, "strip", None),
        P(),
        P(),
        P(None, None, None, "chan"),
        P("chan"),
        P(None, "strip"),
        P("strip"),
        P("strip", "chan"),
    )
    return jax.shard_map(
        body,
        mesh=mesh,
        in_specs=placed,
        out_specs=(P("strip", "chan"), P(None, None, None, "chan"), P("chan")),
        check_vma=False,
    )
```

```python
import functools

import jax
import numpy as np
import jax.numpy as jnp
from jax import lax
from jax.experimental import pallas as pl
from jax.experimental.pallas import tpu as pltpu
from jax.sharding import PartitionSpec as P


def with_halo(cells, sides, width):
    for axis, dim in sides:
        count = lax.axis_size(axis)
        ends = count - 1
        head = lax.slice_in_dim(cells, 0, width, axis=dim)
        tail = lax.slice_in_dim(cells, cells.shape[dim] - width, cells.shape[dim], axis=dim)
        cells = jnp.concatenate(
            [
                lax.ppermute(tail, axis, [(i, (i + 1) % count) for i in range(ends)]),
                cells,
                lax.ppermute(head, axis, [((i + 1) % count, i) for i in range(ends)]),
            ],
            axis=dim,
        )
    return cells


def chip_view(index, shifted):
    if not shifted:
        return index
    core = index % 2
    return ((index // 16 + core) % 4 * 8 + (index // 2 + core) % 8) * 2 + core


def chip_unview(index, shifted):
    if not shifted:
        return index
    core = index % 2
    return ((index // 16 + 4 - core) % 4 * 8 + (index // 2 + 8 - core) % 8) * 2 + core


def strip_partner(index, dist, shifted):
    if dist == 1:
        return index + 1 - 2 * (index % 2)
    view = chip_view(index, shifted)
    return chip_unview(view + dist - 2 * dist * ((view // dist) % 2), shifted)


def strip_bit(index, dist, shifted):
    if dist == 1:
        return index % 2
    return (chip_view(index, shifted) // dist) % 2


def tree_gather(block, axis, order, shifted):
    count = lax.axis_size(axis)
    me = lax.axis_index(axis)
    held = block
    for dist in order:
        pairs = [(i, strip_partner(i, dist, shifted)) for i in range(count)]
        other = lax.ppermute(held, axis, pairs)
        high = strip_bit(me, dist, shifted)
        size = held.shape[0]
        both = jnp.zeros((2 * size,) + held.shape[1:], held.dtype)
        both = lax.dynamic_update_slice_in_dim(both, held, high * size, 0)
        held = lax.dynamic_update_slice_in_dim(both, other, (1 - high) * size, 0)
    return held


def gather_position(order, count, shifted):
    return np.array(
        [sum(strip_bit(j, dist, shifted) << k for k, dist in enumerate(order)) for j in range(count)],
        np.int32,
    )


def tree_kernel(count, chunk, width, dists, shifted, grads_ref, sums_ref, out_ref, every_ref, landing, sems, free):
    me = lax.axis_index("strip")
    chan = lax.axis_index("chan")
    mesh_id = pl.DeviceIdType.MESH

    def partner(dist):
        return strip_partner(me, dist, shifted)

    barrier = pltpu.get_barrier_semaphore()
    for dist in dists:
        pl.semaphore_signal(barrier, inc=1, device_id=(partner(dist), chan), device_id_type=mesh_id)
    pl.semaphore_wait(barrier, len(dists))

    out_ref[...] = grads_ref[...]
    place = 0
    for k, dist in enumerate(dists):
        place = place + (strip_bit(me, dist, shifted)) * (count >> (k + 1))
    every_ref[pl.ds(pl.multiple_of(place * width, 8), width)] = sums_ref[...]

    low = 0
    size = count * chunk
    offset = 0
    for k, dist in enumerate(dists):
        half = size // 2
        high = strip_bit(me, dist, shifted)
        keep = low + high * half
        give = low + (1 - high) * half
        copy = pltpu.make_async_remote_copy(
            src_ref=out_ref.at[pl.ds(pl.multiple_of(give, 8), half)],
            dst_ref=landing.at[pl.ds(offset, half)],
            send_sem=sems.at[0, k],
            recv_sem=sems.at[1, k],
            device_id=(partner(dist), chan),
            device_id_type=mesh_id,
        )
        copy.start()
        copy.wait()
        pl.semaphore_signal(
            free.at[k], inc=1, device_id=(partner(dist), chan), device_id_type=mesh_id
        )

        def accumulate(step, carry, keep=keep, offset=offset):
            mine = pl.ds(pl.multiple_of(keep + step * chunk, 8), chunk)
            got = pl.ds(pl.multiple_of(offset + step * chunk, 8), chunk)
            out_ref[mine] = out_ref[mine] + landing[got]
            return carry

        lax.fori_loop(0, half // chunk, accumulate, 0)
        low = keep
        size = half
        offset += half

    blocks = 1
    for k in reversed(range(len(dists))):
        dist = dists[k]
        pl.semaphore_wait(free.at[k], 1)
        rows = pl.ds(pl.multiple_of(low, 8), size)
        spot = pl.ds(pl.multiple_of(place * width, 8), blocks * width)
        grads_copy = pltpu.make_async_remote_copy(
            src_ref=out_ref.at[rows],
            dst_ref=out_ref.at[rows],
            send_sem=sems.at[2, k],
            recv_sem=sems.at[3, k],
            device_id=(partner(dist), chan),
            device_id_type=mesh_id,
        )
        sums_copy = pltpu.make_async_remote_copy(
            src_ref=every_ref.at[spot],
            dst_ref=every_ref.at[spot],
            send_sem=sems.at[4, k],
            recv_sem=sems.at[5, k],
            device_id=(partner(dist), chan),
            device_id_type=mesh_id,
        )
        grads_copy.start()
        sums_copy.start()
        grads_copy.wait()
        sums_copy.wait()
        high = strip_bit(me, dist, shifted)
        low = low - high * size
        place = place - high * blocks
        size = size * 2
        blocks = blocks * 2


def tree_sum(grads, sums, axis, dists, shifted):
    count = lax.axis_size(axis)
    rows, lanes = grads.shape
    chunk = rows // count
    width = sums.shape[0]
    steps = count.bit_length() - 1
    return pl.pallas_call(
        functools.partial(tree_kernel, count, chunk, width, dists, shifted),
        out_shape=(
            jax.ShapeDtypeStruct((rows, lanes), jnp.float32),
            jax.ShapeDtypeStruct((count * width, lanes), jnp.float32),
        ),
        in_specs=[pl.BlockSpec(memory_space=pltpu.VMEM)] * 2,
        out_specs=(pl.BlockSpec(memory_space=pltpu.VMEM),) * 2,
        scratch_shapes=[
            pltpu.VMEM((rows, lanes), jnp.float32),
            pltpu.SemaphoreType.DMA((6, steps)),
            pltpu.SemaphoreType.REGULAR((steps,)),
        ],
        compiler_params=pltpu.CompilerParams(collective_id=0, has_side_effects=True),
    )(grads, sums)


def swish(value):
    return value * jax.nn.sigmoid(value)


def swish_slope(value):
    sigma = jax.nn.sigmoid(value)
    return sigma * (1.0 + value * (1.0 - sigma))


def convolve(padded, weight, row_count, col_count):
    channels = padded.shape[-1]
    width = -(-padded.shape[1] // 16) * 16
    padded = jnp.pad(padded, ((0, 0), (0, width - padded.shape[1]), (0, 0)))
    running = None
    for shift_col in range(3):
        column_sum = None
        for shift_row in range(3):
            band = padded[shift_row : shift_row + row_count].reshape(row_count * width, channels)
            partial_term = jnp.dot(
                band, weight[shift_row, shift_col], preferred_element_type=jnp.float32
            )
            column_sum = partial_term if column_sum is None else column_sum + partial_term
        column_sum = column_sum.reshape(row_count, width, weight.shape[-1])
        shifted = column_sum[:, shift_col : shift_col + col_count]
        running = shifted if running is None else running + shifted
    return running


def pool_pairs(hidden):
    row_count, col_count, channels = hidden.shape
    return (
        hidden.reshape(row_count // 2, 2, col_count // 2, 2, channels)
        .mean(axis=(1, 3))
        .astype(jnp.bfloat16)
    )


def body(
    section_input, conv_weight, conv_bias, deep_weight, deep_bias, labels, slot_ids, embed_grad
):
    chan_count = lax.axis_size("chan")
    chan_pos = lax.axis_index("chan")
    strip_count = lax.axis_size("strip")
    strip_pos = lax.axis_index("strip")
    row_total, col_local, channels = section_input.shape
    row_part = row_total // chan_count
    half_cols = col_local // 2
    list_len = slot_ids.shape[0]
    owned, width_deep = embed_grad.shape
    lanes = embed_grad.shape[1]

    flat_labels = labels.reshape(-1)
    member = flat_labels[None, :] == jnp.arange(list_len, dtype=jnp.int32)[:, None]
    part_counts = jnp.sum(member.astype(jnp.float32), axis=1)
    meta = jnp.concatenate(
        [part_counts, slot_ids.astype(jnp.float32), jnp.zeros((8 * lanes - 2 * list_len,), jnp.float32)]
    ).reshape(8, lanes)
    packed = jnp.concatenate([embed_grad, meta], axis=0)
    halving = [1 << k for k in range(strip_count.bit_length() - 1)]
    if len(halving) == 6:
        halving = [1, 2, 16, 4, 8, 32]
    order = halving[::-1]
    shifted = strip_count == 64
    position = jnp.asarray(gather_position(order, strip_count, shifted))
    early = tree_gather(packed, "strip", order[:2], shifted)

    padded_rows = jnp.pad(section_input, ((1, 1), (0, 0), (0, 0)))
    own_rows = lax.dynamic_slice_in_dim(padded_rows, chan_pos * row_part, row_part + 2, 0)
    extended = with_halo(own_rows, (("strip", 1),), 3)
    extended, early = lax.optimization_barrier((extended, early))
    early = tree_gather(early, "strip", order[2:4], shifted)
    hidden = swish(convolve(extended, conv_weight, row_part, col_local + 4) + conv_bias)
    pooled = pool_pairs(hidden)
    column = jnp.arange(half_cols + 2)
    outside = (column == 0) & (strip_pos == 0) | (column == half_cols + 1) & (
        strip_pos == strip_count - 1
    )
    pooled = jnp.where(outside[None, :, None], jnp.zeros_like(pooled), pooled)
    pooled, early = lax.optimization_barrier((pooled, early))
    every = tree_gather(early, "strip", order[4:], shifted).reshape(strip_count, owned + 8, lanes)
    every_counts = every[:, owned, :list_len].reshape(-1)
    every_slots = jnp.round(every[:, owned, list_len : 2 * list_len]).astype(jnp.int32).reshape(-1)
    part_rows = pooled.shape[0]
    gathered = jnp.zeros((chan_count * part_rows,) + pooled.shape[1:], pooled.dtype)
    for shift in range(chan_count):
        block = pooled
        if shift:
            block = lax.ppermute(
                pooled, "chan", [(i, (i + shift) % chan_count) for i in range(chan_count)]
            )
        source = (chan_pos + chan_count - shift) % chan_count
        gathered = lax.dynamic_update_slice_in_dim(gathered, block, source * part_rows, 0)
    padded_deep = jnp.pad(gathered, ((1, 1), (0, 0), (0, 0)))
    half_rows = gathered.shape[0]
    deep_pre = convolve(padded_deep, deep_weight, half_rows, half_cols) + deep_bias
    features = swish(deep_pre).astype(jnp.bfloat16).reshape(-1, width_deep)
    part_sums = jnp.dot(member.astype(jnp.bfloat16), features, preferred_element_type=jnp.float32)

    same_slot = (slot_ids[:, None] == every_slots[None, :]).astype(jnp.float32)
    entry_counts = jnp.dot(same_slot, every_counts, precision=lax.Precision.HIGHEST)
    entry_grad = every[position[slot_ids // owned], slot_ids % owned] / jnp.maximum(entry_counts, 1.0)[:, None]
    pixel_grad = lax.dot_general(
        member.astype(jnp.float32),
        entry_grad,
        (((0,), (0,)), ((), ())),
        precision=lax.Precision.HIGHEST,
        preferred_element_type=jnp.float32,
    )
    deep_grad = (pixel_grad * swish_slope(deep_pre.reshape(-1, width_deep))).astype(jnp.bfloat16)
    deep_width = -(-padded_deep.shape[1] // 16) * 16
    wide_deep = jnp.pad(padded_deep, ((0, 0), (0, deep_width - padded_deep.shape[1]), (0, 0)))
    grid_grad = deep_grad.reshape(half_rows, half_cols, width_deep)
    placed_grads = [
        jnp.pad(
            grid_grad, ((0, 0), (shift_col, deep_width - half_cols - shift_col), (0, 0))
        ).reshape(-1, width_deep)
        for shift_col in range(3)
    ]
    pieces = []
    for shift_row in range(3):
        band = wide_deep[shift_row : shift_row + half_rows].reshape(-1, channels)
        for shift_col in range(3):
            pieces.append(
                lax.dot_general(
                    band,
                    placed_grads[shift_col],
                    (((0,), (0,)), ((), ())),
                    preferred_element_type=jnp.float32,
                )
            )
    local_bias = jnp.sum(deep_grad.astype(jnp.float32), axis=0)
    bias_rows = jnp.zeros((strip_count * 8 - 9 * channels % (strip_count * 8), width_deep), jnp.float32)
    bias_rows = bias_rows.at[0].set(local_bias)
    local_grads = jnp.concatenate(pieces + [bias_rows], axis=0)

    total_grads, every_sums = tree_sum(local_grads, part_sums, "strip", halving, shifted)
    mine = strip_pos * owned + jnp.arange(owned, dtype=jnp.int32)
    pick = (mine[:, None] == every_slots[None, :]).astype(jnp.float32)
    slot_sums = jnp.dot(pick, every_sums, precision=lax.Precision.HIGHEST)
    slot_counts = jnp.dot(pick, every_counts, precision=lax.Precision.HIGHEST)
    embeddings = slot_sums / jnp.maximum(slot_counts, 1.0)[:, None]

    weight_grad = total_grads[: 9 * channels].reshape(3, 3, channels, width_deep)
    bias_grad = total_grads[9 * channels]
    return (embeddings, weight_grad, bias_grad)


def solution(mesh):
    placed = (
        P(None, "strip", None),
        P(),
        P(),
        P(None, None, None, "chan"),
        P("chan"),
        P(None, "strip"),
        P("strip"),
        P("strip", "chan"),
    )
    return jax.shard_map(
        body,
        mesh=mesh,
        in_specs=placed,
        out_specs=(P("strip", "chan"), P(None, None, None, "chan"), P("chan")),
        check_vma=False,
    )
```

```python
import functools

import jax
import numpy as np
import jax.numpy as jnp
from jax import lax
from jax.experimental import pallas as pl
from jax.experimental.pallas import tpu as pltpu
from jax.sharding import PartitionSpec as P


def with_halo(cells, sides, width):
    for axis, dim in sides:
        count = lax.axis_size(axis)
        ends = count - 1
        head = lax.slice_in_dim(cells, 0, width, axis=dim)
        tail = lax.slice_in_dim(cells, cells.shape[dim] - width, cells.shape[dim], axis=dim)
        cells = jnp.concatenate(
            [
                lax.ppermute(tail, axis, [(i, (i + 1) % count) for i in range(ends)]),
                cells,
                lax.ppermute(head, axis, [((i + 1) % count, i) for i in range(ends)]),
            ],
            axis=dim,
        )
    return cells


def chip_view(index, shifted):
    if not shifted:
        return index
    core = index % 2
    return ((index // 16 + core) % 4 * 8 + (index // 2 + core) % 8) * 2 + core


def chip_unview(index, shifted):
    if not shifted:
        return index
    core = index % 2
    return ((index // 16 + 4 - core) % 4 * 8 + (index // 2 + 8 - core) % 8) * 2 + core


def strip_partner(index, dist, shifted):
    if dist == 1:
        return index + 1 - 2 * (index % 2)
    view = chip_view(index, shifted)
    return chip_unview(view + dist - 2 * dist * ((view // dist) % 2), shifted)


def strip_bit(index, dist, shifted):
    if dist == 1:
        return index % 2
    return (chip_view(index, shifted) // dist) % 2


def tree_gather(block, axis, order, shifted):
    count = lax.axis_size(axis)
    me = lax.axis_index(axis)
    held = block
    for dist in order:
        pairs = [(i, strip_partner(i, dist, shifted)) for i in range(count)]
        other = lax.ppermute(held, axis, pairs)
        high = strip_bit(me, dist, shifted)
        size = held.shape[0]
        both = jnp.zeros((2 * size,) + held.shape[1:], held.dtype)
        both = lax.dynamic_update_slice_in_dim(both, held, high * size, 0)
        held = lax.dynamic_update_slice_in_dim(both, other, (1 - high) * size, 0)
    return held


def gather_position(order, count, shifted):
    return np.array(
        [sum(strip_bit(j, dist, shifted) << k for k, dist in enumerate(order)) for j in range(count)],
        np.int32,
    )


def tree_kernel(count, chunk, width, dists, shifted, grads_ref, sums_ref, out_ref, every_ref, landing, sems, free):
    me = lax.axis_index("strip")
    chan = lax.axis_index("chan")
    mesh_id = pl.DeviceIdType.MESH

    def partner(dist):
        return strip_partner(me, dist, shifted)

    barrier = pltpu.get_barrier_semaphore()
    for dist in dists:
        pl.semaphore_signal(barrier, inc=1, device_id=(partner(dist), chan), device_id_type=mesh_id)
    pl.semaphore_wait(barrier, len(dists))

    out_ref[...] = grads_ref[...]
    place = 0
    for k, dist in enumerate(dists):
        place = place + (strip_bit(me, dist, shifted)) * (count >> (k + 1))
    every_ref[pl.ds(pl.multiple_of(place * width, 8), width)] = sums_ref[...]

    low = 0
    size = count * chunk
    offset = 0
    for k, dist in enumerate(dists):
        half = size // 2
        high = strip_bit(me, dist, shifted)
        keep = low + high * half
        give = low + (1 - high) * half
        copy = pltpu.make_async_remote_copy(
            src_ref=out_ref.at[pl.ds(pl.multiple_of(give, 8), half)],
            dst_ref=landing.at[pl.ds(offset, half)],
            send_sem=sems.at[0, k],
            recv_sem=sems.at[1, k],
            device_id=(partner(dist), chan),
            device_id_type=mesh_id,
        )
        copy.start()
        copy.wait()
        pl.semaphore_signal(
            free.at[k], inc=1, device_id=(partner(dist), chan), device_id_type=mesh_id
        )

        def accumulate(step, carry, keep=keep, offset=offset):
            mine = pl.ds(pl.multiple_of(keep + step * chunk, 8), chunk)
            got = pl.ds(pl.multiple_of(offset + step * chunk, 8), chunk)
            out_ref[mine] = out_ref[mine] + landing[got]
            return carry

        lax.fori_loop(0, half // chunk, accumulate, 0)
        low = keep
        size = half
        offset += half

    blocks = 1
    for k in reversed(range(len(dists))):
        dist = dists[k]
        pl.semaphore_wait(free.at[k], 1)
        rows = pl.ds(pl.multiple_of(low, 8), size)
        spot = pl.ds(pl.multiple_of(place * width, 8), blocks * width)
        grads_copy = pltpu.make_async_remote_copy(
            src_ref=out_ref.at[rows],
            dst_ref=out_ref.at[rows],
            send_sem=sems.at[2, k],
            recv_sem=sems.at[3, k],
            device_id=(partner(dist), chan),
            device_id_type=mesh_id,
        )
        sums_copy = pltpu.make_async_remote_copy(
            src_ref=every_ref.at[spot],
            dst_ref=every_ref.at[spot],
            send_sem=sems.at[4, k],
            recv_sem=sems.at[5, k],
            device_id=(partner(dist), chan),
            device_id_type=mesh_id,
        )
        grads_copy.start()
        sums_copy.start()
        grads_copy.wait()
        sums_copy.wait()
        high = strip_bit(me, dist, shifted)
        low = low - high * size
        place = place - high * blocks
        size = size * 2
        blocks = blocks * 2


def tree_sum(grads, sums, axis, dists, shifted):
    count = lax.axis_size(axis)
    rows, lanes = grads.shape
    chunk = rows // count
    width = sums.shape[0]
    steps = count.bit_length() - 1
    return pl.pallas_call(
        functools.partial(tree_kernel, count, chunk, width, dists, shifted),
        out_shape=(
            jax.ShapeDtypeStruct((rows, lanes), jnp.float32),
            jax.ShapeDtypeStruct((count * width, lanes), jnp.float32),
        ),
        in_specs=[pl.BlockSpec(memory_space=pltpu.VMEM)] * 2,
        out_specs=(pl.BlockSpec(memory_space=pltpu.VMEM),) * 2,
        scratch_shapes=[
            pltpu.VMEM((rows, lanes), jnp.float32),
            pltpu.SemaphoreType.DMA((6, steps)),
            pltpu.SemaphoreType.REGULAR((steps,)),
        ],
        compiler_params=pltpu.CompilerParams(collective_id=0, has_side_effects=True),
    )(grads, sums)


def swish(value):
    return value * jax.nn.sigmoid(value)


def swish_slope(value):
    sigma = jax.nn.sigmoid(value)
    return sigma * (1.0 + value * (1.0 - sigma))


def convolve(padded, weight, row_count, col_count):
    channels = padded.shape[-1]
    width = -(-padded.shape[1] // 16) * 16
    padded = jnp.pad(padded, ((0, 0), (0, width - padded.shape[1]), (0, 0)))
    running = None
    for shift_col in range(3):
        column_sum = None
        for shift_row in range(3):
            band = padded[shift_row : shift_row + row_count].reshape(row_count * width, channels)
            partial_term = jnp.dot(
                band, weight[shift_row, shift_col], preferred_element_type=jnp.float32
            )
            column_sum = partial_term if column_sum is None else column_sum + partial_term
        column_sum = column_sum.reshape(row_count, width, weight.shape[-1])
        shifted = column_sum[:, shift_col : shift_col + col_count]
        running = shifted if running is None else running + shifted
    return running


def pool_pairs(hidden):
    row_count, col_count, channels = hidden.shape
    return (
        hidden.reshape(row_count // 2, 2, col_count // 2, 2, channels)
        .mean(axis=(1, 3))
        .astype(jnp.bfloat16)
    )


def body(
    section_input, conv_weight, conv_bias, deep_weight, deep_bias, labels, slot_ids, embed_grad
):
    chan_count = lax.axis_size("chan")
    chan_pos = lax.axis_index("chan")
    strip_count = lax.axis_size("strip")
    strip_pos = lax.axis_index("strip")
    row_total, col_local, channels = section_input.shape
    row_part = row_total // chan_count
    half_cols = col_local // 2
    list_len = slot_ids.shape[0]
    owned, width_deep = embed_grad.shape
    lanes = embed_grad.shape[1]

    flat_labels = labels.reshape(-1)
    member = flat_labels[None, :] == jnp.arange(list_len, dtype=jnp.int32)[:, None]
    part_counts = jnp.sum(member.astype(jnp.float32), axis=1)
    meta = jnp.concatenate(
        [part_counts, slot_ids.astype(jnp.float32), jnp.zeros((8 * lanes - 2 * list_len,), jnp.float32)]
    ).reshape(8, lanes)
    packed = jnp.concatenate([embed_grad, meta], axis=0)
    halving = [1 << k for k in range(strip_count.bit_length() - 1)]
    if len(halving) == 6:
        halving = [1, 2, 16, 4, 32, 8]
    order = halving[::-1]
    shifted = strip_count == 64
    position = jnp.asarray(gather_position(order, strip_count, shifted))
    early = tree_gather(packed, "strip", order[:2], shifted)

    padded_rows = jnp.pad(section_input, ((1, 1), (0, 0), (0, 0)))
    own_rows = lax.dynamic_slice_in_dim(padded_rows, chan_pos * row_part, row_part + 2, 0)
    extended = with_halo(own_rows, (("strip", 1),), 3)
    extended, early = lax.optimization_barrier((extended, early))
    early = tree_gather(early, "strip", order[2:4], shifted)
    hidden = swish(convolve(extended, conv_weight, row_part, col_local + 4) + conv_bias)
    pooled = pool_pairs(hidden)
    column = jnp.arange(half_cols + 2)
    outside = (column == 0) & (strip_pos == 0) | (column == half_cols + 1) & (
        strip_pos == strip_count - 1
    )
    pooled = jnp.where(outside[None, :, None], jnp.zeros_like(pooled), pooled)
    pooled, early = lax.optimization_barrier((pooled, early))
    every = tree_gather(early, "strip", order[4:], shifted).reshape(strip_count, owned + 8, lanes)
    every_counts = every[:, owned, :list_len].reshape(-1)
    every_slots = jnp.round(every[:, owned, list_len : 2 * list_len]).astype(jnp.int32).reshape(-1)
    part_rows = pooled.shape[0]
    gathered = jnp.zeros((chan_count * part_rows,) + pooled.shape[1:], pooled.dtype)
    for shift in range(chan_count):
        block = pooled
        if shift:
            block = lax.ppermute(
                pooled, "chan", [(i, (i + shift) % chan_count) for i in range(chan_count)]
            )
        source = (chan_pos + chan_count - shift) % chan_count
        gathered = lax.dynamic_update_slice_in_dim(gathered, block, source * part_rows, 0)
    padded_deep = jnp.pad(gathered, ((1, 1), (0, 0), (0, 0)))
    half_rows = gathered.shape[0]
    deep_pre = convolve(padded_deep, deep_weight, half_rows, half_cols) + deep_bias
    features = swish(deep_pre).astype(jnp.bfloat16).reshape(-1, width_deep)
    part_sums = jnp.dot(member.astype(jnp.bfloat16), features, preferred_element_type=jnp.float32)

    same_slot = (slot_ids[:, None] == every_slots[None, :]).astype(jnp.float32)
    entry_counts = jnp.dot(same_slot, every_counts, precision=lax.Precision.HIGHEST)
    entry_grad = every[position[slot_ids // owned], slot_ids % owned] / jnp.maximum(entry_counts, 1.0)[:, None]
    pixel_grad = lax.dot_general(
        member.astype(jnp.float32),
        entry_grad,
        (((0,), (0,)), ((), ())),
        precision=lax.Precision.HIGHEST,
        preferred_element_type=jnp.float32,
    )
    deep_grad = (pixel_grad * swish_slope(deep_pre.reshape(-1, width_deep))).astype(jnp.bfloat16)
    deep_width = -(-padded_deep.shape[1] // 16) * 16
    wide_deep = jnp.pad(padded_deep, ((0, 0), (0, deep_width - padded_deep.shape[1]), (0, 0)))
    grid_grad = deep_grad.reshape(half_rows, half_cols, width_deep)
    placed_grads = [
        jnp.pad(
            grid_grad, ((0, 0), (shift_col, deep_width - half_cols - shift_col), (0, 0))
        ).reshape(-1, width_deep)
        for shift_col in range(3)
    ]
    pieces = []
    for shift_row in range(3):
        band = wide_deep[shift_row : shift_row + half_rows].reshape(-1, channels)
        for shift_col in range(3):
            pieces.append(
                lax.dot_general(
                    band,
                    placed_grads[shift_col],
                    (((0,), (0,)), ((), ())),
                    preferred_element_type=jnp.float32,
                )
            )
    local_bias = jnp.sum(deep_grad.astype(jnp.float32), axis=0)
    bias_rows = jnp.zeros((strip_count * 8 - 9 * channels % (strip_count * 8), width_deep), jnp.float32)
    bias_rows = bias_rows.at[0].set(local_bias)
    local_grads = jnp.concatenate(pieces + [bias_rows], axis=0)

    total_grads, every_sums = tree_sum(local_grads, part_sums, "strip", halving, shifted)
    mine = strip_pos * owned + jnp.arange(owned, dtype=jnp.int32)
    pick = (mine[:, None] == every_slots[None, :]).astype(jnp.float32)
    slot_sums = jnp.dot(pick, every_sums, precision=lax.Precision.HIGH)
    slot_counts = jnp.dot(pick, every_counts, precision=lax.Precision.HIGHEST)
    embeddings = slot_sums / jnp.maximum(slot_counts, 1.0)[:, None]

    weight_grad = total_grads[: 9 * channels].reshape(3, 3, channels, width_deep)
    bias_grad = total_grads[9 * channels]
    return (embeddings, weight_grad, bias_grad)


def solution(mesh):
    placed = (
        P(None, "strip", None),
        P(),
        P(),
        P(None, None, None, "chan"),
        P("chan"),
        P(None, "strip"),
        P("strip"),
        P("strip", "chan"),
    )
    return jax.shard_map(
        body,
        mesh=mesh,
        in_specs=placed,
        out_specs=(P("strip", "chan"), P(None, None, None, "chan"), P("chan")),
        check_vma=False,
    )
```
